32 devices in a mesh: dp: 16 (over z, y, x), mp: 2 (over core).
Axes of the slice: x: 2, y: 2, z: 4, core: 2. Of those that a mesh axis runs over, the one named last changes fastest.
Arguments:
- content_in: bfloat16 [32, 512, 768], P('dp', 'mp'), may hold values from -6 to 6
- query_in: bfloat16 [32, 512, 768], P('dp', 'mp'), may hold values from -6 to 6
- doc_lengths: int32 [32], P('dp'), may hold values from 64 to 512, as said below
- order_ranks: int32 [32, 512], P('dp'), may hold values from 0 to 511, each once within a row
- segment_ids: int32 [32, 512], P('dp'), may hold values from 0 to 3, never falling along the last dimension, each value on 1 to 256 neighbouring positions
- target_flags: int32 [32, 512], P('dp'), may hold values 0 or 1
- query_weight: bfloat16 [768, 768], P(None, 'mp'), may hold values from -0.21875 to 0.21875
- key_weight: bfloat16 [768, 768], P(None, 'mp'), may hold values from -0.21875 to 0.21875
- value_weight: bfloat16 [768, 768], P(None, 'mp'), may hold values from -0.21875 to 0.21875
- out_weight: bfloat16 [768, 768], P('mp'), may hold values from -0.875 to 0.875
- rel_weight: bfloat16 [768, 768], P(None, 'mp'), may hold values from -0.21875 to 0.21875
- content_bias: bfloat16 [768], P('mp'), may hold values from -3 to 3
- position_bias: bfloat16 [768], P('mp'), may hold values from -3 to 3
- segment_bias: bfloat16 [768], P('mp'), may hold values from -3 to 3
- segment_embed: bfloat16 [2, 768], P(None, 'mp'), may hold values from -5 to 5
- first_gain: bfloat16 [768], replicated, may hold values from 0.5 to 1.5
- first_shift: bfloat16 [768], replicated, may hold values from -2 to 2
- up_weight: bfloat16 [768, 3072], P(None, 'mp'), may hold values from -0.21875 to 0.21875
- up_bias: bfloat16 [3072], P('mp'), may hold values from -2 to 2
- down_weight: bfloat16 [3072, 768], P('mp'), may hold values from -0.109375 to 0.109375
- down_bias: bfloat16 [768], replicated, may hold values from -2 to 2
- second_gain: bfloat16 [768], replicated, may hold values from 0.5 to 1.5
- second_shift: bfloat16 [768], replicated, may hold values from -2 to 2
- content_cot: bfloat16 [32, 512, 768], P('dp', 'mp'), may hold values from -6 to 6
- query_cot: bfloat16 [32, 512, 768], P('dp', 'mp'), may hold values from -6 to 6
Outputs:
- content_out: bfloat16 [32, 512, 768], P('dp', 'mp')
- query_out: bfloat16 [32, 512, 768], P('dp', 'mp')
- content_grad: bfloat16 [32, 512, 768], P('dp', 'mp')
- query_grad: bfloat16 [32, 512, 768], P('dp', 'mp')
- query_weight_grad: float32 [768, 768], P(None, 'mp')
- key_weight_grad: float32 [768, 768], P(None, 'mp')
- value_weight_grad: float32 [768, 768], P(None, 'mp')
- out_weight_grad: float32 [768, 768], P('mp')
- rel_weight_grad: float32 [768, 768], P(None, 'mp')
- content_bias_grad: float32 [768], P('mp')
- position_bias_grad: float32 [768], P('mp')
- segment_bias_grad: float32 [768], P('mp')
- segment_embed_grad: float32 [2, 768], P(None, 'mp')
- first_gain_grad: float32 [768], replicated
- first_shift_grad: float32 [768], replicated
- up_weight_grad: float32 [768, 3072], P(None, 'mp')
- up_bias_grad: float32 [3072], P('mp')
- down_weight_grad: float32 [3072, 768], P('mp')
- down_bias_grad: float32 [768], replicated
- second_gain_grad: float32 [768], replicated
- second_shift_grad: float32 [768], replicated
The draws below stay inside these ranges and needn't reach their ends.
Inputs may be any that keep to these rules, and one draw needn't show every extreme that they name: `doc_lengths`: each document's true length; positions from it on are padding that no query attends to. Document 0 has 512 tokens and document 1 has 64. `order_ranks`: each document's row is a permutation of 0 to 511. `segment_ids`: never falling along a document; each segment at most 256 positions.
All inputs are finite; a program needn't handle non-finite values. No bound on the sum of `target_flags` on one device may be relied on, other than what follows from the above.
Results may differ from the reference program's by a relative error of at most 0.02.
Values may be sent and summed in bfloat16 or wider, within the bound.
A program may use at most 320 MiB of HBM per device.

```python
import math
import jax
import jax.numpy as jnp
import numpy as np
from jax import lax

D = 768
H = 12
DH = 64
FF = 3072
SEQ = 512
HD = 768
DOCS = 32


def draw_doc_lengths(key, part):
    lengths = jax.random.randint(key, (DOCS,), SEQ // 8, SEQ + 1)
    places = jnp.arange(DOCS)
    lengths = jnp.where(places == 0, SEQ, lengths)
    lengths = jnp.where(places == 1, SEQ // 8, lengths)
    return lengths.astype(jnp.int32)


def touch_ends(result, key, smallest, largest):
    spot = [jax.random.randint(jax.random.fold_in(key, axis), (), 0, length) for axis, length in enumerate(result.shape)]
    main_axis = result.shape.index(max(result.shape))
    neighbour = spot[:main_axis] + [(spot[main_axis] + 1) % result.shape[main_axis]] + spot[main_axis + 1:]
    return result.at[tuple(spot)].set(smallest).at[tuple(neighbour)].set(largest)


def block_levels(own_key, shape, shards, low, high):
    level, own = 1.0, jax.random.fold_in(own_key, 6)
    for position, shards_of in shards:
        draws = jnp.exp(jax.random.uniform(jax.random.fold_in(own, position), (shards_of,), jnp.float32, low / len(shards), high / len(shards)))
        level = level * jnp.repeat(draws, shape[position] // shards_of).reshape([-1 if axis == position else 1 for axis in range(len(shape))])
    return level


def profile(number_of, total, most, slope):
    weights = [(1 << 20) // math.isqrt(grade ** slope) + 1 for grade in range(2, number_of + 1)]
    spare, given = total - most - (number_of - 1), [1] * (number_of - 1)
    while spare > 0:
        candidates = [i for i in range(number_of - 1) if given[i] < most]
        mass, left = sum([weights[i] for i in candidates]), spare
        for i in candidates:
            addition = min(most - given[i], max(1, left * weights[i] // mass), spare)
            given[i] = given[i] + addition
            spare = spare - addition
    return np.array([most] + given)


def uneven_parts(rng, count, total, most, skew):
    if count == 2:
        one = jax.random.randint(rng, (), max(1, total - most), min(most, total - 1) + 1)
        return jnp.stack([one, total - one])
    sizes = jnp.asarray(profile(count, total, most, skew), jnp.int32)
    pairs = (count - 1) // 2
    source_of, receiver = sizes[1:1 + 2 * pairs:2], sizes[2:2 + 2 * pairs:2]
    room = jnp.minimum(source_of - 1, most - receiver)
    shifted = jax.random.randint(jax.random.fold_in(rng, 1), (pairs,), 0, 1 << 20) % (room + 1)
    sizes = sizes.at[1:1 + 2 * pairs:2].set(source_of - shifted).at[2:2 + 2 * pairs:2].set(receiver + shifted)
    return sizes[jax.random.permutation(jax.random.fold_in(rng, 2), count)]


def scatter_about(stream_key, shape, scale, limit, cuts=(), held_as=jnp.bfloat16):
    array = jax.random.normal(stream_key, shape, jnp.float32) * scale
    if len(cuts) > 0:
        array = block_levels(stream_key, shape, cuts, -0.22, 0.18) * array
    return jnp.clip(array, min=-limit, max=limit).astype(held_as)


def setup_inputs(seed: int = 0) -> dict:
    key_of = jax.random.split(jax.random.key(seed), 26)
    return {
        "content_in": scatter_about(key_of[0], (DOCS, SEQ, D), 1.0, 6.0, ((0, 16), (1, 2))),
        "query_in": scatter_about(key_of[1], (DOCS, SEQ, D), 1.0, 6.0, ((0, 16), (1, 2))),
        "doc_lengths": draw_doc_lengths(jax.random.fold_in(key_of[25], 71), 0),
        "order_ranks": jax.vmap(lambda own: jax.random.permutation(own, SEQ))(jax.random.split(key_of[3], DOCS)).reshape((DOCS, SEQ)).astype(jnp.int32),
        "segment_ids": jax.vmap(lambda own: jnp.searchsorted(jnp.cumsum(uneven_parts(own, 4, SEQ, SEQ // 2, 0)), jnp.arange(SEQ), side="right"))(jax.random.split(key_of[4], DOCS)).reshape((DOCS, SEQ)).astype(jnp.int32),
        "target_flags": touch_ends((jax.random.randint(key_of[5], (DOCS, SEQ), 0, 6) < 1).astype(jnp.int32), jax.random.fold_in(key_of[5], 1), 0, 1),
        "query_weight": scatter_about(key_of[6], (D, HD), D ** -0.5, 0.21875, ((1, 2),)),
        "key_weight": scatter_about(key_of[7], (D, HD), D ** -0.5, 0.21875, ((1, 2),)),
        "value_weight": scatter_about(key_of[8], (D, HD), D ** -0.5, 0.21875, ((1, 2),)),
        "out_weight": scatter_about(key_of[9], (HD, D), (D // 16) ** -0.5, 0.875, ((0, 2),)),
        "rel_weight": scatter_about(key_of[10], (D, HD), D ** -0.5, 0.21875, ((1, 2),)),
        "content_bias": scatter_about(key_of[11], (HD,), 0.5, 3.0, ((0, 2),)),
        "position_bias": scatter_about(key_of[12], (HD,), 0.5, 3.0, ((0, 2),)),
        "segment_bias": scatter_about(key_of[13], (HD,), 0.5, 3.0, ((0, 2),)),
        "segment_embed": scatter_about(key_of[14], (2, HD), 1.0, 5.0, ((1, 2),)),
        "first_gain": jnp.clip(1.0 + 0.1 * jax.random.normal(key_of[15], (D,), jnp.float32), 0.5, 1.5).astype(jnp.bfloat16),
        "first_shift": scatter_about(key_of[16], (D,), 0.3, 2.0),
        "up_weight": scatter_about(key_of[17], (D, FF), D ** -0.5, 0.21875, ((1, 2),)),
        "up_bias": scatter_about(key_of[18], (FF,), 0.3, 2.0, ((0, 2),)),
        "down_weight": scatter_about(key_of[19], (FF, D), FF ** -0.5, 0.109375, ((0, 2),)),
        "down_bias": scatter_about(key_of[20], (D,), 0.3, 2.0),
        "second_gain": jnp.clip(1.0 + 0.1 * jax.random.normal(key_of[21], (D,), jnp.float32), 0.5, 1.5).astype(jnp.bfloat16),
        "second_shift": scatter_about(key_of[22], (D,), 0.3, 2.0),
        "content_cot": scatter_about(key_of[23], (DOCS, SEQ, D), 1.0, 6.0, ((0, 16), (1, 2))),
        "query_cot": scatter_about(key_of[24], (DOCS, SEQ, D), 1.0, 6.0, ((0, 16), (1, 2))),
    }


@jax.custom_vjp
def low(v):
    return lax.optimization_barrier(v.astype(jnp.bfloat16)).astype(jnp.float32)

@jax.custom_vjp
def low_back(v):
    return v

def low_keep(v):
    return (low(v), None)

def low_pass(kept, grad):
    return (grad,)

def back_keep(v):
    return (v, None)

def back_low(kept, grad):
    return (low(grad),)
low.defvjp(low_keep, low_pass)
low_back.defvjp(back_keep, back_low)
epsilon = 1e-06
highest = lax.Precision.HIGHEST

def matmul_hi(left_op, right_op):
    return jnp.dot(left_op, right_op, precision=highest)

def layer_norm(value_in, gain, shift):
    center = value_in - lax.optimization_barrier(jnp.mean(value_in, axis=-1, keepdims=True))
    spread = lax.optimization_barrier(jnp.mean(center * center, axis=-1, keepdims=True))
    return center * lax.rsqrt(spread + epsilon) * gain + shift

def positions(seq_len, width):
    column = jnp.arange(2 * seq_len - 1).astype(jnp.float32)
    distance = seq_len - 1.0 - column
    freq_exp = jnp.arange(0, width, 2).astype(jnp.float32) / width
    inverse = 1.0 / 10000.0 ** freq_exp
    angle = distance[:, None] * inverse[None, :]
    return jnp.concatenate([jnp.sin(angle), jnp.cos(angle)], axis=1)

def skew_rows(table):
    length = table.shape[-2]
    leading = table.shape[:-2]
    flat = table.reshape(leading + (length * (2 * length - 1),))
    middle = flat[..., length - 1:length - 1 + length * (2 * length - 2)]
    return middle.reshape(leading + (length, 2 * length - 2))[..., :length]

def doc_masks(length, rank_row, segment_row, target_row):
    seq_len = rank_row.shape[0]
    places = jnp.arange(seq_len, dtype=jnp.int32)
    target_live = target_row * (places >= 2).astype(jnp.int32)
    visible = (places[None, :] < length) & ((target_live[None, :] == 0) | (rank_row[None, :] < rank_row[:, None]))
    diagonal = places[:, None] == places[None, :]
    return (visible | diagonal, visible & jnp.logical_not(diagonal), segment_row[:, None] == segment_row[None, :])

def attend(query_c, query_p, query_s, key_rows, values, rel_keys, embed, same, mask):
    content_part = jnp.einsum('qhd,khd->hqk', query_c, key_rows, precision=highest)
    rel_part = skew_rows(jnp.einsum('qhd,thd->hqt', query_p, rel_keys, precision=highest))
    paired = jnp.einsum('qhd,shd->hqs', query_s, embed, precision=highest)
    seg_part = jnp.where(same[None], paired[..., 0:1], paired[..., 1:2])
    scores = low_back((content_part + rel_part + seg_part) * 0.125)
    scores = jnp.where(mask[None], scores, -1e+30)
    row_max = lax.optimization_barrier(jnp.max(scores, axis=-1, keepdims=True))
    exp_terms = jnp.exp(scores - row_max)
    attn_prob = exp_terms / lax.optimization_barrier(jnp.sum(exp_terms, axis=-1, keepdims=True))
    return jnp.einsum('hqk,khd->qhd', low(attn_prob), values, precision=highest)

def forward(params, content, query, lengths, ranks, segments, targets, pos_low):
    query_weight, key_weight, value_weight, out_weight, rel_weight, content_bias, position_bias, segment_bias, segment_embed, first_gain, first_shift, up_weight, up_bias, down_weight, down_bias, second_gain, second_shift = params
    doc_count = lengths.shape[0]
    row_count = content.shape[0]

    def split_heads(value_in):
        return value_in.reshape(doc_count, SEQ, H, DH)
    content_proj = low_back(matmul_hi(content, query_weight))
    query_proj = low_back(matmul_hi(query, query_weight))
    key_rows = split_heads(low(low_back(matmul_hi(content, key_weight))))
    values = split_heads(low(low_back(matmul_hi(content, value_weight))))
    rel_keys = low(matmul_hi(pos_low, rel_weight)).reshape(2 * SEQ - 1, H, DH)
    embed = segment_embed.reshape(2, H, DH)

    def query_parts(proj):
        return (split_heads(low(proj + content_bias)), split_heads(low(proj + position_bias)), split_heads(proj + segment_bias))

    def one_doc(entry):
        content_parts, stream_parts, key_doc, value_doc, length, rank_row, segment_row, target_row = entry
        content_mask, query_mask, same = doc_masks(length, rank_row, segment_row, target_row)
        out_content = attend(content_parts[0], content_parts[1], content_parts[2], key_doc, value_doc, rel_keys, embed, same, content_mask)
        out_query = attend(stream_parts[0], stream_parts[1], stream_parts[2], key_doc, value_doc, rel_keys, embed, same, query_mask)
        return (out_content, out_query)
    attn_content, attn_query = lax.map(jax.checkpoint(one_doc), (query_parts(content_proj), query_parts(query_proj), key_rows, values, lengths, ranks, segments, targets))

    def finish(attn, resid):
        vec = low(low_back(attn.reshape(row_count, H * DH)))
        mixed = low_back(matmul_hi(vec, out_weight))
        first = low(layer_norm(mixed + resid, first_gain, first_shift))
        hidden = low_back(matmul_hi(first, up_weight) + up_bias)
        act = low(jax.nn.gelu(hidden, approximate=True))
        down = low_back(matmul_hi(act, down_weight)) + down_bias
        return layer_norm(first + down, second_gain, second_shift)
    return (finish(attn_content, content), finish(attn_query, query))

def reference(content_in, query_in, doc_lengths, order_ranks, segment_ids, target_flags, query_weight, key_weight, value_weight, out_weight, rel_weight, content_bias, position_bias, segment_bias, segment_embed, first_gain, first_shift, up_weight, up_bias, down_weight, down_bias, second_gain, second_shift, content_cot, query_cot):
    params = tuple((param.astype(jnp.float32) for param in (query_weight, key_weight, value_weight, out_weight, rel_weight, content_bias, position_bias, segment_bias, segment_embed, first_gain, first_shift, up_weight, up_bias, down_weight, down_bias, second_gain, second_shift)))
    pos_low = low(positions(SEQ, D))
    group = 8
    step_count = DOCS // group

    def token_blocks(value_in):
        return value_in.astype(jnp.float32).reshape(step_count, group * SEQ, D)

    def doc_blocks(value_in):
        return value_in.reshape(step_count, group, SEQ)

    def add_trees(left_op, right_op):
        return left_op + right_op

    def step(running, entry):
        content, query, lengths, ranks, segments, targets, cot_content, cot_query = entry

        def run_layer(param_set, content_x, query_x):
            return forward(param_set, content_x, query_x, lengths, ranks, segments, targets, pos_low)
        outputs, pullback = jax.vjp(run_layer, params, content, query)
        grads, grad_content, grad_query = pullback((cot_content, cot_query))
        running = jax.tree.map(add_trees, running, grads)
        return (running, (outputs[0].astype(jnp.bfloat16), outputs[1].astype(jnp.bfloat16), grad_content.astype(jnp.bfloat16), grad_query.astype(jnp.bfloat16)))
    zeros_tree = jax.tree.map(jnp.zeros_like, params)
    running, stacked = lax.scan(step, zeros_tree, (token_blocks(content_in), token_blocks(query_in), doc_lengths.reshape(step_count, group), doc_blocks(order_ranks), doc_blocks(segment_ids), doc_blocks(target_flags), token_blocks(content_cot), token_blocks(query_cot)))
    return (stacked[0].reshape(DOCS, SEQ, D), stacked[1].reshape(DOCS, SEQ, D), stacked[2].reshape(DOCS, SEQ, D), stacked[3].reshape(DOCS, SEQ, D), running[0], running[1], running[2], running[3], running[4], running[5], running[6], running[7], running[8], running[9], running[10], running[11], running[12], running[13], running[14], running[15], running[16])
```

```python
import jax
import jax.numpy as jnp
import ml_dtypes
import numpy as np
from jax import lax
from jax.experimental import pallas as pl
from jax.experimental.pallas import tpu as pltpu
from jax.sharding import PartitionSpec as P

DH = 64
PAIR = 2 * DH
ROWS = 256
NEG = -1e30


def nt(left_op, right_op):
    return lax.dot_general(
        left_op, right_op, (((1,), (1,)), ((), ())), preferred_element_type=jnp.float32
    )


def nn(left_op, right_op):
    return jnp.dot(left_op, right_op, preferred_element_type=jnp.float32)


def lane_ids(rows):
    return lax.broadcasted_iota(jnp.int32, (rows, PAIR), 1)


def attend_forward_body(
    len_ref, rank_col, rank_row, live_row, seg_hot, proj_c, proj_q, key_ref, value_ref, rel_ref,
    bias_ref, embed_ref, vec_c, vec_q, prob_ref, mask_scr, ext_scr,
):
    seq_len = key_ref.shape[0]
    blocks = seq_len // ROWS
    wide = seq_len + ROWS

    @pl.when(pl.program_id(1) == 0)
    def _():
        length = len_ref[pl.program_id(0)]
        for block in range(blocks):
            rows = pl.ds(block * ROWS, ROWS)
            place_j = lax.broadcasted_iota(jnp.int32, (ROWS, seq_len), 1)
            place_i = lax.broadcasted_iota(jnp.int32, (ROWS, seq_len), 0) + block * ROWS
            visible = (place_j < length) & (
                (live_row[...] == 0) | (rank_row[...] < rank_col[rows, :])
            )
            diagonal = place_i == place_j
            mask_scr[0, rows, :] = jnp.where(visible | diagonal, 0.0, NEG)
            mask_scr[1, rows, :] = jnp.where(visible & jnp.logical_not(diagonal), 0.0, NEG)

    ext_scr[:, :PAIR] = key_ref[...]
    ext_scr[:, PAIR:] = seg_hot[...]
    lane = lane_ids(ROWS)
    diff = embed_ref[0:1, :] - embed_ref[1:2, :]
    for stream in range(2):
        proj_ref = (proj_c, proj_q)[stream]
        vec_ref = (vec_c, vec_q)[stream]
        for block in range(blocks):
            rows = pl.ds(block * ROWS, ROWS)
            proj = proj_ref[rows, :]
            query_c = ((proj + bias_ref[0:1, :]) * 0.125).astype(jnp.bfloat16)
            query_p = ((proj + bias_ref[1:2, :]) * 0.125).astype(jnp.bfloat16)
            seg_gap = (proj + bias_ref[2:3, :]) * (diff * 0.125)
            hot = seg_hot[rows, :].astype(jnp.float32)
            window = rel_ref[pl.ds(seq_len - (block + 1) * ROWS, wide), :]
            vec_pair = None
            for head in range(2):
                own = (lane >= DH) if head else (lane < DH)
                zero = jnp.zeros((), jnp.bfloat16)
                gap = jnp.sum(jnp.where(own, seg_gap, 0.0), axis=1, keepdims=True)
                gap_high = gap.astype(jnp.bfloat16).astype(jnp.float32)
                seg_part = (jnp.where(lane < 4, gap_high, gap - gap_high) * hot).astype(jnp.bfloat16)
                left = jnp.concatenate([jnp.where(own, query_c, zero), seg_part], axis=1)
                scores = nt(left, ext_scr[...])
                table = nt(jnp.where(own, query_p, zero), window)
                table = pltpu.roll(table, 1, 1, stride=1, stride_axis=0)
                scores = scores + table[:, ROWS:] + mask_scr[stream, rows, :]
                top = jnp.max(scores, axis=1, keepdims=True)
                terms = jnp.exp(scores - top)
                total = jnp.sum(terms, axis=1, keepdims=True)
                prob = (terms * (1.0 / total)).astype(jnp.bfloat16)
                prob_ref[stream, head, rows, :] = prob
                part = nn(prob, value_ref[...])
                vec_pair = part if head == 0 else jnp.where(own, part, vec_pair)
            vec_ref[rows, :] = vec_pair.astype(jnp.bfloat16)


def attend_forward(lengths, rank_col, rank_row, live_row, seg_hot, proj_c, proj_q, keys, values, rel_keys, bias, embed):
    docs, seq_len, width = proj_c.shape
    pairs = width // PAIR
    per_doc = lambda d, p, *_: (d, 0, 0)
    per_pair = lambda d, p, *_: (d, 0, p)
    shared = lambda d, p, *_: (0, p)
    tile = pl.BlockSpec((None, seq_len, PAIR), per_pair)
    return pl.pallas_call(
        attend_forward_body,
        out_shape=(
            jax.ShapeDtypeStruct((docs, seq_len, width), jnp.bfloat16),
            jax.ShapeDtypeStruct((docs, seq_len, width), jnp.bfloat16),
            jax.ShapeDtypeStruct((docs, pairs, 2, 2, seq_len, seq_len), jnp.bfloat16),
        ),
        grid_spec=pltpu.PrefetchScalarGridSpec(
            num_scalar_prefetch=1,
            grid=(docs, pairs),
            in_specs=[
                pl.BlockSpec((None, seq_len, 1), per_doc),
                pl.BlockSpec((None, 1, seq_len), per_doc),
                pl.BlockSpec((None, 1, seq_len), per_doc),
                pl.BlockSpec((None, seq_len, PAIR), per_doc),
                tile, tile, tile, tile,
                pl.BlockSpec((2 * seq_len, PAIR), shared),
                pl.BlockSpec((3, PAIR), shared),
                pl.BlockSpec((2, PAIR), shared),
            ],
            out_specs=[
                tile, tile,
                pl.BlockSpec((None, None, 2, 2, seq_len, seq_len), lambda d, p, *_: (d, p, 0, 0, 0, 0)),
            ],
            scratch_shapes=[
                pltpu.VMEM((2, seq_len, seq_len), jnp.float32),
                pltpu.VMEM((seq_len, 2 * PAIR), jnp.bfloat16),
            ],
        ),
        name="attend_forward",
    )(lengths, rank_col, rank_row, live_row, seg_hot, proj_c, proj_q, keys, values, rel_keys, bias, embed)


def shear_left(value_in):
    rows, wide = value_in.shape
    pack = 16
    groups = []
    for group in range(rows // pack):
        piece = value_in[group * pack : (group + 1) * pack]
        groups.append(pltpu.roll(piece, wide - 1 - group * pack, 1))
    moved = jnp.concatenate(groups, axis=0)
    place = lax.broadcasted_iota(jnp.int32, (rows, wide), 0)
    step = 1
    while step < pack:
        moved = jnp.where((place & step) != 0, pltpu.roll(moved, wide - step, 1), moved)
        step = step * 2
    return moved


def attend_backward_body(
    seg_hot, proj_c, proj_q, key_ref, value_ref, rel_ref, bias_ref, embed_ref, vec_c, vec_q,
    grad_c, grad_q, prob_ref, gproj_c, gproj_q, gkey_ref, gvalue_ref, grel_ref, small_ref,
    ext_scr, key_acc, value_acc, rel_acc,
):
    seq_len = key_ref.shape[0]
    blocks = seq_len // ROWS
    wide = seq_len + ROWS
    ext_scr[:, :PAIR] = (key_ref[...].astype(jnp.float32) * 0.125).astype(jnp.bfloat16)
    ext_scr[:, PAIR:] = (seg_hot[...].astype(jnp.float32) * 0.125).astype(jnp.bfloat16)
    key_acc[...] = jnp.zeros_like(key_acc)
    value_acc[...] = jnp.zeros_like(value_acc)
    rel_acc[...] = jnp.zeros_like(rel_acc)
    lane = lane_ids(ROWS)
    first = lane < DH
    sums = [jnp.zeros((1, PAIR), jnp.float32) for _ in range(5)]
    for stream in range(2):
        proj_ref = (proj_c, proj_q)[stream]
        vec_ref = (vec_c, vec_q)[stream]
        grad_ref = (grad_c, grad_q)[stream]
        gproj_ref = (gproj_c, gproj_q)[stream]
        for block in range(blocks):
            rows = pl.ds(block * ROWS, ROWS)
            start = seq_len - (block + 1) * ROWS
            proj = proj_ref[rows, :]
            query_ct = jnp.transpose(((proj + bias_ref[0:1, :]) * 0.125).astype(jnp.bfloat16))
            query_pt = jnp.transpose(((proj + bias_ref[1:2, :]) * 0.125).astype(jnp.bfloat16))
            query_s = proj + bias_ref[2:3, :]
            hot = jnp.where(lane < 4, seg_hot[rows, :].astype(jnp.float32), 0.0)
            grad = grad_ref[rows, :]
            grad_t = jnp.transpose(grad)
            inner = grad.astype(jnp.float32) * vec_ref[rows, :].astype(jnp.float32)
            window = (rel_ref[pl.ds(start, wide), :].astype(jnp.float32) * 0.125).astype(jnp.bfloat16)
            parts = []
            for head in range(2):
                own = (lane >= DH) if head else first
                low, high = head * DH, (head + 1) * DH
                prob = prob_ref[stream, head, rows, :]
                grad_prob = nt(jnp.where(own, grad, jnp.zeros((), jnp.bfloat16)), value_ref[...])
                row_inner = jnp.sum(jnp.where(own, inner, 0.0), axis=1, keepdims=True)
                gscore = (prob.astype(jnp.float32) * (grad_prob - row_inner)).astype(jnp.bfloat16)
                value_acc[low:high, :] += nn(grad_t[low:high, :], prob)
                key_acc[low:high, :] += nn(query_ct[low:high, :], gscore)
                both = nn(gscore, ext_scr[...])
                table = jnp.concatenate([jnp.zeros((ROWS, ROWS), jnp.bfloat16), gscore], axis=1)
                table = shear_left(table)
                gpos = nn(table, window)
                rel_acc[low:high, start : start + wide] += nn(query_pt[low:high, :], table)
                tail = both[:, PAIR:]
                tail = jnp.where(lane < 4, tail, 0.0)
                g_same = jnp.sum(tail * hot, axis=1, keepdims=True)
                g_other = jnp.sum(tail, axis=1, keepdims=True) - g_same
                parts.append((both[:, :PAIR], gpos, g_same, g_other))
            g_content = jnp.where(first, parts[0][0], parts[1][0])
            g_position = jnp.where(first, parts[0][1], parts[1][1])
            g_same = jnp.where(first, parts[0][2], parts[1][2])
            g_other = jnp.where(first, parts[0][3], parts[1][3])
            g_segment = g_same * embed_ref[0:1, :] + g_other * embed_ref[1:2, :]
            gproj_ref[rows, :] = (g_content + g_position + g_segment).astype(jnp.bfloat16)
            terms = (g_content, g_position, g_segment, g_same * query_s, g_other * query_s)
            sums = [kept + jnp.sum(term, axis=0, keepdims=True) for kept, term in zip(sums, terms)]
    gkey_ref[...] = jnp.transpose(key_acc[...]).astype(jnp.bfloat16)
    gvalue_ref[...] = jnp.transpose(value_acc[...]).astype(jnp.bfloat16)
    grel_ref[...] = rel_acc[...].astype(jnp.bfloat16)
    small_ref[...] = jnp.concatenate(sums + [jnp.zeros((3, PAIR), jnp.float32)], axis=0)


def attend_backward(seg_hot, proj_c, proj_q, keys, values, rel_keys, bias, embed, vec_c, vec_q, grad_c, grad_q, prob):
    docs, seq_len, width = proj_c.shape
    pairs = width // PAIR
    per_doc = lambda d, p: (d, 0, 0)
    per_pair = lambda d, p: (d, 0, p)
    shared = lambda d, p: (0, p)
    tile = pl.BlockSpec((None, seq_len, PAIR), per_pair)
    low = jax.ShapeDtypeStruct((docs, seq_len, width), jnp.bfloat16)
    return pl.pallas_call(
        attend_backward_body,
        out_shape=(
            low, low, low, low,
            jax.ShapeDtypeStruct((docs, width, 2 * seq_len), jnp.bfloat16),
            jax.ShapeDtypeStruct((docs, 8, width), jnp.float32),
        ),
        grid_spec=pltpu.PrefetchScalarGridSpec(
            num_scalar_prefetch=0,
            grid=(docs, pairs),
            in_specs=[
                pl.BlockSpec((None, seq_len, PAIR), per_doc),
                tile, tile, tile, tile,
                pl.BlockSpec((2 * seq_len, PAIR), shared),
                pl.BlockSpec((3, PAIR), shared),
                pl.BlockSpec((2, PAIR), shared),
                tile, tile, tile, tile,
                pl.BlockSpec((None, None, 2, 2, seq_len, seq_len), lambda d, p: (d, p, 0, 0, 0, 0)),
            ],
            out_specs=[
                tile, tile, tile, tile,
                pl.BlockSpec((None, PAIR, 2 * seq_len), lambda d, p: (d, p, 0)),
                pl.BlockSpec((None, 8, PAIR), per_pair),
            ],
            scratch_shapes=[
                pltpu.VMEM((seq_len, 2 * PAIR), jnp.bfloat16),
                pltpu.VMEM((PAIR, seq_len), jnp.float32),
                pltpu.VMEM((PAIR, seq_len), jnp.float32),
                pltpu.VMEM((PAIR, 2 * seq_len), jnp.float32),
            ],
        ),
        name="attend_backward",
    )(seg_hot, proj_c, proj_q, keys, values, rel_keys, bias, embed, vec_c, vec_q, grad_c, grad_q, prob)


epsilon = 1e-06


def layer_norm(value_in, gain, shift):
    center = value_in - jnp.mean(value_in, axis=-1, keepdims=True)
    spread = jnp.mean(center * center, axis=-1, keepdims=True)
    return center * lax.rsqrt(spread + epsilon) * gain + shift


def gelu_tanh(value_in):
    return jax.nn.gelu(value_in, approximate=True)


def position_table(seq_len, width):
    distance = seq_len - 1.0 - np.arange(2 * seq_len - 1, dtype=np.float32)
    freq_exp = np.arange(0, width, 2).astype(np.float32) / np.float32(width)
    inverse = np.float32(1.0) / np.float32(10000.0) ** freq_exp
    angle = (distance[:, None] * inverse[None, :]).astype(np.float32)
    table = np.concatenate([np.sin(angle), np.cos(angle)], axis=1)
    table = np.concatenate([table, np.zeros((1, width), np.float32)], axis=0)
    return table.astype(ml_dtypes.bfloat16)


def dot_left(left_op, right_op):
    return lax.dot_general(
        left_op, right_op, (((0,), (0,)), ((), ())), preferred_element_type=jnp.float32
    )


def on_device(
    content_in,
    query_in,
    doc_lengths,
    order_ranks,
    segment_ids,
    target_flags,
    query_weight,
    key_weight,
    value_weight,
    out_weight,
    rel_weight,
    content_bias,
    position_bias,
    segment_bias,
    segment_embed,
    first_gain,
    first_shift,
    up_weight,
    up_bias,
    down_weight,
    down_bias,
    second_gain,
    second_shift,
    content_cot,
    query_cot,
):
    docs_dev, half, width = content_in.shape
    seq_len = order_ranks.shape[1]
    mine = lax.axis_index("mp")
    wide_f = lambda value: value.astype(jnp.float32)
    low_f = lambda value: value.astype(jnp.bfloat16)

    def swap(value):
        return lax.ppermute(value, "mp", [(0, 1), (1, 0)])

    def gather_doc(value):
        keep = lax.dynamic_index_in_dim(value, mine, 0, keepdims=False)
        came = swap(lax.dynamic_index_in_dim(value, 1 - mine, 0, keepdims=False))
        head = jnp.where(mine == 0, keep, came)
        tail = jnp.where(mine == 0, came, keep)
        return jnp.concatenate([head, tail], axis=0)

    def return_doc(value):
        pair = value.reshape(2, half, width)
        keep = lax.dynamic_index_in_dim(pair, mine, 0, keepdims=False)
        came = swap(lax.dynamic_index_in_dim(pair, 1 - mine, 0, keepdims=False))
        return jnp.stack([jnp.where(mine == 0, keep, came), jnp.where(mine == 0, came, keep)])

    def both(value, axis):
        return jnp.concatenate([value, swap(value)], axis=axis)

    content = gather_doc(content_in)
    query = gather_doc(query_in)
    query_use = both(query_weight, 1)
    key_use = both(key_weight, 1)
    value_use = both(value_weight, 1)
    rel_use = both(rel_weight, 1)
    vectors = both(
        jnp.concatenate(
            [
                wide_f(content_bias)[None],
                wide_f(position_bias)[None],
                wide_f(segment_bias)[None],
                wide_f(segment_embed),
            ],
            axis=0,
        ),
        1,
    )
    bias, embed = vectors[:3], vectors[3:]
    out_use = both(out_weight, 0)
    up_use = both(up_weight, 1)
    down_use = both(down_weight, 0)
    up_bias_use = both(wide_f(up_bias)[None], 1)
    cot = jnp.concatenate([gather_doc(content_cot), gather_doc(query_cot)], axis=0)

    lengths = lax.dynamic_slice_in_dim(doc_lengths, mine, 1, 0)
    ranks = lax.dynamic_slice_in_dim(order_ranks, mine, 1, 0)
    segments = lax.dynamic_slice_in_dim(segment_ids, mine, 1, 0)
    targets = lax.dynamic_slice_in_dim(target_flags, mine, 1, 0)
    live = targets * (jnp.arange(seq_len) >= 2).astype(jnp.int32)[None]
    lanes = jnp.arange(PAIR)
    seg_hot = low_f((segments[:, :, None] == lanes % 4) & (lanes < 8))
    table = jnp.asarray(position_table(seq_len, width))
    rel_keys = low_f(nn(table, rel_use))
    proj_c = nn(content, query_use)[None]
    proj_q = nn(query, query_use)[None]
    keys = low_f(nn(content, key_use))[None]
    values = low_f(nn(content, value_use))[None]
    vec_c, vec_q, prob = attend_forward(
        lengths, ranks[:, :, None], ranks[:, None, :], live[:, None, :], seg_hot,
        proj_c, proj_q, keys, values, rel_keys, bias, embed,
    )
    vec = jnp.concatenate([vec_c[0], vec_q[0]], axis=0)
    resid = jnp.concatenate([content, query], axis=0)
    gain_first, shift_first = wide_f(first_gain), wide_f(first_shift)
    gain_second, shift_second = wide_f(second_gain), wide_f(second_shift)
    pre1 = nn(vec, out_use) + wide_f(resid)
    first = low_f(layer_norm(pre1, gain_first, shift_first))
    hidden = nn(first, up_use) + up_bias_use
    act = low_f(gelu_tanh(hidden))
    pre2 = wide_f(first) + nn(act, down_use) + wide_f(down_bias)
    norm2, pull2 = jax.vjp(layer_norm, pre2, gain_second, shift_second)
    out_rows = low_f(norm2)
    grad_pre2, g_gain2, g_shift2 = pull2(wide_f(cot))
    g_down_bias = jnp.sum(grad_pre2, axis=0)
    grad_down = low_f(grad_pre2)
    grad_act = nt(grad_down, down_use)
    grad_hidden = low_f(jax.vjp(gelu_tanh, hidden)[1](grad_act)[0])
    g_up_bias = jnp.sum(wide_f(grad_hidden), axis=0)
    back = nt(grad_hidden, up_use)
    grad_pre1, g_gain1, g_shift1 = jax.vjp(layer_norm, pre1, gain_first, shift_first)[1](back + grad_pre2)
    grad_mixed = low_f(grad_pre1)
    grad_vec = low_f(nt(grad_mixed, out_use))

    ff = up_weight.shape[1]
    cols = query_weight.shape[1]

    def merge(left, right, axis):
        if axis == 1:
            split = right.shape[1] // 2
            other = low_f(dot_left(left, right[:, split:]))
            own = dot_left(left, right[:, :split])
        else:
            split = left.shape[1] // 2
            other = low_f(dot_left(left[:, split:], right))
            own = dot_left(left[:, :split], right)
        return low_f(own + wide_f(swap(other)))

    g_down = lax.psum(merge(act, grad_down, 0), "dp")
    g_up = lax.psum(merge(first, grad_hidden, 1), "dp")
    g_out = lax.psum(merge(vec, grad_mixed, 0), "dp")

    gproj_c, gproj_q, gkeys, gvalues, grel, small = attend_backward(
        seg_hot, proj_c, proj_q, keys, values, rel_keys, bias, embed, vec_c, vec_q,
        grad_vec[None, :seq_len], grad_vec[None, seq_len:], prob,
    )
    gproj = jnp.concatenate([gproj_c[0], gproj_q[0]], axis=0)
    g_query = lax.psum(merge(resid, gproj, 1), "dp")
    g_key = lax.psum(merge(content, gkeys[0], 1), "dp")
    g_value = lax.psum(merge(content, gvalues[0], 1), "dp")
    g_rel = lax.psum(merge(table, jnp.transpose(grel[0]), 1), "dp")
    content_grad = low_f(
        nt(gproj_c[0], query_use) + nt(gkeys[0], key_use) + nt(gvalues[0], value_use) + grad_pre1[:seq_len]
    )
    query_grad = low_f(nt(gproj_q[0], query_use) + grad_pre1[seq_len:])

    small = small[0]
    pack_split = jnp.concatenate([small[:5].reshape(-1, 2, cols).transpose(1, 0, 2).reshape(2, -1), g_up_bias.reshape(2, ff)], axis=1)
    pack_same = jnp.stack([g_gain1, g_shift1, g_gain2, g_shift2, g_down_bias]).reshape(-1)
    got = swap(jnp.concatenate([pack_split[1], pack_same]))
    tiny = lax.psum(jnp.concatenate([pack_split[0], pack_same]) + got, "dp")
    at = 5 * cols
    split_part = tiny[:at].reshape(5, cols)
    same_part = tiny[at + ff :].reshape(5, width)
    return (
        return_doc(out_rows[:seq_len]),
        return_doc(out_rows[seq_len:]),
        return_doc(content_grad),
        return_doc(query_grad),
        wide_f(g_query),
        wide_f(g_key),
        wide_f(g_value),
        wide_f(g_out),
        wide_f(g_rel),
        split_part[0],
        split_part[1],
        split_part[2],
        split_part[3:5],
        same_part[0],
        same_part[1],
        wide_f(g_up),
        tiny[at : at + ff],
        wide_f(g_down),
        same_part[4],
        same_part[2],
        same_part[3],
    )


def solution(mesh):
    placed = (
        P("dp", "mp", None),
        P("dp", "mp", None),
        P("dp"),
        P("dp", None),
        P("dp", None),
        P("dp", None),
        P(None, "mp"),
        P(None, "mp"),
        P(None, "mp"),
        P("mp", None),
        P(None, "mp"),
        P("mp"),
        P("mp"),
        P("mp"),
        P(None, "mp"),
        P(),
        P(),
        P(None, "mp"),
        P("mp"),
        P("mp", None),
        P(),
        P(),
        P(),
        P("dp", "mp", None),
        P("dp", "mp", None),
    )
    return jax.shard_map(
        on_device,
        mesh=mesh,
        in_specs=placed,
        out_specs=(
            P("dp", "mp", None),
            P("dp", "mp", None),
            P("dp", "mp", None),
            P("dp", "mp", None),
            P(None, "mp"),
            P(None, "mp"),
            P(None, "mp"),
            P("mp", None),
            P(None, "mp"),
            P("mp"),
            P("mp"),
            P("mp"),
            P(None, "mp"),
            P(),
            P(),
            P(None, "mp"),
            P("mp"),
            P("mp", None),
            P(),
            P(),
            P(),
        ),
        check_vma=False,
    )
```

```python
import functools

import jax
import jax.numpy as jnp
import ml_dtypes
import numpy as np
from jax import lax
from jax.experimental import pallas as pl
from jax.experimental.pallas import tpu as pltpu
from jax.sharding import PartitionSpec as P

DH = 64
PAIR = 2 * DH
ROWS = 256
NEG = -1e30


def nt(left_op, right_op):
    return lax.dot_general(
        left_op, right_op, (((1,), (1,)), ((), ())), preferred_element_type=jnp.float32
    )


def nn(left_op, right_op):
    return jnp.dot(left_op, right_op, preferred_element_type=jnp.float32)


def lane_ids(rows):
    return lax.broadcasted_iota(jnp.int32, (rows, PAIR), 1)


def attend_forward_body(
    len_ref, rank_col, rank_row, live_row, seg_hot, proj_c, proj_q, key_ref, value_ref, rel_ref,
    bias_ref, embed_ref, vec_c, vec_q, prob_ref, mask_scr, ext_scr,
):
    seq_len = key_ref.shape[0]
    blocks = seq_len // ROWS
    wide = seq_len + ROWS

    @pl.when(pl.program_id(1) == 0)
    def _():
        length = len_ref[pl.program_id(0)]
        for block in range(blocks):
            rows = pl.ds(block * ROWS, ROWS)
            place_j = lax.broadcasted_iota(jnp.int32, (ROWS, seq_len), 1)
            place_i = lax.broadcasted_iota(jnp.int32, (ROWS, seq_len), 0) + block * ROWS
            visible = (place_j < length) & (
                (live_row[...] == 0) | (rank_row[...] < rank_col[rows, :])
            )
            diagonal = place_i == place_j
            mask_scr[0, rows, :] = jnp.where(visible | diagonal, 0.0, NEG)
            mask_scr[1, rows, :] = jnp.where(visible & jnp.logical_not(diagonal), 0.0, NEG)

    ext_scr[:, :PAIR] = key_ref[...]
    ext_scr[:, PAIR:] = seg_hot[...]
    lane = lane_ids(ROWS)
    diff = embed_ref[0:1, :] - embed_ref[1:2, :]
    for stream in range(2):
        proj_ref = (proj_c, proj_q)[stream]
        vec_ref = (vec_c, vec_q)[stream]
        for block in range(blocks):
            rows = pl.ds(block * ROWS, ROWS)
            proj = proj_ref[rows, :]
            query_c = ((proj + bias_ref[0:1, :]) * 0.125).astype(jnp.bfloat16)
            query_p = ((proj + bias_ref[1:2, :]) * 0.125).astype(jnp.bfloat16)
            seg_gap = (proj + bias_ref[2:3, :]) * (diff * 0.125)
            hot = seg_hot[rows, :].astype(jnp.float32)
            window = rel_ref[pl.ds(seq_len - (block + 1) * ROWS, wide), :]
            vec_pair = None
            for head in range(2):
                own = (lane >= DH) if head else (lane < DH)
                zero = jnp.zeros((), jnp.bfloat16)
                gap = jnp.sum(jnp.where(own, seg_gap, 0.0), axis=1, keepdims=True)
                gap_high = gap.astype(jnp.bfloat16).astype(jnp.float32)
                seg_part = (jnp.where(lane < 4, gap_high, gap - gap_high) * hot).astype(jnp.bfloat16)
                left = jnp.concatenate([jnp.where(own, query_c, zero), seg_part], axis=1)
                scores = nt(left, ext_scr[...])
                table = nt(jnp.where(own, query_p, zero), window)
                table = pltpu.roll(table, 1, 1, stride=1, stride_axis=0)
                scores = scores + table[:, ROWS:] + mask_scr[stream, rows, :]
                top = jnp.max(scores, axis=1, keepdims=True)
                terms = jnp.exp(scores - top)
                total = jnp.sum(terms, axis=1, keepdims=True)
                prob = (terms * (1.0 / total)).astype(jnp.bfloat16)
                prob_ref[stream, head, rows, :] = prob
                part = nn(prob, value_ref[...])
                vec_pair = part if head == 0 else jnp.where(own, part, vec_pair)
            vec_ref[rows, :] = vec_pair.astype(jnp.bfloat16)


def attend_forward(lengths, rank_col, rank_row, live_row, seg_hot, proj_c, proj_q, keys, values, rel_keys, bias, embed):
    docs, seq_len, width = proj_c.shape
    pairs = width // PAIR
    per_doc = lambda d, p, *_: (d, 0, 0)
    per_pair = lambda d, p, *_: (d, 0, p)
    shared = lambda d, p, *_: (0, p)
    tile = pl.BlockSpec((None, seq_len, PAIR), per_pair)
    return pl.pallas_call(
        attend_forward_body,
        out_shape=(
            jax.ShapeDtypeStruct((docs, seq_len, width), jnp.bfloat16),
            jax.ShapeDtypeStruct((docs, seq_len, width), jnp.bfloat16),
            jax.ShapeDtypeStruct((docs, pairs, 2, 2, seq_len, seq_len), jnp.bfloat16),
        ),
        grid_spec=pltpu.PrefetchScalarGridSpec(
            num_scalar_prefetch=1,
            grid=(docs, pairs),
            in_specs=[
                pl.BlockSpec((None, seq_len, 1), per_doc),
                pl.BlockSpec((None, 1, seq_len), per_doc),
                pl.BlockSpec((None, 1, seq_len), per_doc),
                pl.BlockSpec((None, seq_len, PAIR), per_doc),
                tile, tile, tile, tile,
                pl.BlockSpec((2 * seq_len, PAIR), shared),
                pl.BlockSpec((3, PAIR), shared),
                pl.BlockSpec((2, PAIR), shared),
            ],
            out_specs=[
                tile, tile,
                pl.BlockSpec((None, None, 2, 2, seq_len, seq_len), lambda d, p, *_: (d, p, 0, 0, 0, 0)),
            ],
            scratch_shapes=[
                pltpu.VMEM((2, seq_len, seq_len), jnp.float32),
                pltpu.VMEM((seq_len, 2 * PAIR), jnp.bfloat16),
            ],
        ),
        name="attend_forward",
    )(lengths, rank_col, rank_row, live_row, seg_hot, proj_c, proj_q, keys, values, rel_keys, bias, embed)


def shear_left(value_in):
    rows, wide = value_in.shape
    pack = 16
    groups = []
    for group in range(rows // pack):
        piece = value_in[group * pack : (group + 1) * pack]
        groups.append(pltpu.roll(piece, wide - 1 - group * pack, 1))
    moved = jnp.concatenate(groups, axis=0)
    place = lax.broadcasted_iota(jnp.int32, (rows, wide), 0)
    step = 1
    while step < pack:
        moved = jnp.where((place & step) != 0, pltpu.roll(moved, wide - step, 1), moved)
        step = step * 2
    return moved


def attend_backward_body(
    seg_hot, proj_c, proj_q, key_ref, value_ref, rel_ref, bias_ref, embed_ref, vec_c, vec_q,
    grad_c, grad_q, prob_ref, gproj_c, gproj_q, gkey_ref, gvalue_ref, grel_ref, small_ref,
    ext_scr, key_acc, value_acc, rel_acc,
):
    seq_len = key_ref.shape[0]
    blocks = seq_len // ROWS
    wide = seq_len + ROWS
    ext_scr[:, :PAIR] = (key_ref[...].astype(jnp.float32) * 0.125).astype(jnp.bfloat16)
    ext_scr[:, PAIR:] = (seg_hot[...].astype(jnp.float32) * 0.125).astype(jnp.bfloat16)
    key_acc[...] = jnp.zeros_like(key_acc)
    value_acc[...] = jnp.zeros_like(value_acc)
    rel_acc[...] = jnp.zeros_like(rel_acc)
    lane = lane_ids(ROWS)
    first = lane < DH
    sums = [jnp.zeros((1, PAIR), jnp.float32) for _ in range(5)]
    for stream in range(2):
        proj_ref = (proj_c, proj_q)[stream]
        vec_ref = (vec_c, vec_q)[stream]
        grad_ref = (grad_c, grad_q)[stream]
        gproj_ref = (gproj_c, gproj_q)[stream]
        for block in range(blocks):
            rows = pl.ds(block * ROWS, ROWS)
            start = seq_len - (block + 1) * ROWS
            proj = proj_ref[rows, :]
            query_ct = jnp.transpose(((proj + bias_ref[0:1, :]) * 0.125).astype(jnp.bfloat16))
            query_pt = jnp.transpose(((proj + bias_ref[1:2, :]) * 0.125).astype(jnp.bfloat16))
            query_s = proj + bias_ref[2:3, :]
            hot = jnp.where(lane < 4, seg_hot[rows, :].astype(jnp.float32), 0.0)
            grad = grad_ref[rows, :]
            grad_t = jnp.transpose(grad)
            inner = grad.astype(jnp.float32) * vec_ref[rows, :].astype(jnp.float32)
            window = (rel_ref[pl.ds(start, wide), :].astype(jnp.float32) * 0.125).astype(jnp.bfloat16)
            parts = []
            for head in range(2):
                own = (lane >= DH) if head else first
                low, high = head * DH, (head + 1) * DH
                prob = prob_ref[stream, head, rows, :]
                grad_prob = nt(jnp.where(own, grad, jnp.zeros((), jnp.bfloat16)), value_ref[...])
                row_inner = jnp.sum(jnp.where(own, inner, 0.0), axis=1, keepdims=True)
                gscore = (prob.astype(jnp.float32) * (grad_prob - row_inner)).astype(jnp.bfloat16)
                value_acc[low:high, :] += nn(grad_t[low:high, :], prob)
                key_acc[low:high, :] += nn(query_ct[low:high, :], gscore)
                both = nn(gscore, ext_scr[...])
                table = jnp.concatenate([jnp.zeros((ROWS, ROWS), jnp.bfloat16), gscore], axis=1)
                table = shear_left(table)
                gpos = nn(table, window)
                rel_acc[low:high, start : start + wide] += nn(query_pt[low:high, :], table)
                tail = both[:, PAIR:]
                tail = jnp.where(lane < 4, tail, 0.0)
                g_same = jnp.sum(tail * hot, axis=1, keepdims=True)
                g_other = jnp.sum(tail, axis=1, keepdims=True) - g_same
                parts.append((both[:, :PAIR], gpos, g_same, g_other))
            g_content = jnp.where(first, parts[0][0], parts[1][0])
            g_position = jnp.where(first, parts[0][1], parts[1][1])
            g_same = jnp.where(first, parts[0][2], parts[1][2])
            g_other = jnp.where(first, parts[0][3], parts[1][3])
            g_segment = g_same * embed_ref[0:1, :] + g_other * embed_ref[1:2, :]
            gproj_ref[rows, :] = (g_content + g_position + g_segment).astype(jnp.bfloat16)
            terms = (g_content, g_position, g_segment, g_same * query_s, g_other * query_s)
            sums = [kept + jnp.sum(term, axis=0, keepdims=True) for kept, term in zip(sums, terms)]
    gkey_ref[...] = jnp.transpose(key_acc[...]).astype(jnp.bfloat16)
    gvalue_ref[...] = jnp.transpose(value_acc[...]).astype(jnp.bfloat16)
    grel_ref[...] = rel_acc[...].astype(jnp.bfloat16)
    small_ref[...] = jnp.concatenate(sums + [jnp.zeros((3, PAIR), jnp.float32)], axis=0)


def attend_backward(seg_hot, proj_c, proj_q, keys, values, rel_keys, bias, embed, vec_c, vec_q, grad_c, grad_q, prob):
    docs, seq_len, width = proj_c.shape
    pairs = width // PAIR
    per_doc = lambda d, p: (d, 0, 0)
    per_pair = lambda d, p: (d, 0, p)
    shared = lambda d, p: (0, p)
    tile = pl.BlockSpec((None, seq_len, PAIR), per_pair)
    low = jax.ShapeDtypeStruct((docs, seq_len, width), jnp.bfloat16)
    return pl.pallas_call(
        attend_backward_body,
        out_shape=(
            low, low, low, low,
            jax.ShapeDtypeStruct((docs, width, 2 * seq_len), jnp.bfloat16),
            jax.ShapeDtypeStruct((docs, 8, width), jnp.float32),
        ),
        grid_spec=pltpu.PrefetchScalarGridSpec(
            num_scalar_prefetch=0,
            grid=(docs, pairs),
            in_specs=[
                pl.BlockSpec((None, seq_len, PAIR), per_doc),
                tile, tile, tile, tile,
                pl.BlockSpec((2 * seq_len, PAIR), shared),
                pl.BlockSpec((3, PAIR), shared),
                pl.BlockSpec((2, PAIR), shared),
                tile, tile, tile, tile,
                pl.BlockSpec((None, None, 2, 2, seq_len, seq_len), lambda d, p: (d, p, 0, 0, 0, 0)),
            ],
            out_specs=[
                tile, tile, tile, tile,
                pl.BlockSpec((None, PAIR, 2 * seq_len), lambda d, p: (d, p, 0)),
                pl.BlockSpec((None, 8, PAIR), per_pair),
            ],
            scratch_shapes=[
                pltpu.VMEM((seq_len, 2 * PAIR), jnp.bfloat16),
                pltpu.VMEM((PAIR, seq_len), jnp.float32),
                pltpu.VMEM((PAIR, seq_len), jnp.float32),
                pltpu.VMEM((PAIR, 2 * seq_len), jnp.float32),
            ],
        ),
        name="attend_backward",
    )(seg_hot, proj_c, proj_q, keys, values, rel_keys, bias, embed, vec_c, vec_q, grad_c, grad_q, prob)


MESH = pl.DeviceIdType.MESH
FOLDS = 4


def sum_devices_body(dp_size, count, arrays, layout, offsets, *refs):
    inputs = refs[:arrays]
    small_in, out_ref, small_out = refs[arrays : arrays + 3]
    (
        work, swapped, landed, extra, small_work, small_land, load_sem, store_sem, swap_send, swap_recv,
        fold_send, fold_recv, spread_send, spread_recv, more_send, more_recv, tiny_send, tiny_recv,
    ) = refs[arrays + 3 :]
    rows = work.shape[1]
    place = lax.axis_index("dp")
    core = lax.axis_index("mp")
    strides = [1 + core, 2 - core, 4, 8]
    more = [16 << step for step in range(8) if (16 << step) < dp_size]
    bits = [(place // stride) % 2 for stride in strides]
    partners = [place + (1 - 2 * bit) * stride for bit, stride in zip(bits, strides)]
    more_partners = [place + (1 - 2 * ((place // stride) % 2)) * stride for stride in more]
    lengths = [rows >> (fold + 1) for fold in range(FOLDS)]
    starts, begin = [], 0
    for bit, length in zip(bits, lengths):
        begin = begin + bit * length
        starts.append(begin)
    land_at = [rows - 2 * length for length in lengths]

    def kept(fold):
        return pl.ds(pl.multiple_of(starts[fold], 16), lengths[fold])

    def given(fold):
        return pl.ds(pl.multiple_of(starts[fold] + (1 - 2 * bits[fold]) * lengths[fold], 16), lengths[fold])

    def remote(source, target, send, recv, device):
        return pltpu.make_async_remote_copy(
            src_ref=source, dst_ref=target, send_sem=send, recv_sem=recv,
            device_id=device, device_id_type=MESH,
        )

    def fold_copy(fold, piece):
        return remote(
            work.at[piece, given(fold)],
            landed.at[piece, pl.ds(land_at[fold], lengths[fold])],
            fold_send.at[fold, piece], fold_recv.at[fold, piece], {"dp": partners[fold]},
        )

    def spread_copy(fold, piece):
        return remote(
            swapped.at[piece, kept(fold)],
            swapped.at[piece, kept(fold)],
            spread_send.at[fold, piece], spread_recv.at[fold, piece], {"dp": partners[fold]},
        )

    def more_copy(step, piece):
        return remote(
            work.at[piece, kept(FOLDS - 1)],
            extra.at[step, piece],
            more_send.at[step, piece], more_recv.at[step, piece], {"dp": more_partners[step]},
        )

    def whole_swap(piece):
        return remote(
            work.at[piece], swapped.at[piece], swap_send.at[piece], swap_recv.at[piece], {"mp": 1 - core}
        )

    def whole_load(piece):
        return pltpu.make_async_copy(swapped.at[piece], work.at[piece], load_sem.at[piece])

    def store(piece):
        return pltpu.make_async_copy(swapped.at[piece], out_ref.at[piece], store_sem.at[piece])

    def add_rows(piece, where, other):
        mine = work[piece, where, :].astype(jnp.float32)
        work[piece, where, :] = (mine + other.astype(jnp.float32)).astype(jnp.bfloat16)

    tiny_devices = [{"mp": 1 - core}] + [{"dp": partner} for partner in partners + more_partners]

    def tiny_copy(step):
        return remote(
            small_in.at[1] if step == 0 else small_work.at[step],
            small_land.at[step], tiny_send.at[step], tiny_recv.at[step], tiny_devices[step],
        )

    barrier = pltpu.get_barrier_semaphore()
    for device in tiny_devices:
        pl.semaphore_signal(barrier, inc=1, device_id=device, device_id_type=MESH)
    pl.semaphore_wait(barrier, len(tiny_devices))

    tiny_copy(0).start()
    small_work[0] = small_in[0]
    for piece in range(count):
        for index, row, col, far_row, far_col, height, to_row in layout[piece]:
            width = work.shape[2]
            here = pl.ds(to_row, height)
            remote(
                inputs[index].at[pl.ds(far_row, height), pl.ds(far_col, width)],
                swapped.at[piece, here],
                swap_send.at[piece], swap_recv.at[piece], {"mp": 1 - core},
            ).start()
            pltpu.make_async_copy(
                inputs[index].at[pl.ds(row, height), pl.ds(col, width)], work.at[piece, here], load_sem.at[piece]
            ).start()

    def stage(number, piece):
        if number == 0:
            whole_load(piece).wait()
            whole_swap(piece).wait_recv()
            add_rows(piece, pl.ds(0, rows), swapped[piece])
            fold_copy(0, piece).start()
        elif number <= FOLDS:
            fold = number - 1
            fold_copy(fold, piece).wait_recv()
            add_rows(piece, kept(fold), landed[piece, pl.ds(land_at[fold], lengths[fold]), :])
            if fold + 1 < FOLDS:
                fold_copy(fold + 1, piece).start()
                return
            for step in range(len(more)):
                more_copy(step, piece).start()
                more_copy(step, piece).wait()
                add_rows(piece, kept(fold), extra[step, piece])
            swapped[piece, kept(fold), :] = work[piece, kept(fold), :]
            spread_copy(fold, piece).start()
        else:
            fold = 2 * FOLDS - number
            remote(
                swapped.at[piece, kept(fold)], swapped.at[piece, given(fold)],
                spread_send.at[fold, piece], spread_recv.at[fold, piece], {"dp": partners[fold]},
            ).wait_recv()
            if fold > 0:
                spread_copy(fold - 1, piece).start()
            else:
                store(piece).start()

    def advance(tick, carry):
        for step in range(len(tiny_devices)):
            @pl.when(tick == step + 1)
            def _():
                tiny_copy(step).wait_recv()
                small_work[step + 1] = small_work[step] + small_land[step]
                if step + 1 < len(tiny_devices):
                    tiny_copy(step + 1).start()

        for number in reversed(range(2 * FOLDS + 1)):
            piece = tick - offsets[number]

            @pl.when((piece >= 0) & (piece < count))
            def _():
                stage(number, piece)

        return carry

    lax.fori_loop(0, count + offsets[-1], advance, 0)
    small_out[...] = small_work[len(tiny_devices)]
    for step in range(len(tiny_devices)):
        tiny_copy(step).wait_send()

    def drain(piece, carry):
        whole_swap(piece).wait_send()
        for fold in range(FOLDS):
            fold_copy(fold, piece).wait_send()
            spread_copy(fold, piece).wait_send()
        store(piece).wait()
        return carry

    lax.fori_loop(0, count, drain, 0)


def sum_devices(dp_size, grads, layout, small, lag):
    rows = sum(part[5] for part in layout[0])
    cols = layout_width(grads, layout)
    count = len(layout)
    more = max(1, dp_size.bit_length() - 1 - FOLDS)
    stages = 2 * FOLDS + 1
    offsets = [number * lag for number in range(stages)]
    tiny = dp_size.bit_length()
    low = jnp.bfloat16
    dma = pltpu.SemaphoreType.DMA
    return pl.pallas_call(
        functools.partial(sum_devices_body, dp_size, count, len(grads), layout, offsets),
        out_shape=(
            jax.ShapeDtypeStruct((count, rows, cols), low),
            jax.ShapeDtypeStruct(small.shape[1:], jnp.float32),
        ),
        in_specs=[pl.BlockSpec(memory_space=pl.ANY)] * len(grads) + [pl.BlockSpec(memory_space=pltpu.VMEM)],
        out_specs=(pl.BlockSpec(memory_space=pl.ANY), pl.BlockSpec(memory_space=pltpu.VMEM)),
        scratch_shapes=[
            pltpu.VMEM((count, rows, cols), low),
            pltpu.VMEM((count, rows, cols), low),
            pltpu.VMEM((count, rows, cols), low),
            pltpu.VMEM((more, count, rows >> FOLDS, cols), low),
            pltpu.VMEM((tiny + 1,) + small.shape[1:], jnp.float32),
            pltpu.VMEM((tiny,) + small.shape[1:], jnp.float32),
            dma((count,)), dma((count,)), dma((count,)), dma((count,)),
            dma((FOLDS, count)), dma((FOLDS, count)), dma((FOLDS, count)), dma((FOLDS, count)),
            dma((more, count)), dma((more, count)), dma((tiny,)), dma((tiny,)),
        ],
        compiler_params=pltpu.CompilerParams(
            collective_id=0, has_side_effects=True, vmem_limit_bytes=48 << 20
        ),
        name="sum_devices",
    )(*grads, small)


def layout_width(grads, layout):
    return grads[0].shape[1] // 2


def piece_layout(up_at, down_at, out_at, square_at, cols, half_ff):
    width = 2 * cols
    pieces = []
    for rblock in range(half_ff // width):
        for cblock in range(2):
            pieces.append([(down_at, rblock * width, cblock * cols, half_ff + rblock * width, cblock * cols, width, 0)])
    for block in range(half_ff // cols):
        pieces.append([(up_at, 0, block * cols, 0, half_ff + block * cols, width, 0)])
    pieces.append([(out_at, 0, 0, cols, 0, cols, 0), (out_at, 0, cols, cols, cols, cols, cols)])
    for index in square_at:
        pieces.append([(index, 0, 0, 0, cols, width, 0)])
    return pieces


epsilon = 1e-06


def layer_norm(value_in, gain, shift):
    center = value_in - jnp.mean(value_in, axis=-1, keepdims=True)
    spread = jnp.mean(center * center, axis=-1, keepdims=True)
    return center * lax.rsqrt(spread + epsilon) * gain + shift


def gelu_tanh(value_in):
    return jax.nn.gelu(value_in, approximate=True)


def position_table(seq_len, width):
    distance = seq_len - 1.0 - np.arange(2 * seq_len - 1, dtype=np.float32)
    freq_exp = np.arange(0, width, 2).astype(np.float32) / np.float32(width)
    inverse = np.float32(1.0) / np.float32(10000.0) ** freq_exp
    angle = (distance[:, None] * inverse[None, :]).astype(np.float32)
    table = np.concatenate([np.sin(angle), np.cos(angle)], axis=1)
    table = np.concatenate([table, np.zeros((1, width), np.float32)], axis=0)
    return table.astype(ml_dtypes.bfloat16)


def dot_left(left_op, right_op):
    return lax.dot_general(
        left_op, right_op, (((0,), (0,)), ((), ())), preferred_element_type=jnp.float32
    )


def on_device(
    dp_size,
    content_in,
    query_in,
    doc_lengths,
    order_ranks,
    segment_ids,
    target_flags,
    query_weight,
    key_weight,
    value_weight,
    out_weight,
    rel_weight,
    content_bias,
    position_bias,
    segment_bias,
    segment_embed,
    first_gain,
    first_shift,
    up_weight,
    up_bias,
    down_weight,
    down_bias,
    second_gain,
    second_shift,
    content_cot,
    query_cot,
):
    docs_dev, half, width = content_in.shape
    seq_len = order_ranks.shape[1]
    mine = lax.axis_index("mp")
    wide_f = lambda value: value.astype(jnp.float32)
    low_f = lambda value: value.astype(jnp.bfloat16)

    def swap(value):
        return lax.ppermute(value, "mp", [(0, 1), (1, 0)])

    def gather_doc(value):
        keep = lax.dynamic_index_in_dim(value, mine, 0, keepdims=False)
        came = swap(lax.dynamic_index_in_dim(value, 1 - mine, 0, keepdims=False))
        head = jnp.where(mine == 0, keep, came)
        tail = jnp.where(mine == 0, came, keep)
        return jnp.concatenate([head, tail], axis=0)

    def return_doc(value):
        pair = value.reshape(2, half, width)
        keep = lax.dynamic_index_in_dim(pair, mine, 0, keepdims=False)
        came = swap(lax.dynamic_index_in_dim(pair, 1 - mine, 0, keepdims=False))
        return jnp.stack([jnp.where(mine == 0, keep, came), jnp.where(mine == 0, came, keep)])

    def both(value, axis):
        return jnp.concatenate([value, swap(value)], axis=axis)

    content = gather_doc(content_in)
    query = gather_doc(query_in)
    query_use = both(query_weight, 1)
    key_use = both(key_weight, 1)
    value_use = both(value_weight, 1)
    rel_use = both(rel_weight, 1)
    vectors = both(
        jnp.concatenate(
            [
                wide_f(content_bias)[None],
                wide_f(position_bias)[None],
                wide_f(segment_bias)[None],
                wide_f(segment_embed),
            ],
            axis=0,
        ),
        1,
    )
    bias, embed = vectors[:3], vectors[3:]
    out_use = both(out_weight, 0)
    up_use = both(up_weight, 1)
    down_use = both(down_weight, 0)
    up_bias_use = both(wide_f(up_bias)[None], 1)
    cot = jnp.concatenate([gather_doc(content_cot), gather_doc(query_cot)], axis=0)

    lengths = lax.dynamic_slice_in_dim(doc_lengths, mine, 1, 0)
    ranks = lax.dynamic_slice_in_dim(order_ranks, mine, 1, 0)
    segments = lax.dynamic_slice_in_dim(segment_ids, mine, 1, 0)
    targets = lax.dynamic_slice_in_dim(target_flags, mine, 1, 0)
    live = targets * (jnp.arange(seq_len) >= 2).astype(jnp.int32)[None]
    lanes = jnp.arange(PAIR)
    seg_hot = low_f((segments[:, :, None] == lanes % 4) & (lanes < 8))
    table = jnp.asarray(position_table(seq_len, width))
    rel_keys = low_f(nn(table, rel_use))
    proj_c = nn(content, query_use)[None]
    proj_q = nn(query, query_use)[None]
    keys = low_f(nn(content, key_use))[None]
    values = low_f(nn(content, value_use))[None]
    vec_c, vec_q, prob = attend_forward(
        lengths, ranks[:, :, None], ranks[:, None, :], live[:, None, :], seg_hot,
        proj_c, proj_q, keys, values, rel_keys, bias, embed,
    )
    vec = jnp.concatenate([vec_c[0], vec_q[0]], axis=0)
    resid = jnp.concatenate([content, query], axis=0)
    gain_first, shift_first = wide_f(first_gain), wide_f(first_shift)
    gain_second, shift_second = wide_f(second_gain), wide_f(second_shift)
    pre1 = nn(vec, out_use) + wide_f(resid)
    first = low_f(layer_norm(pre1, gain_first, shift_first))
    hidden = nn(first, up_use) + up_bias_use
    act = low_f(gelu_tanh(hidden))
    pre2 = wide_f(first) + nn(act, down_use) + wide_f(down_bias)
    norm2, pull2 = jax.vjp(layer_norm, pre2, gain_second, shift_second)
    out_rows = low_f(norm2)
    grad_pre2, g_gain2, g_shift2 = pull2(wide_f(cot))
    g_down_bias = jnp.sum(grad_pre2, axis=0)
    grad_down = low_f(grad_pre2)
    grad_act = nt(grad_down, down_use)
    grad_hidden = low_f(jax.vjp(gelu_tanh, hidden)[1](grad_act)[0])
    g_up_bias = jnp.sum(wide_f(grad_hidden), axis=0)
    back = nt(grad_hidden, up_use)
    grad_pre1, g_gain1, g_shift1 = jax.vjp(layer_norm, pre1, gain_first, shift_first)[1](back + grad_pre2)
    grad_mixed = low_f(grad_pre1)
    grad_vec = low_f(nt(grad_mixed, out_use))

    ff = up_weight.shape[1]
    cols = query_weight.shape[1]

    g_down = low_f(dot_left(act, grad_down))
    g_up = low_f(dot_left(first, grad_hidden))
    g_out = low_f(dot_left(vec, grad_mixed))

    gproj_c, gproj_q, gkeys, gvalues, grel, small = attend_backward(
        seg_hot, proj_c, proj_q, keys, values, rel_keys, bias, embed, vec_c, vec_q,
        grad_vec[None, :seq_len], grad_vec[None, seq_len:], prob,
    )
    gproj = jnp.concatenate([gproj_c[0], gproj_q[0]], axis=0)
    g_query = low_f(dot_left(resid, gproj))
    g_key = low_f(dot_left(content, gkeys[0]))
    g_value = low_f(dot_left(content, gvalues[0]))
    g_rel = low_f(lax.dot_general(table, grel[0], (((0,), (1,)), ((), ())), preferred_element_type=jnp.float32))
    content_grad = low_f(
        nt(gproj_c[0], query_use) + nt(gkeys[0], key_use) + nt(gvalues[0], value_use) + grad_pre1[:seq_len]
    )
    query_grad = low_f(nt(gproj_q[0], query_use) + grad_pre1[seq_len:])

    small = small[0]
    up_rows = ff // cols
    halves = jnp.concatenate(
        [jnp.stack([small[:5, :cols], small[:5, cols:]]), g_up_bias.reshape(2, up_rows, cols)], axis=1
    )
    same = jnp.stack([g_gain1, g_shift1, g_gain2, g_shift2, g_down_bias]).reshape(2 * 5, cols)
    split_rows = 5 + up_rows
    filler = jnp.zeros((2, (-split_rows - 10) % 8, cols), jnp.float32)
    packed = jnp.concatenate([halves, jnp.stack([same, same]), filler], axis=1)
    layout = piece_layout(1, 0, 2, (3, 4, 5, 6), cols, ff)
    pieces, tiny = sum_devices(
        dp_size, [g_down, g_up, g_out, g_query, g_key, g_value, g_rel], layout, packed, 2
    )
    pieces = wide_f(pieces)
    down_count = 2 * (ff // width)
    down_sum = jnp.concatenate(
        [jnp.concatenate([pieces[at], pieces[at + 1]], axis=1) for at in range(0, down_count, 2)], axis=0
    )
    up_sum = jnp.concatenate([pieces[down_count + at] for at in range(up_rows)], axis=1)
    at = down_count + up_rows
    out_sum = jnp.concatenate([pieces[at, :cols], pieces[at, cols:]], axis=1)
    same_part = tiny[split_rows : split_rows + 10].reshape(5, width)
    split_part = tiny[:5]
    return (
        return_doc(out_rows[:seq_len]),
        return_doc(out_rows[seq_len:]),
        return_doc(content_grad),
        return_doc(query_grad),
        pieces[at + 1],
        pieces[at + 2],
        pieces[at + 3],
        out_sum,
        pieces[at + 4],
        split_part[0],
        split_part[1],
        split_part[2],
        split_part[3:5],
        same_part[0],
        same_part[1],
        up_sum,
        tiny[5:split_rows].reshape(ff),
        down_sum,
        same_part[4],
        same_part[2],
        same_part[3],
    )


def solution(mesh):
    placed = (
        P("dp", "mp", None),
        P("dp", "mp", None),
        P("dp"),
        P("dp", None),
        P("dp", None),
        P("dp", None),
        P(None, "mp"),
        P(None, "mp"),
        P(None, "mp"),
        P("mp", None),
        P(None, "mp"),
        P("mp"),
        P("mp"),
        P("mp"),
        P(None, "mp"),
        P(),
        P(),
        P(None, "mp"),
        P("mp"),
        P("mp", None),
        P(),
        P(),
        P(),
        P("dp", "mp", None),
        P("dp", "mp", None),
    )
    return jax.shard_map(
        functools.partial(on_device, mesh.shape["dp"]),
        mesh=mesh,
        in_specs=placed,
        out_specs=(
            P("dp", "mp", None),
            P("dp", "mp", None),
            P("dp", "mp", None),
            P("dp", "mp", None),
            P(None, "mp"),
            P(None, "mp"),
            P(None, "mp"),
            P("mp", None),
            P(None, "mp"),
            P("mp"),
            P("mp"),
            P("mp"),
            P(None, "mp"),
            P(),
            P(),
            P(None, "mp"),
            P("mp"),
            P("mp", None),
            P(),
            P(),
            P(),
        ),
        check_vma=False,
    )
```

```python
import functools

import jax
import jax.numpy as jnp
import ml_dtypes
import numpy as np
from jax import lax
from jax.experimental import pallas as pl
from jax.experimental.pallas import tpu as pltpu
from jax.sharding import PartitionSpec as P

DH = 64
PAIR = 2 * DH
ROWS = 256
NEG = -1e30


def nt(left_op, right_op):
    return lax.dot_general(
        left_op, right_op, (((1,), (1,)), ((), ())), preferred_element_type=jnp.float32
    )


def nn(left_op, right_op):
    return jnp.dot(left_op, right_op, preferred_element_type=jnp.float32)


def lane_ids(rows):
    return lax.broadcasted_iota(jnp.int32, (rows, PAIR), 1)


def attend_forward_body(
    len_ref, rank_col, rank_row, live_row, seg_hot, proj_c, proj_q, key_ref, value_ref, rel_ref,
    bias_ref, embed_ref, vec_c, vec_q, prob_ref, mask_scr, ext_scr,
):
    seq_len = key_ref.shape[0]
    blocks = seq_len // ROWS
    wide = seq_len + ROWS

    @pl.when(pl.program_id(1) == 0)
    def _():
        length = len_ref[pl.program_id(0)]
        for block in range(blocks):
            rows = pl.ds(block * ROWS, ROWS)
            place_j = lax.broadcasted_iota(jnp.int32, (ROWS, seq_len), 1)
            place_i = lax.broadcasted_iota(jnp.int32, (ROWS, seq_len), 0) + block * ROWS
            visible = (place_j < length) & (
                (live_row[...] == 0) | (rank_row[...] < rank_col[rows, :])
            )
            diagonal = place_i == place_j
            mask_scr[0, rows, :] = jnp.where(visible | diagonal, 0.0, NEG)
            mask_scr[1, rows, :] = jnp.where(visible & jnp.logical_not(diagonal), 0.0, NEG)

    ext_scr[:, :PAIR] = key_ref[...]
    ext_scr[:, PAIR:] = seg_hot[...]
    lane = lane_ids(ROWS)
    diff = embed_ref[0:1, :] - embed_ref[1:2, :]
    for stream in range(2):
        proj_ref = (proj_c, proj_q)[stream]
        vec_ref = (vec_c, vec_q)[stream]
        for block in range(blocks):
            rows = pl.ds(block * ROWS, ROWS)
            proj = proj_ref[rows, :]
            query_c = ((proj + bias_ref[0:1, :]) * 0.125).astype(jnp.bfloat16)
            query_p = ((proj + bias_ref[1:2, :]) * 0.125).astype(jnp.bfloat16)
            seg_gap = (proj + bias_ref[2:3, :]) * (diff * 0.125)
            hot = seg_hot[rows, :].astype(jnp.float32)
            window = rel_ref[pl.ds(seq_len - (block + 1) * ROWS, wide), :]
            vec_pair = None
            for head in range(2):
                own = (lane >= DH) if head else (lane < DH)
                zero = jnp.zeros((), jnp.bfloat16)
                gap = jnp.sum(jnp.where(own, seg_gap, 0.0), axis=1, keepdims=True)
                gap_high = gap.astype(jnp.bfloat16).astype(jnp.float32)
                seg_part = (jnp.where(lane < 4, gap_high, gap - gap_high) * hot).astype(jnp.bfloat16)
                left = jnp.concatenate([jnp.where(own, query_c, zero), seg_part], axis=1)
                scores = nt(left, ext_scr[...])
                table = nt(jnp.where(own, query_p, zero), window)
                table = pltpu.roll(table, 1, 1, stride=1, stride_axis=0)
                scores = scores + table[:, ROWS:] + mask_scr[stream, rows, :]
                top = jnp.max(scores, axis=1, keepdims=True)
                terms = jnp.exp(scores - top)
                total = jnp.sum(terms, axis=1, keepdims=True)
                prob = (terms * (1.0 / total)).astype(jnp.bfloat16)
                prob_ref[stream, head, rows, :] = prob
                part = nn(prob, value_ref[...])
                vec_pair = part if head == 0 else jnp.where(own, part, vec_pair)
            vec_ref[rows, :] = vec_pair.astype(jnp.bfloat16)


def attend_forward(lengths, rank_col, rank_row, live_row, seg_hot, proj_c, proj_q, keys, values, rel_keys, bias, embed):
    docs, seq_len, width = proj_c.shape
    pairs = width // PAIR
    per_doc = lambda d, p, *_: (d, 0, 0)
    per_pair = lambda d, p, *_: (d, 0, p)
    shared = lambda d, p, *_: (0, p)
    tile = pl.BlockSpec((None, seq_len, PAIR), per_pair)
    return pl.pallas_call(
        attend_forward_body,
        out_shape=(
            jax.ShapeDtypeStruct((docs, seq_len, width), jnp.bfloat16),
            jax.ShapeDtypeStruct((docs, seq_len, width), jnp.bfloat16),
            jax.ShapeDtypeStruct((docs, pairs, 2, 2, seq_len, seq_len), jnp.bfloat16),
        ),
        grid_spec=pltpu.PrefetchScalarGridSpec(
            num_scalar_prefetch=1,
            grid=(docs, pairs),
            in_specs=[
                pl.BlockSpec((None, seq_len, 1), per_doc),
                pl.BlockSpec((None, 1, seq_len), per_doc),
                pl.BlockSpec((None, 1, seq_len), per_doc),
                pl.BlockSpec((None, seq_len, PAIR), per_doc),
                tile, tile, tile, tile,
                pl.BlockSpec((2 * seq_len, PAIR), shared),
                pl.BlockSpec((3, PAIR), shared),
                pl.BlockSpec((2, PAIR), shared),
            ],
            out_specs=[
                tile, tile,
                pl.BlockSpec((None, None, 2, 2, seq_len, seq_len), lambda d, p, *_: (d, p, 0, 0, 0, 0)),
            ],
            scratch_shapes=[
                pltpu.VMEM((2, seq_len, seq_len), jnp.float32),
                pltpu.VMEM((seq_len, 2 * PAIR), jnp.bfloat16),
            ],
        ),
        name="attend_forward",
    )(lengths, rank_col, rank_row, live_row, seg_hot, proj_c, proj_q, keys, values, rel_keys, bias, embed)


MESH = pl.DeviceIdType.MESH
FOLDS = 4
LAG = 2


def shear_left(value_in):
    rows, wide = value_in.shape
    pack = 16
    groups = []
    for group in range(rows // pack):
        piece = value_in[group * pack : (group + 1) * pack]
        groups.append(pltpu.roll(piece, wide - 1 - group * pack, 1))
    moved = jnp.concatenate(groups, axis=0)
    place = lax.broadcasted_iota(jnp.int32, (rows, wide), 0)
    step = 1
    while step < pack:
        moved = jnp.where((place & step) != 0, pltpu.roll(moved, wide - step, 1), moved)
        step = step * 2
    return moved


def attend_backward_body(dp_size, layout, count, *refs):
    (
        seg_hot, proj_c, proj_q, key_ref, value_ref, rel_ref, bias_ref, embed_ref, vec_c, vec_q,
        grad_c, grad_q, prob_ref, content_t, query_t, table_t, small_in, down_in, up_in, out_in,
        gproj_c, gproj_q, gkey_ref, gvalue_ref, sum_out, small_out,
        ext_scr, key_acc, value_acc, rel_acc, work, swapped, landed, extra, far_work,
        small_work, small_far, small_land, load_sem, store_sem, swap_send, swap_recv,
        fold_send, fold_recv, spread_send, spread_recv, more_send, more_recv, tiny_send, tiny_recv,
    ) = refs
    inputs = (down_in, up_in, out_in)
    step_at = pl.program_id(0)
    steps = pl.num_programs(0)
    half_steps = 3
    early = len(layout)
    rows, cols = work.shape[1:]
    place = lax.axis_index("dp")
    core = lax.axis_index("mp")
    strides = [1 + core, 2 - core, 4, 8]
    more = [16 << step for step in range(8) if (16 << step) < dp_size]
    bits = [(place // stride) % 2 for stride in strides]
    partners = [place + (1 - 2 * bit) * stride for bit, stride in zip(bits, strides)]
    more_partners = [place + (1 - 2 * ((place // stride) % 2)) * stride for stride in more]
    lengths = [rows >> (fold + 1) for fold in range(FOLDS)]
    starts, begin = [], 0
    for bit, length in zip(bits, lengths):
        begin = begin + bit * length
        starts.append(begin)
    land_at = [rows - 2 * length for length in lengths]
    offsets = [number * LAG for number in range(2 * FOLDS + 1)]

    def kept(fold):
        return pl.ds(pl.multiple_of(starts[fold], 16), lengths[fold])

    def given(fold):
        return pl.ds(pl.multiple_of(starts[fold] + (1 - 2 * bits[fold]) * lengths[fold], 16), lengths[fold])

    def remote(source, target, send, recv, device):
        return pltpu.make_async_remote_copy(
            src_ref=source, dst_ref=target, send_sem=send, recv_sem=recv,
            device_id=device, device_id_type=MESH,
        )

    def fold_copy(fold, piece):
        return remote(
            work.at[piece, given(fold)],
            landed.at[piece, pl.ds(land_at[fold], lengths[fold])],
            fold_send.at[fold, piece], fold_recv.at[fold, piece], {"dp": partners[fold]},
        )

    def spread_copy(fold, piece):
        return remote(
            swapped.at[piece, kept(fold)],
            swapped.at[piece, kept(fold)],
            spread_send.at[fold, piece], spread_recv.at[fold, piece], {"dp": partners[fold]},
        )

    def more_copy(step, piece):
        return remote(
            work.at[piece, kept(FOLDS - 1)],
            extra.at[step, piece],
            more_send.at[step, piece], more_recv.at[step, piece], {"dp": more_partners[step]},
        )

    def whole_swap(piece):
        return remote(
            work.at[piece], swapped.at[piece], swap_send.at[piece], swap_recv.at[piece], {"mp": 1 - core}
        )

    def late_swap(late):
        return remote(
            far_work.at[late], swapped.at[early + late],
            swap_send.at[early + late], swap_recv.at[early + late], {"mp": 1 - core},
        )

    def whole_load(piece):
        return pltpu.make_async_copy(swapped.at[piece], work.at[piece], load_sem.at[piece])

    def store(piece):
        return pltpu.make_async_copy(swapped.at[piece], sum_out.at[piece], store_sem.at[piece])

    def add_rows(piece, where, other):
        mine = work[piece, where, :].astype(jnp.float32)
        work[piece, where, :] = (mine + other.astype(jnp.float32)).astype(jnp.bfloat16)

    tiny_devices = [{"mp": 1 - core}] + [{"dp": partner} for partner in partners + more_partners]

    def tiny_copy(step):
        return remote(
            small_far if step == 0 else small_work.at[step],
            small_land.at[step], tiny_send.at[step], tiny_recv.at[step], tiny_devices[step],
        )

    @pl.when(step_at == 0)
    def _():
        barrier = pltpu.get_barrier_semaphore()
        for device in tiny_devices:
            pl.semaphore_signal(barrier, inc=1, device_id=device, device_id_type=MESH)
        pl.semaphore_wait(barrier, len(tiny_devices))
        for piece in range(early):
            for index, row, col, far_row, far_col, height, to_row in layout[piece]:
                here = pl.ds(to_row, height)
                remote(
                    inputs[index].at[pl.ds(far_row, height), pl.ds(far_col, cols)],
                    swapped.at[piece, here],
                    swap_send.at[piece], swap_recv.at[piece], {"mp": 1 - core},
                ).start()
                pltpu.make_async_copy(
                    inputs[index].at[pl.ds(row, height), pl.ds(col, cols)], work.at[piece, here], load_sem.at[piece]
                ).start()
        small_work[0] = small_in[0]
        small_far[...] = small_in[1]

    def stage(number, piece):
        if number == 0:
            @pl.when(piece < early)
            def _():
                whole_load(piece).wait()
                whole_swap(piece).wait_recv()
                add_rows(piece, pl.ds(0, rows), swapped[piece])

            fold_copy(0, piece).start()
        elif number <= FOLDS:
            fold = number - 1
            fold_copy(fold, piece).wait_recv()
            add_rows(piece, kept(fold), landed[piece, pl.ds(land_at[fold], lengths[fold]), :])
            if fold + 1 < FOLDS:
                fold_copy(fold + 1, piece).start()
                return
            for step in range(len(more)):
                more_copy(step, piece).start()
                more_copy(step, piece).wait()
                add_rows(piece, kept(fold), extra[step, piece])
            swapped[piece, kept(fold), :] = work[piece, kept(fold), :]
            spread_copy(fold, piece).start()
        else:
            fold = 2 * FOLDS - number
            remote(
                swapped.at[piece, kept(fold)], swapped.at[piece, given(fold)],
                spread_send.at[fold, piece], spread_recv.at[fold, piece], {"dp": partners[fold]},
            ).wait_recv()
            if fold > 0:
                spread_copy(fold - 1, piece).start()
            else:
                store(piece).start()

    def advance(tick):
        for number in reversed(range(2 * FOLDS + 1)):
            piece = tick - offsets[number]

            @pl.when((piece >= 0) & (piece < count))
            def _():
                stage(number, piece)

    seq_len = key_ref.shape[0]
    blocks = seq_len // ROWS
    wide = seq_len + ROWS
    ext_scr[:, :PAIR] = (key_ref[...].astype(jnp.float32) * 0.125).astype(jnp.bfloat16)
    ext_scr[:, PAIR:] = (seg_hot[...].astype(jnp.float32) * 0.125).astype(jnp.bfloat16)
    key_acc[...] = jnp.zeros_like(key_acc)
    value_acc[...] = jnp.zeros_like(value_acc)
    rel_acc[...] = jnp.zeros_like(rel_acc)
    lane = lane_ids(ROWS)
    first = lane < DH
    sums = [jnp.zeros((1, PAIR), jnp.float32) for _ in range(5)]
    for stream in range(2):
        proj_ref = (proj_c, proj_q)[stream]
        vec_ref = (vec_c, vec_q)[stream]
        grad_ref = (grad_c, grad_q)[stream]
        gproj_ref = (gproj_c, gproj_q)[stream]
        for block in range(blocks):
            where = pl.ds(block * ROWS, ROWS)
            start = seq_len - (block + 1) * ROWS
            proj = proj_ref[where, :]
            query_ct = jnp.transpose(((proj + bias_ref[0:1, :]) * 0.125).astype(jnp.bfloat16))
            query_pt = jnp.transpose(((proj + bias_ref[1:2, :]) * 0.125).astype(jnp.bfloat16))
            query_s = proj + bias_ref[2:3, :]
            hot = jnp.where(lane < 4, seg_hot[where, :].astype(jnp.float32), 0.0)
            grad = grad_ref[where, :]
            grad_t = jnp.transpose(grad)
            inner = grad.astype(jnp.float32) * vec_ref[where, :].astype(jnp.float32)
            window = (rel_ref[pl.ds(start, wide), :].astype(jnp.float32) * 0.125).astype(jnp.bfloat16)
            parts = []
            for head in range(2):
                own = (lane >= DH) if head else first
                low, high = head * DH, (head + 1) * DH
                prob = prob_ref[stream, head, where, :]
                grad_prob = nt(jnp.where(own, grad, jnp.zeros((), jnp.bfloat16)), value_ref[...])
                row_inner = jnp.sum(jnp.where(own, inner, 0.0), axis=1, keepdims=True)
                gscore = (prob.astype(jnp.float32) * (grad_prob - row_inner)).astype(jnp.bfloat16)
                value_acc[low:high, :] += nn(grad_t[low:high, :], prob)
                key_acc[low:high, :] += nn(query_ct[low:high, :], gscore)
                both = nn(gscore, ext_scr[...])
                table = jnp.concatenate([jnp.zeros((ROWS, ROWS), jnp.bfloat16), gscore], axis=1)
                table = shear_left(table)
                gpos = nn(table, window)
                rel_acc[low:high, start : start + wide] += nn(query_pt[low:high, :], table)
                tail = both[:, PAIR:]
                tail = jnp.where(lane < 4, tail, 0.0)
                g_same = jnp.sum(tail * hot, axis=1, keepdims=True)
                g_other = jnp.sum(tail, axis=1, keepdims=True) - g_same
                parts.append((both[:, :PAIR], gpos, g_same, g_other))
            g_content = jnp.where(first, parts[0][0], parts[1][0])
            g_position = jnp.where(first, parts[0][1], parts[1][1])
            g_same = jnp.where(first, parts[0][2], parts[1][2])
            g_other = jnp.where(first, parts[0][3], parts[1][3])
            g_segment = g_same * embed_ref[0:1, :] + g_other * embed_ref[1:2, :]
            gproj_ref[where, :] = (g_content + g_position + g_segment).astype(jnp.bfloat16)
            terms = (g_content, g_position, g_segment, g_same * query_s, g_other * query_s)
            sums = [kept_sum + jnp.sum(term, axis=0, keepdims=True) for kept_sum, term in zip(sums, terms)]
        if stream == 0:
            advance(2 * step_at)
    gkey_ref[...] = jnp.transpose(key_acc[...]).astype(jnp.bfloat16)
    gvalue_ref[...] = jnp.transpose(value_acc[...]).astype(jnp.bfloat16)
    g_query = nn(content_t[...], gproj_c[...]) + nn(query_t[...], gproj_q[...])
    g_key = nn(content_t[...], gkey_ref[...])
    g_value = nn(content_t[...], gvalue_ref[...])
    g_rel = nt(table_t[...], rel_acc[...].astype(jnp.bfloat16))
    vectors = jnp.concatenate(sums, axis=0)

    @pl.when(step_at < half_steps)
    def _():
        lanes = pl.ds(pl.multiple_of(step_at * PAIR, PAIR), PAIR)
        far_work[step_at, :, 0:PAIR] = g_query.astype(jnp.bfloat16)
        far_work[step_at, :, PAIR : 2 * PAIR] = g_key.astype(jnp.bfloat16)
        far_work[step_at, :, 2 * PAIR :] = g_value.astype(jnp.bfloat16)
        far_work[half_steps, :, lanes] = g_rel.astype(jnp.bfloat16)
        small_far[0:5, lanes] = vectors
        late_swap(step_at).start()

        @pl.when(step_at == half_steps - 1)
        def _():
            late_swap(half_steps).start()
            tiny_copy(0).start()

    @pl.when(step_at >= half_steps)
    def _():
        late = step_at - half_steps
        lanes = pl.ds(pl.multiple_of(late * PAIR, PAIR), PAIR)
        late_swap(late).wait_recv()
        for at, value in enumerate((g_query, g_key, g_value)):
            cut = slice(at * PAIR, (at + 1) * PAIR)
            value = value + swapped[early + late, :, cut].astype(jnp.float32)
            work[early + late, :, cut] = value.astype(jnp.bfloat16)
        work[early + half_steps, :, lanes] = g_rel.astype(jnp.bfloat16)
        small_work[0, 0:5, lanes] = vectors

        @pl.when(step_at == steps - 1)
        def _():
            late_swap(half_steps).wait_recv()
            add_rows(early + half_steps, pl.ds(0, rows), swapped[early + half_steps])

    advance(2 * step_at + 1)

    @pl.when(step_at == steps - 1)
    def _():
        begin_tick = 2 * 2 * half_steps

        def finish(tick, carry):
            for step in range(len(tiny_devices)):
                @pl.when(tick == begin_tick + 1 + step)
                def _():
                    tiny_copy(step).wait_recv()
                    small_work[step + 1] = small_work[step] + small_land[step]
                    if step + 1 < len(tiny_devices):
                        tiny_copy(step + 1).start()

            advance(tick)
            return carry

        lax.fori_loop(begin_tick, count + offsets[-1], finish, 0)
        small_out[...] = small_work[len(tiny_devices)]
        for step in range(len(tiny_devices)):
            tiny_copy(step).wait_send()

        def drain(piece, carry):
            whole_swap(piece).wait_send()
            for fold in range(FOLDS):
                fold_copy(fold, piece).wait_send()
                spread_copy(fold, piece).wait_send()
            store(piece).wait()
            return carry

        lax.fori_loop(0, count, drain, 0)


def piece_layout(cols, half_ff):
    width = 2 * cols
    pieces = []
    for rblock in range(half_ff // width):
        for cblock in range(2):
            pieces.append([(0, rblock * width, cblock * cols, half_ff + rblock * width, cblock * cols, width, 0)])
    for block in range(half_ff // cols):
        pieces.append([(1, 0, block * cols, 0, half_ff + block * cols, width, 0)])
    pieces.append([(2, 0, 0, cols, 0, cols, 0), (2, 0, cols, cols, cols, cols, cols)])
    return pieces


def attend_backward(
    dp_size, layout, seg_hot, proj_c, proj_q, keys, values, rel_keys, bias, embed, vec_c, vec_q,
    grad_c, grad_q, prob, content_t, query_t, table_t, small, g_down, g_up, g_out,
):
    seq_len, width = proj_c.shape
    pairs = width // PAIR
    cols = width // 2
    rows = width
    count = len(layout) + 4
    more = max(1, dp_size.bit_length() - 1 - FOLDS)
    tiny = dp_size.bit_length()
    low = jnp.bfloat16
    dma = pltpu.SemaphoreType.DMA
    whole = lambda g: (0, 0)
    turn = lambda g: (g + pairs // 2) % pairs
    per_pair = lambda g: (0, turn(g))
    tile = pl.BlockSpec((seq_len, PAIR), per_pair)
    once = pl.Buffered(1)
    anywhere = pl.BlockSpec(memory_space=pl.ANY)
    low_rows = jax.ShapeDtypeStruct((seq_len, width), low)
    return pl.pallas_call(
        functools.partial(attend_backward_body, dp_size, layout, count),
        out_shape=(
            low_rows, low_rows, low_rows, low_rows,
            jax.ShapeDtypeStruct((count, rows, cols), low),
            jax.ShapeDtypeStruct(small.shape[1:], jnp.float32),
        ),
        grid_spec=pltpu.PrefetchScalarGridSpec(
            num_scalar_prefetch=0,
            grid=(pairs,),
            in_specs=[
                pl.BlockSpec((seq_len, PAIR), whole, pipeline_mode=once),
                tile, tile, tile, tile,
                pl.BlockSpec((2 * seq_len, PAIR), per_pair),
                pl.BlockSpec((3, PAIR), per_pair),
                pl.BlockSpec((2, PAIR), per_pair),
                tile, tile, tile, tile,
                pl.BlockSpec((None, 2, 2, seq_len, seq_len), lambda g: (turn(g), 0, 0, 0, 0)),
                pl.BlockSpec((width, seq_len), whole, pipeline_mode=once),
                pl.BlockSpec((width, seq_len), whole, pipeline_mode=once),
                pl.BlockSpec((width, 2 * seq_len), whole, pipeline_mode=once),
                pl.BlockSpec(small.shape, lambda g: (0, 0, 0), pipeline_mode=once),
                anywhere, anywhere, anywhere,
            ],
            out_specs=[
                tile, tile, tile, tile,
                anywhere,
                pl.BlockSpec(small.shape[1:], whole),
            ],
            scratch_shapes=[
                pltpu.VMEM((seq_len, 2 * PAIR), low),
                pltpu.VMEM((PAIR, seq_len), jnp.float32),
                pltpu.VMEM((PAIR, seq_len), jnp.float32),
                pltpu.VMEM((PAIR, 2 * seq_len), jnp.float32),
                pltpu.VMEM((count, rows, cols), low),
                pltpu.VMEM((count, rows, cols), low),
                pltpu.VMEM((count, rows, cols), low),
                pltpu.VMEM((more, count, rows >> FOLDS, cols), low),
                pltpu.VMEM((4, rows, cols), low),
                pltpu.VMEM((tiny + 1,) + small.shape[1:], jnp.float32),
                pltpu.VMEM(small.shape[1:], jnp.float32),
                pltpu.VMEM((tiny,) + small.shape[1:], jnp.float32),
                dma((count,)), dma((count,)), dma((count,)), dma((count,)),
                dma((FOLDS, count)), dma((FOLDS, count)), dma((FOLDS, count)), dma((FOLDS, count)),
                dma((more, count)), dma((more, count)), dma((tiny,)), dma((tiny,)),
            ],
        ),
        compiler_params=pltpu.CompilerParams(
            collective_id=0, has_side_effects=True, vmem_limit_bytes=60 << 20
        ),
        name="attend_backward",
    )(
        seg_hot, proj_c, proj_q, keys, values, rel_keys, bias, embed, vec_c, vec_q,
        grad_c, grad_q, prob, content_t, query_t, table_t, small, g_down, g_up, g_out,
    )


def finish_body(counts, piece_ref, down_ref, up_ref, out_ref, query_ref, key_ref, value_ref, rel_ref):
    down_count, up_count = counts
    at = pl.program_id(0)
    cols = piece_ref.shape[1]
    value = piece_ref[...].astype(jnp.float32)
    tail = down_count + up_count

    @pl.when(at < down_count)
    def _():
        down_ref[...] = value

    @pl.when((at >= down_count) & (at < tail))
    def _():
        up_ref[...] = value

    @pl.when(at == tail)
    def _():
        out_ref[:, :cols] = value[:cols]
        out_ref[:, cols:] = value[cols:]

    for turn in range(3):
        lanes = slice(turn * PAIR, (turn + 1) * PAIR)

        @pl.when(at == tail + 1 + turn)
        def _():
            query_ref[:, lanes] = value[:, :PAIR]
            key_ref[:, lanes] = value[:, PAIR : 2 * PAIR]
            value_ref[:, lanes] = value[:, 2 * PAIR :]

    @pl.when(at == tail + 4)
    def _():
        rel_ref[...] = value


def finish(pieces, half_ff):
    count, rows, cols = pieces.shape
    down_count, up_count = 2 * (half_ff // rows), half_ff // cols
    square = jax.ShapeDtypeStruct((rows, cols), jnp.float32)
    whole = lambda p: (0, 0)
    block = pl.BlockSpec((rows, cols), whole)

    def down_at(p):
        turn = jnp.minimum(p, down_count - 1)
        return (turn // 2, turn % 2)

    return pl.pallas_call(
        functools.partial(finish_body, (down_count, up_count)),
        out_shape=(
            jax.ShapeDtypeStruct((half_ff, rows), jnp.float32),
            jax.ShapeDtypeStruct((rows, half_ff), jnp.float32),
            jax.ShapeDtypeStruct((cols, rows), jnp.float32),
            square, square, square, square,
        ),
        grid=(count,),
        in_specs=[pl.BlockSpec((None, rows, cols), lambda p: (p, 0, 0))],
        out_specs=[
            pl.BlockSpec((rows, cols), down_at),
            pl.BlockSpec((rows, cols), lambda p: (0, jnp.clip(p - down_count, 0, up_count - 1))),
            pl.BlockSpec((cols, rows), whole),
            block, block, block, block,
        ],
        compiler_params=pltpu.CompilerParams(vmem_limit_bytes=40 << 20),
        name="finish",
    )(pieces)


epsilon = 1e-06


def layer_norm(value_in, gain, shift):
    center = value_in - jnp.mean(value_in, axis=-1, keepdims=True)
    spread = jnp.mean(center * center, axis=-1, keepdims=True)
    return center * lax.rsqrt(spread + epsilon) * gain + shift


def gelu_tanh(value_in):
    return jax.nn.gelu(value_in, approximate=True)


def position_table(seq_len, width):
    distance = seq_len - 1.0 - np.arange(2 * seq_len - 1, dtype=np.float32)
    freq_exp = np.arange(0, width, 2).astype(np.float32) / np.float32(width)
    inverse = np.float32(1.0) / np.float32(10000.0) ** freq_exp
    angle = (distance[:, None] * inverse[None, :]).astype(np.float32)
    table = np.concatenate([np.sin(angle), np.cos(angle)], axis=1)
    table = np.concatenate([table, np.zeros((1, width), np.float32)], axis=0)
    return table.astype(ml_dtypes.bfloat16)


def dot_left(left_op, right_op):
    return lax.dot_general(
        left_op, right_op, (((0,), (0,)), ((), ())), preferred_element_type=jnp.float32
    )


def on_device(
    dp_size,
    content_in,
    query_in,
    doc_lengths,
    order_ranks,
    segment_ids,
    target_flags,
    query_weight,
    key_weight,
    value_weight,
    out_weight,
    rel_weight,
    content_bias,
    position_bias,
    segment_bias,
    segment_embed,
    first_gain,
    first_shift,
    up_weight,
    up_bias,
    down_weight,
    down_bias,
    second_gain,
    second_shift,
    content_cot,
    query_cot,
):
    docs_dev, half, width = content_in.shape
    seq_len = order_ranks.shape[1]
    mine = lax.axis_index("mp")
    wide_f = lambda value: value.astype(jnp.float32)
    low_f = lambda value: value.astype(jnp.bfloat16)

    def swap(value):
        return lax.ppermute(value, "mp", [(0, 1), (1, 0)])

    def gather_doc(value):
        keep = lax.dynamic_index_in_dim(value, mine, 0, keepdims=False)
        came = swap(lax.dynamic_index_in_dim(value, 1 - mine, 0, keepdims=False))
        head = jnp.where(mine == 0, keep, came)
        tail = jnp.where(mine == 0, came, keep)
        return jnp.concatenate([head, tail], axis=0)

    def return_doc(value):
        pair = value.reshape(2, half, width)
        keep = lax.dynamic_index_in_dim(pair, mine, 0, keepdims=False)
        came = swap(lax.dynamic_index_in_dim(pair, 1 - mine, 0, keepdims=False))
        return jnp.stack([jnp.where(mine == 0, keep, came), jnp.where(mine == 0, came, keep)])

    def both(value, axis):
        return jnp.concatenate([value, swap(value)], axis=axis)

    content = gather_doc(content_in)
    query = gather_doc(query_in)
    query_use = both(query_weight, 1)
    key_use = both(key_weight, 1)
    value_use = both(value_weight, 1)
    rel_use = both(rel_weight, 1)
    vectors = both(
        jnp.concatenate(
            [
                wide_f(content_bias)[None],
                wide_f(position_bias)[None],
                wide_f(segment_bias)[None],
                wide_f(segment_embed),
            ],
            axis=0,
        ),
        1,
    )
    bias, embed = vectors[:3], vectors[3:]
    out_use = both(out_weight, 0)
    up_use = both(up_weight, 1)
    down_use = both(down_weight, 0)
    up_bias_use = both(wide_f(up_bias)[None], 1)
    cot = jnp.concatenate([gather_doc(content_cot), gather_doc(query_cot)], axis=0)

    lengths = lax.dynamic_slice_in_dim(doc_lengths, mine, 1, 0)
    ranks = lax.dynamic_slice_in_dim(order_ranks, mine, 1, 0)
    segments = lax.dynamic_slice_in_dim(segment_ids, mine, 1, 0)
    targets = lax.dynamic_slice_in_dim(target_flags, mine, 1, 0)
    live = targets * (jnp.arange(seq_len) >= 2).astype(jnp.int32)[None]
    lanes = jnp.arange(PAIR)
    seg_hot = low_f((segments[:, :, None] == lanes % 4) & (lanes < 8))
    table = jnp.asarray(position_table(seq_len, width))
    rel_keys = low_f(nn(table, rel_use))
    proj_c = nn(content, query_use)[None]
    proj_q = nn(query, query_use)[None]
    keys = low_f(nn(content, key_use))[None]
    values = low_f(nn(content, value_use))[None]
    vec_c, vec_q, prob = attend_forward(
        lengths, ranks[:, :, None], ranks[:, None, :], live[:, None, :], seg_hot,
        proj_c, proj_q, keys, values, rel_keys, bias, embed,
    )
    vec = jnp.concatenate([vec_c[0], vec_q[0]], axis=0)
    resid = jnp.concatenate([content, query], axis=0)
    gain_first, shift_first = wide_f(first_gain), wide_f(first_shift)
    gain_second, shift_second = wide_f(second_gain), wide_f(second_shift)
    pre1 = nn(vec, out_use) + wide_f(resid)
    first = low_f(layer_norm(pre1, gain_first, shift_first))
    hidden = nn(first, up_use) + up_bias_use
    act = low_f(gelu_tanh(hidden))
    pre2 = wide_f(first) + nn(act, down_use) + wide_f(down_bias)
    norm2, pull2 = jax.vjp(layer_norm, pre2, gain_second, shift_second)
    out_rows = low_f(norm2)
    grad_pre2, g_gain2, g_shift2 = pull2(wide_f(cot))
    g_down_bias = jnp.sum(grad_pre2, axis=0)
    grad_down = low_f(grad_pre2)
    grad_act = nt(grad_down, down_use)
    grad_hidden = low_f(jax.vjp(gelu_tanh, hidden)[1](grad_act)[0])
    g_up_bias = jnp.sum(wide_f(grad_hidden), axis=0)
    back = nt(grad_hidden, up_use)
    grad_pre1, g_gain1, g_shift1 = jax.vjp(layer_norm, pre1, gain_first, shift_first)[1](back + grad_pre2)
    grad_mixed = low_f(grad_pre1)
    grad_vec = low_f(nt(grad_mixed, out_use))

    ff = up_weight.shape[1]
    cols = query_weight.shape[1]

    g_down = low_f(dot_left(act, grad_down))
    g_up = low_f(dot_left(first, grad_hidden))
    g_out = low_f(dot_left(vec, grad_mixed))

    up_rows = ff // cols
    halves = jnp.concatenate([jnp.zeros((2, 5, cols), jnp.float32), g_up_bias.reshape(2, up_rows, cols)], axis=1)
    same = jnp.stack([g_gain1, g_shift1, g_gain2, g_shift2, g_down_bias]).reshape(2 * 5, cols)
    split_rows = 5 + up_rows
    filler = jnp.zeros((2, (-split_rows - 10) % 8, cols), jnp.float32)
    packed = jnp.concatenate([halves, jnp.stack([same, same]), filler], axis=1)
    gproj_c, gproj_q, gkeys, gvalues, pieces, tiny = attend_backward(
        dp_size, piece_layout(cols, ff), seg_hot[0], proj_c[0], proj_q[0], keys[0], values[0], rel_keys,
        bias, embed, vec_c[0], vec_q[0], grad_vec[:seq_len], grad_vec[seq_len:], prob[0],
        jnp.transpose(content), jnp.transpose(query), jnp.asarray(position_table(seq_len, width).T), packed,
        g_down, g_up, g_out,
    )
    content_grad = low_f(
        nt(gproj_c, query_use) + nt(gkeys, key_use) + nt(gvalues, value_use) + grad_pre1[:seq_len]
    )
    query_grad = low_f(nt(gproj_q, query_use) + grad_pre1[seq_len:])

    down_sum, up_sum, out_sum, query_sum, key_sum, value_sum, rel_sum = finish(pieces, ff)
    same_part = tiny[split_rows : split_rows + 10].reshape(5, width)
    split_part = tiny[:5]
    return (
        return_doc(out_rows[:seq_len]),
        return_doc(out_rows[seq_len:]),
        return_doc(content_grad),
        return_doc(query_grad),
        query_sum,
        key_sum,
        value_sum,
        out_sum,
        rel_sum,
        split_part[0],
        split_part[1],
        split_part[2],
        split_part[3:5],
        same_part[0],
        same_part[1],
        up_sum,
        tiny[5:split_rows].reshape(ff),
        down_sum,
        same_part[4],
        same_part[2],
        same_part[3],
    )


def solution(mesh):
    placed = (
        P("dp", "mp", None),
        P("dp", "mp", None),
        P("dp"),
        P("dp", None),
        P("dp", None),
        P("dp", None),
        P(None, "mp"),
        P(None, "mp"),
        P(None, "mp"),
        P("mp", None),
        P(None, "mp"),
        P("mp"),
        P("mp"),
        P("mp"),
        P(None, "mp"),
        P(),
        P(),
        P(None, "mp"),
        P("mp"),
        P("mp", None),
        P(),
        P(),
        P(),
        P("dp", "mp", None),
        P("dp", "mp", None),
    )
    return jax.shard_map(
        functools.partial(on_device, mesh.shape["dp"]),
        mesh=mesh,
        in_specs=placed,
        out_specs=(
            P("dp", "mp", None),
            P("dp", "mp", None),
            P("dp", "mp", None),
            P("dp", "mp", None),
            P(None, "mp"),
            P(None, "mp"),
            P(None, "mp"),
            P("mp", None),
            P(None, "mp"),
            P("mp"),
            P("mp"),
            P("mp"),
            P(None, "mp"),
            P(),
            P(),
            P(None, "mp"),
            P("mp"),
            P("mp", None),
            P(),
            P(),
            P(),
        ),
        check_vma=False,
    )
```

```python
import functools

import jax
import jax.numpy as jnp
import ml_dtypes
import numpy as np
from jax import lax
from jax.experimental import pallas as pl
from jax.experimental.pallas import tpu as pltpu
from jax.sharding import PartitionSpec as P

epsilon = 1e-06
DH = 64
PAIR = 2 * DH
ROWS = 256
NEG = -1e30


def nt(left_op, right_op):
    return lax.dot_general(
        left_op, right_op, (((1,), (1,)), ((), ())), preferred_element_type=jnp.float32
    )


def nn(left_op, right_op):
    return jnp.dot(left_op, right_op, preferred_element_type=jnp.float32)


def lane_ids(rows):
    return lax.broadcasted_iota(jnp.int32, (rows, PAIR), 1)


def attend_forward_body(
    len_ref, rank_col, rank_row, live_row, seg_hot, proj_c, proj_q, key_ref, value_ref, rel_ref,
    bias_ref, embed_ref, vec_c, vec_q, prob_ref, mask_scr, ext_scr,
):
    seq_len = key_ref.shape[0]
    blocks = seq_len // ROWS
    wide = seq_len + ROWS

    @pl.when(pl.program_id(1) == 0)
    def _():
        length = len_ref[pl.program_id(0)]
        for block in range(blocks):
            rows = pl.ds(block * ROWS, ROWS)
            place_j = lax.broadcasted_iota(jnp.int32, (ROWS, seq_len), 1)
            place_i = lax.broadcasted_iota(jnp.int32, (ROWS, seq_len), 0) + block * ROWS
            visible = (place_j < length) & (
                (live_row[...] == 0) | (rank_row[...] < rank_col[rows, :])
            )
            diagonal = place_i == place_j
            mask_scr[0, rows, :] = jnp.where(visible | diagonal, 0.0, NEG)
            mask_scr[1, rows, :] = jnp.where(visible & jnp.logical_not(diagonal), 0.0, NEG)

    ext_scr[:, :PAIR] = key_ref[...]
    ext_scr[:, PAIR:] = seg_hot[...]
    lane = lane_ids(ROWS)
    diff = embed_ref[0:1, :] - embed_ref[1:2, :]
    for stream in range(2):
        proj_ref = (proj_c, proj_q)[stream]
        vec_ref = (vec_c, vec_q)[stream]
        for block in range(blocks):
            rows = pl.ds(block * ROWS, ROWS)
            proj = proj_ref[rows, :]
            query_c = ((proj + bias_ref[0:1, :]) * 0.125).astype(jnp.bfloat16)
            query_p = ((proj + bias_ref[1:2, :]) * 0.125).astype(jnp.bfloat16)
            seg_gap = (proj + bias_ref[2:3, :]) * (diff * 0.125)
            hot = seg_hot[rows, :].astype(jnp.float32)
            window = rel_ref[pl.ds(seq_len - (block + 1) * ROWS, wide), :]
            vec_pair = None
            for head in range(2):
                own = (lane >= DH) if head else (lane < DH)
                zero = jnp.zeros((), jnp.bfloat16)
                gap = jnp.sum(jnp.where(own, seg_gap, 0.0), axis=1, keepdims=True)
                gap_high = gap.astype(jnp.bfloat16).astype(jnp.float32)
                seg_part = (jnp.where(lane < 4, gap_high, gap - gap_high) * hot).astype(jnp.bfloat16)
                left = jnp.concatenate([jnp.where(own, query_c, zero), seg_part], axis=1)
                scores = nt(left, ext_scr[...])
                table = nt(jnp.where(own, query_p, zero), window)
                table = pltpu.roll(table, 1, 1, stride=1, stride_axis=0)
                scores = scores + table[:, ROWS:] + mask_scr[stream, rows, :]
                top = jnp.max(scores, axis=1, keepdims=True)
                terms = jnp.exp(scores - top)
                total = jnp.sum(terms, axis=1, keepdims=True)
                prob = (terms * (1.0 / total)).astype(jnp.bfloat16)
                prob_ref[stream, head, rows, :] = prob
                part = nn(prob, value_ref[...])
                vec_pair = part if head == 0 else jnp.where(own, part, vec_pair)
            vec_ref[rows, :] = vec_pair.astype(jnp.bfloat16)


def attend_forward(lengths, rank_col, rank_row, live_row, seg_hot, proj_c, proj_q, keys, values, rel_keys, bias, embed):
    docs, seq_len, width = proj_c.shape
    pairs = width // PAIR
    per_doc = lambda d, p, *_: (d, 0, 0)
    per_pair = lambda d, p, *_: (d, 0, p)
    shared = lambda d, p, *_: (0, p)
    tile = pl.BlockSpec((None, seq_len, PAIR), per_pair)
    return pl.pallas_call(
        attend_forward_body,
        out_shape=(
            jax.ShapeDtypeStruct((docs, seq_len, width), jnp.bfloat16),
            jax.ShapeDtypeStruct((docs, seq_len, width), jnp.bfloat16),
            jax.ShapeDtypeStruct((docs, pairs, 2, 2, seq_len, seq_len), jnp.bfloat16),
        ),
        grid_spec=pltpu.PrefetchScalarGridSpec(
            num_scalar_prefetch=1,
            grid=(docs, pairs),
            in_specs=[
                pl.BlockSpec((None, seq_len, 1), per_doc),
                pl.BlockSpec((None, 1, seq_len), per_doc),
                pl.BlockSpec((None, 1, seq_len), per_doc),
                pl.BlockSpec((None, seq_len, PAIR), per_doc),
                tile, tile, tile, tile,
                pl.BlockSpec((2 * seq_len, PAIR), shared),
                pl.BlockSpec((3, PAIR), shared),
                pl.BlockSpec((2, PAIR), shared),
            ],
            out_specs=[
                tile, tile,
                pl.BlockSpec((None, None, 2, 2, seq_len, seq_len), lambda d, p, *_: (d, p, 0, 0, 0, 0)),
            ],
            scratch_shapes=[
                pltpu.VMEM((2, seq_len, seq_len), jnp.float32),
                pltpu.VMEM((seq_len, 2 * PAIR), jnp.bfloat16),
            ],
        ),
        name="attend_forward",
    )(lengths, rank_col, rank_row, live_row, seg_hot, proj_c, proj_q, keys, values, rel_keys, bias, embed)


GELU_A = 0.7978845608028654
GELU_B = 0.044715


def norm_parts(value_in):
    center = value_in - jnp.mean(value_in, axis=1, keepdims=True)
    scale = lax.rsqrt(jnp.mean(center * center, axis=1, keepdims=True) + epsilon)
    return center * scale, scale


def norm_pull(normal, scale, grad):
    return scale * (
        grad
        - jnp.mean(grad, axis=1, keepdims=True)
        - normal * jnp.mean(grad * normal, axis=1, keepdims=True)
    )


def feed_forward_body(
    vec_c, vec_q, content, query, cot_c, cot_q, out_ref, up_ref, down_ref, up_bias, norms,
    first_t, normal_ref, scale_ref, act_ref, slope_ref, grad_ref, low_ref, low_t, rows_ref, sums_ref,
    first_scr, total_scr,
):
    step = pl.program_id(0)
    half_rows = vec_c.shape[0]
    chunks = [(s, at) for s in range(2) for at in range(0, half_rows, ROWS)]

    @pl.when(step == 0)
    def _():
        for stream, at in chunks:
            here = pl.ds(at, ROWS)
            there = slice(stream * half_rows + at, stream * half_rows + at + ROWS)
            mixed = nn((vec_c, vec_q)[stream][here, :], out_ref[...])
            mixed = mixed + (content, query)[stream][here, :].astype(jnp.float32)
            normal, scale = norm_parts(mixed)
            first = (normal * norms[0:1, :] + norms[1:2, :]).astype(jnp.bfloat16)
            first_scr[there, :] = first
            first_t[:, there] = jnp.transpose(first)
            normal_ref[there, :] = normal.astype(jnp.bfloat16)
            scale_ref[there, :] = scale
            total_scr[there, :] = first.astype(jnp.float32) + norms[4:5, :]

    for stream, at in chunks:
        there = slice(stream * half_rows + at, stream * half_rows + at + ROWS)
        value = nn(first_scr[there, :], up_ref[...]) + up_bias[...]
        square = value * value
        half = 0.5 + 0.5 * jnp.tanh(value * (GELU_A + (GELU_A * GELU_B) * square))
        wide = value * half
        act = wide.astype(jnp.bfloat16)
        slope = half + (wide * (1.0 - half)) * ((2.0 * GELU_A) + (6.0 * GELU_A * GELU_B) * square)
        act_ref[there, :] = act
        slope_ref[there, :] = slope.astype(jnp.bfloat16)
        total_scr[there, :] += nn(act, down_ref[...])

    @pl.when(step == pl.num_programs(0) - 1)
    def _():
        sums = [jnp.zeros((1, content.shape[1]), jnp.float32) for _ in range(3)]
        for stream, at in chunks:
            here = pl.ds(at, ROWS)
            there = slice(stream * half_rows + at, stream * half_rows + at + ROWS)
            normal, scale = norm_parts(total_scr[there, :])
            rows_ref[there, :] = (normal * norms[2:3, :] + norms[3:4, :]).astype(jnp.bfloat16)
            cot = (cot_c, cot_q)[stream][here, :].astype(jnp.float32)
            grad = norm_pull(normal, scale, cot * norms[2:3, :])
            grad_ref[there, :] = grad
            low = grad.astype(jnp.bfloat16)
            low_ref[there, :] = low
            low_t[:, there] = jnp.transpose(low)
            for at_sum, term in enumerate((cot * normal, cot, grad)):
                sums[at_sum] = sums[at_sum] + jnp.sum(term, axis=0, keepdims=True)
        sums_ref[...] = jnp.concatenate(sums + [jnp.zeros((5, content.shape[1]), jnp.float32)], axis=0)


def feed_forward(vec_c, vec_q, content, query, cot_c, cot_q, out_use, up_use, down_use, up_bias, norms):
    seq_len, width = content.shape
    hidden = up_use.shape[1]
    cols = width // 2
    rows = 2 * seq_len
    low = jnp.bfloat16
    once = pl.Buffered(1)
    whole = lambda f: (0, 0)
    side = lambda f: (0, f)
    keep = lambda shape: pl.BlockSpec(shape, whole, pipeline_mode=once)
    stream = keep((seq_len, width))
    return pl.pallas_call(
        feed_forward_body,
        out_shape=(
            jax.ShapeDtypeStruct((width, rows), low),
            jax.ShapeDtypeStruct((rows, width), low),
            jax.ShapeDtypeStruct((rows, 1), jnp.float32),
            jax.ShapeDtypeStruct((rows, hidden), low),
            jax.ShapeDtypeStruct((rows, hidden), low),
            jax.ShapeDtypeStruct((rows, width), jnp.float32),
            jax.ShapeDtypeStruct((rows, width), low),
            jax.ShapeDtypeStruct((width, rows), low),
            jax.ShapeDtypeStruct((rows, width), low),
            jax.ShapeDtypeStruct((8, width), jnp.float32),
        ),
        grid=(hidden // cols,),
        in_specs=[
            stream, stream, stream, stream, stream, stream,
            keep((width, width)),
            pl.BlockSpec((width, cols), side),
            pl.BlockSpec((cols, width), lambda f: (f, 0)),
            pl.BlockSpec((1, cols), side),
            keep((8, width)),
        ],
        out_specs=[
            pl.BlockSpec((width, rows), whole),
            pl.BlockSpec((rows, width), whole),
            pl.BlockSpec((rows, 1), whole),
            pl.BlockSpec((rows, cols), side),
            pl.BlockSpec((rows, cols), side),
            pl.BlockSpec((rows, width), whole),
            pl.BlockSpec((rows, width), whole),
            pl.BlockSpec((width, rows), whole),
            pl.BlockSpec((rows, width), whole),
            pl.BlockSpec((8, width), whole),
        ],
        scratch_shapes=[
            pltpu.VMEM((rows, width), low),
            pltpu.VMEM((rows, width), jnp.float32),
        ],
        compiler_params=pltpu.CompilerParams(vmem_limit_bytes=60 << 20),
        name="feed_forward",
    )(vec_c, vec_q, content, query, cot_c, cot_q, out_use, up_use, down_use, up_bias, norms)


MESH = pl.DeviceIdType.MESH
FOLDS = 4
LAG = 2
EARLY = 9
COUNT = 13


def shear_left(value_in):
    rows, wide = value_in.shape
    pack = 16
    groups = []
    for group in range(rows // pack):
        piece = value_in[group * pack : (group + 1) * pack]
        groups.append(pltpu.roll(piece, wide - 1 - group * pack, 1))
    moved = jnp.concatenate(groups, axis=0)
    place = lax.broadcasted_iota(jnp.int32, (rows, wide), 0)
    step = 1
    while step < pack:
        moved = jnp.where((place & step) != 0, pltpu.roll(moved, wide - step, 1), moved)
        step = step * 2
    return moved


def backward_body(dp_size, *refs):
    (
        seg_hot, proj_c, proj_q, key_ref, value_ref, rel_ref, bias_ref, embed_ref, prob_ref,
        query_w, key_w, value_w, vec_c, vec_q, content_t, query_t, table_t, out_w,
        act_ref, slope_ref, up_ref, down_ref, low_ref, low_t, first_t, normal_ref, scale_ref,
        norms, sums_in, grad_in, rows_in,
        sum_out, small_out, keep_out, rows_came, grad_came,
        vt_scr, key_acc, value_acc, rel_acc, total, vec_grad, hid_scr,
        work, swapped, landed, extra, small_work, small_far, small_land,
        store_sem, swap_send, swap_recv, fold_send, fold_recv, spread_send, spread_recv,
        more_send, more_recv, tiny_send, tiny_recv, grad_sem, keep_sem, back_send, back_recv,
    ) = refs
    gproj_c = hid_scr.at[: key_ref.shape[0], :]
    gproj_q = hid_scr.at[key_ref.shape[0] :, :PAIR]
    ext_scr = hid_scr.at[key_ref.shape[0] :, PAIR:]
    grid_at = pl.program_id(0)
    feeds = 8
    pairs = 6
    half_pairs = pairs // 2
    last = pl.num_programs(0) - 1
    rows, cols = work.shape[1:]
    seq_len = key_ref.shape[0]
    place = lax.axis_index("dp")
    core = lax.axis_index("mp")
    strides = [1 + core, 2 - core, 4, 8]
    more = [16 << step for step in range(8) if (16 << step) < dp_size]
    bits = [(place // stride) % 2 for stride in strides]
    partners = [place + (1 - 2 * bit) * stride for bit, stride in zip(bits, strides)]
    more_partners = [place + (1 - 2 * ((place // stride) % 2)) * stride for stride in more]
    lengths = [rows >> (fold + 1) for fold in range(FOLDS)]
    starts, begin = [], 0
    for bit, length in zip(bits, lengths):
        begin = begin + bit * length
        starts.append(begin)
    land_at = [rows - 2 * length for length in lengths]
    offsets = [number * LAG for number in range(2 * FOLDS + 1)]
    final_slot = 20

    def kept(fold):
        return pl.ds(pl.multiple_of(starts[fold], 16), lengths[fold])

    def given(fold):
        return pl.ds(pl.multiple_of(starts[fold] + (1 - 2 * bits[fold]) * lengths[fold], 16), lengths[fold])

    def remote(source, target, send, recv, device):
        return pltpu.make_async_remote_copy(
            src_ref=source, dst_ref=target, send_sem=send, recv_sem=recv,
            device_id=device, device_id_type=MESH,
        )

    def swap_copy(piece):
        return remote(
            work.at[piece], swapped.at[piece], swap_send.at[piece], swap_recv.at[piece], {"mp": 1 - core}
        )

    def fold_copy(fold, piece):
        return remote(
            work.at[piece, given(fold)],
            landed.at[piece, pl.ds(land_at[fold], lengths[fold])],
            fold_send.at[fold, piece], fold_recv.at[fold, piece], {"dp": partners[fold]},
        )

    def spread_copy(fold, piece):
        return remote(
            swapped.at[piece, kept(fold)],
            swapped.at[piece, kept(fold)],
            spread_send.at[fold, piece], spread_recv.at[fold, piece], {"dp": partners[fold]},
        )

    def extra_ref(step, piece):
        if step == 0:
            return landed.at[piece, pl.ds(rows - lengths[-1], lengths[-1])]
        return extra.at[step - 1, piece]

    def more_copy(step, piece):
        return remote(
            work.at[piece, kept(FOLDS - 1)],
            extra_ref(step, piece),
            more_send.at[step, piece], more_recv.at[step, piece], {"dp": more_partners[step]},
        )

    def store(piece):
        return pltpu.make_async_copy(swapped.at[piece], sum_out.at[piece], store_sem.at[piece])

    def add_rows(piece, where, other):
        mine = work[piece, where, :].astype(jnp.float32)
        work[piece, where, :] = (mine + other.astype(jnp.float32)).astype(jnp.bfloat16)

    tiny_devices = [{"mp": 1 - core}] + [{"dp": partner} for partner in partners + more_partners]

    def tiny_copy(step):
        return remote(
            small_far if step == 0 else small_work.at[step],
            small_land.at[step], tiny_send.at[step], tiny_recv.at[step], tiny_devices[step],
        )

    far_rows = (1 - core) * ROWS

    def rows_copy(stream):
        return remote(
            rows_in.at[pl.ds(pl.multiple_of(stream * seq_len + far_rows, ROWS), ROWS)], rows_came.at[stream],
            back_send.at[stream], back_recv.at[stream], {"mp": 1 - core},
        )

    def grad_copy(stream):
        return remote(
            vec_grad.at[pl.ds(pl.multiple_of(stream * seq_len + far_rows, ROWS), ROWS)], grad_came.at[stream],
            back_send.at[2 + stream], back_recv.at[2 + stream], {"mp": 1 - core},
        )

    def keep_copy(stream):
        return pltpu.make_async_copy(
            vec_grad.at[pl.ds(pl.multiple_of(stream * seq_len + core * ROWS, ROWS), ROWS)],
            keep_out.at[stream], keep_sem.at[stream],
        )

    grad_load = pltpu.make_async_copy(grad_in, total, grad_sem)

    def stage(number, piece):
        if number == 0:
            fold_copy(0, piece).start()
        elif number <= FOLDS:
            fold = number - 1
            fold_copy(fold, piece).wait_recv()
            add_rows(piece, kept(fold), landed[piece, pl.ds(land_at[fold], lengths[fold]), :])
            if fold + 1 < FOLDS:
                fold_copy(fold + 1, piece).start()
                return
            for step in range(len(more)):
                more_copy(step, piece).start()
                more_copy(step, piece).wait()
                add_rows(piece, kept(fold), extra_ref(step, piece)[...])
            swapped[piece, kept(fold), :] = work[piece, kept(fold), :]
            spread_copy(fold, piece).start()
        else:
            fold = 2 * FOLDS - number
            remote(
                swapped.at[piece, kept(fold)], swapped.at[piece, given(fold)],
                spread_send.at[fold, piece], spread_recv.at[fold, piece], {"dp": partners[fold]},
            ).wait_recv()
            if fold > 0:
                spread_copy(fold - 1, piece).start()
            else:
                store(piece).start()

    def advance(tick):
        for number in reversed(range(2 * FOLDS + 1)):
            slot = tick - offsets[number]
            piece = jnp.where(slot < EARLY, slot, EARLY + (slot - 14) // 2)

            @pl.when(
                (slot >= 0)
                & ((slot < EARLY) | (slot == 15) | (slot == 17) | (slot == 19) | (slot == final_slot))
            )
            def _():
                stage(number, piece)

    def settle(piece):
        swap_copy(piece).wait_recv()
        add_rows(piece, pl.ds(0, rows), swapped[piece])

    @pl.when(grid_at == 0)
    def _():
        barrier = pltpu.get_barrier_semaphore()
        for device in tiny_devices:
            pl.semaphore_signal(barrier, inc=1, device_id=device, device_id_type=MESH)
        pl.semaphore_wait(barrier, len(tiny_devices))
        grad_load.start()
        rows_copy(0).start()
        rows_copy(1).start()
        small_work[0] = jnp.zeros_like(small_work[0])
        small_far[...] = jnp.zeros_like(small_far)
        for at in range(3):
            for side in range(2):
                line = sums_in[at : at + 1, side * cols : (side + 1) * cols]
                spot = slice(13 + 2 * at + side, 14 + 2 * at + side)
                small_work[0, spot, :] = line
                small_far[spot, :] = line
        grad_load.wait()

    @pl.when(grid_at < feeds)
    def _():
        chunk = grid_at // 2
        near = grid_at % 2 == 1
        bias_sum = jnp.zeros((1, cols), jnp.float32)
        for at in range(0, total.shape[0], ROWS):
            here = slice(at, at + ROWS)
            grad_act = nt(low_ref[here, :], down_ref[...])
            hid = (grad_act * slope_ref[here, :].astype(jnp.float32)).astype(jnp.bfloat16)
            hid_scr[here, :] = hid
            bias_sum = bias_sum + jnp.sum(hid.astype(jnp.float32), axis=0, keepdims=True)
            total[here, :] += nt(hid, up_ref[...])

        @pl.when(near)
        def _():
            swap_copy(2 * chunk).wait_send()
            swap_copy(2 * chunk + 1).wait_send()

        for at in range(0, rows, ROWS):
            here = slice(at, at + ROWS)
            work[2 * chunk, here, :] = nn(low_t[here, :], act_ref[...]).astype(jnp.bfloat16)
            work[2 * chunk + 1, here, :] = nn(first_t[here, :], hid_scr[...]).astype(jnp.bfloat16)

        @pl.when(near)
        def _():
            small_work[0, pl.ds(5 + chunk, 1), :] = bias_sum
            settle(2 * chunk)
            settle(2 * chunk + 1)

        @pl.when(jnp.logical_not(near))
        def _():
            small_far[pl.ds(5 + chunk, 1), :] = bias_sum
            swap_copy(2 * chunk).start()
            swap_copy(2 * chunk + 1).start()

    @pl.when(grid_at == feeds)
    def _():
        sums = [jnp.zeros((1, 2 * cols), jnp.float32) for _ in range(2)]
        out_piece = EARLY - 1
        near_sum = jnp.zeros((rows, cols), jnp.float32)
        far_sum = jnp.zeros((rows, cols), jnp.float32)
        for at in range(0, total.shape[0], ROWS):
            here = slice(at, at + ROWS)
            normal = normal_ref[here, :].astype(jnp.float32)
            grad = total[here, :]
            sums[0] = sums[0] + jnp.sum(grad * normal, axis=0, keepdims=True)
            sums[1] = sums[1] + jnp.sum(grad, axis=0, keepdims=True)
            grad = norm_pull(normal, scale_ref[here, :], grad * norms[0:1, :])
            total[here, :] = grad
            low = grad.astype(jnp.bfloat16)
            hid_scr[here, :] = low[:, :cols]
            vec_grad[here, :] = low
        for at in range(0, total.shape[0], ROWS):
            here = slice(at, at + ROWS)
            low = vec_grad[here, :]
            low_turn = jnp.transpose(low)
            vec = (vec_c, vec_q)[at // seq_len][at % seq_len : at % seq_len + ROWS, :]
            far_sum = far_sum + nn(low_turn, vec[:, cols:])
            near_sum = near_sum + nn(low_turn, vec[:, :cols])
            vec_grad[here, :] = nt(low, out_w[...]).astype(jnp.bfloat16)
        work[out_piece] = far_sum.astype(jnp.bfloat16)
        swap_copy(out_piece).start()
        for at in range(2):
            for side in range(2):
                line = sums[at][:, side * cols : (side + 1) * cols]
                spot = slice(9 + 2 * at + side, 10 + 2 * at + side)
                small_work[0, spot, :] = line
                small_far[spot, :] = line
        swap_copy(out_piece).wait()
        work[out_piece] = (near_sum + swapped[out_piece].astype(jnp.float32)).astype(jnp.bfloat16)

    @pl.when(grid_at > feeds)
    def _():
        turn = grid_at - feeds - 1
        pair = (turn + half_pairs) % pairs
        pair_lanes = pl.ds(pl.multiple_of(pair * PAIR, PAIR), PAIR)
        blocks = seq_len // ROWS
        wide = seq_len + ROWS
        ext_scr[:, :PAIR] = (key_ref[...].astype(jnp.float32) * 0.125).astype(jnp.bfloat16)
        ext_scr[:, PAIR:] = (seg_hot[...].astype(jnp.float32) * 0.125).astype(jnp.bfloat16)
        vt_scr[...] = jnp.transpose(value_ref[...])
        key_acc[...] = jnp.zeros_like(key_acc)
        value_acc[...] = jnp.zeros_like(value_acc)
        rel_acc[...] = jnp.zeros_like(rel_acc)
        lane = lane_ids(ROWS)
        first = lane < DH
        sums = [jnp.zeros((1, PAIR), jnp.float32) for _ in range(5)]
        for stream in range(2):
            proj_ref = (proj_c, proj_q)[stream]
            vec_ref = (vec_c, vec_q)[stream]
            gproj_ref = (gproj_c, gproj_q)[stream]
            for block in range(blocks):
                where = pl.ds(block * ROWS, ROWS)
                start = seq_len - (block + 1) * ROWS
                proj = proj_ref[where, :]
                query_ct = jnp.transpose(((proj + bias_ref[0:1, :]) * 0.125).astype(jnp.bfloat16))
                query_pt = jnp.transpose(((proj + bias_ref[1:2, :]) * 0.125).astype(jnp.bfloat16))
                query_s = proj + bias_ref[2:3, :]
                hot = jnp.where(lane < 4, seg_hot[where, :].astype(jnp.float32), 0.0)
                grad = vec_grad[pl.ds(stream * seq_len + block * ROWS, ROWS), pair_lanes]
                grad_t = jnp.transpose(grad)
                inner = grad.astype(jnp.float32) * vec_ref[where, pair_lanes].astype(jnp.float32)
                window = (rel_ref[pl.ds(start, wide), :].astype(jnp.float32) * 0.125).astype(jnp.bfloat16)
                parts = []
                for head in range(2):
                    own = (lane >= DH) if head else first
                    low, high = head * DH, (head + 1) * DH
                    prob = prob_ref[stream, head, where, :]
                    grad_prob = nn(jnp.where(own, grad, jnp.zeros((), jnp.bfloat16)), vt_scr[...])
                    row_inner = jnp.sum(jnp.where(own, inner, 0.0), axis=1, keepdims=True)
                    gscore = (prob.astype(jnp.float32) * (grad_prob - row_inner)).astype(jnp.bfloat16)
                    value_acc[low:high, :] += nn(grad_t[low:high, :], prob)
                    key_acc[low:high, :] += nn(query_ct[low:high, :], gscore)
                    both = nn(gscore, ext_scr[...])
                    table = jnp.concatenate([jnp.zeros((ROWS, ROWS), jnp.bfloat16), gscore], axis=1)
                    table = shear_left(table)
                    gpos = nn(table, window)
                    rel_acc[low:high, start : start + wide] += nn(query_pt[low:high, :], table)
                    tail = both[:, PAIR:]
                    tail = jnp.where(lane < 4, tail, 0.0)
                    g_same = jnp.sum(tail * hot, axis=1, keepdims=True)
                    g_other = jnp.sum(tail, axis=1, keepdims=True) - g_same
                    parts.append((both[:, :PAIR], gpos, g_same, g_other))
                g_content = jnp.where(first, parts[0][0], parts[1][0])
                g_position = jnp.where(first, parts[0][1], parts[1][1])
                g_same = jnp.where(first, parts[0][2], parts[1][2])
                g_other = jnp.where(first, parts[0][3], parts[1][3])
                g_segment = g_same * embed_ref[0:1, :] + g_other * embed_ref[1:2, :]
                gproj_ref[where, :PAIR] = (g_content + g_position + g_segment).astype(jnp.bfloat16)
                terms = (g_content, g_position, g_segment, g_same * query_s, g_other * query_s)
                sums = [old + jnp.sum(term, axis=0, keepdims=True) for old, term in zip(sums, terms)]
            if stream == 0:
                advance(2 * grid_at - 10)
        gproj_c[:, PAIR : 2 * PAIR] = jnp.transpose(key_acc[...]).astype(jnp.bfloat16)
        gproj_c[:, 2 * PAIR :] = jnp.transpose(value_acc[...]).astype(jnp.bfloat16)
        triple = nn(content_t[...], gproj_c[...])
        g_query = triple[:, :PAIR] + nn(query_t[...], gproj_q[...])
        g_rel = nt(table_t[...], rel_acc[...].astype(jnp.bfloat16))
        vectors = jnp.concatenate(sums, axis=0)
        weights = jnp.concatenate([query_w[...], key_w[...], value_w[...]], axis=1)
        total[:seq_len, :] += nt(gproj_c[...], weights)
        total[seq_len:, :] += nt(gproj_q[...], query_w[...])
        late = turn % half_pairs
        piece = EARLY + late
        rel_piece = EARLY + half_pairs
        lanes = pl.ds(pl.multiple_of(late * PAIR, PAIR), PAIR)

        @pl.when(turn >= half_pairs)
        def _():
            swap_copy(piece).wait_send()

            @pl.when(turn == half_pairs)
            def _():
                swap_copy(rel_piece).wait_send()

        work[piece, :, :PAIR] = g_query.astype(jnp.bfloat16)
        work[piece, :, PAIR:] = triple[:, PAIR:].astype(jnp.bfloat16)
        work[rel_piece, :, lanes] = g_rel.astype(jnp.bfloat16)

        @pl.when(turn < half_pairs)
        def _():
            small_far[0:5, lanes] = vectors
            swap_copy(piece).start()

            @pl.when(turn == half_pairs - 1)
            def _():
                swap_copy(rel_piece).start()
                tiny_copy(0).start()

        @pl.when(turn >= half_pairs)
        def _():
            small_work[0, 0:5, lanes] = vectors
            settle(piece)

            @pl.when(turn == pairs - 1)
            def _():
                settle(rel_piece)

    advance(grid_at - 1 + (grid_at // (feeds + 1)) * (grid_at - feeds))

    @pl.when(grid_at == last)
    def _():
        for at in range(0, total.shape[0], ROWS):
            vec_grad[at : at + ROWS, :] = total[at : at + ROWS, :].astype(jnp.bfloat16)
        begin_tick = final_slot

        def finish_tick(tick, carry):
            for step in range(len(tiny_devices)):
                @pl.when(tick == begin_tick + 1 + step)
                def _():
                    tiny_copy(step).wait_recv()
                    small_work[step + 1] = small_work[step] + small_land[step]
                    if step + 1 < len(tiny_devices):
                        tiny_copy(step + 1).start()

            advance(tick)

            @pl.when(tick == begin_tick)
            def _():
                grad_copy(0).start()
                grad_copy(1).start()
                keep_copy(0).start()
                keep_copy(1).start()

            return carry

        lax.fori_loop(begin_tick, final_slot + 1 + offsets[-1], finish_tick, 0)
        small_out[...] = small_work[len(tiny_devices)]
        for step in range(len(tiny_devices)):
            tiny_copy(step).wait_send()
        for stream in range(2):
            rows_copy(stream).wait()
            grad_copy(stream).wait()
            keep_copy(stream).wait()

        def drain(piece, carry):
            for fold in range(FOLDS):
                fold_copy(fold, piece).wait_send()
                spread_copy(fold, piece).wait_send()
            store(piece).wait()
            return carry

        lax.fori_loop(0, COUNT, drain, 0)


def backward(
    dp_size, seg_hot, proj_c, proj_q, keys, values, rel_keys, bias, embed, prob, query_w, key_w, value_w,
    vec_c, vec_q, content_t, query_t, table_t, out_w, act, slope, up_w, down_w, low_rows, low_t, first_t,
    normal, scale, norms, sums, grad, rows_in,
):
    seq_len, width = proj_c.shape
    pairs = width // PAIR
    cols = width // 2
    feeds = up_w.shape[1] // cols
    rows = 2 * seq_len
    small_rows = 24
    more = max(1, dp_size.bit_length() - 1 - FOLDS)
    tiny = dp_size.bit_length()
    low = jnp.bfloat16
    dma = pltpu.SemaphoreType.DMA
    once = pl.Buffered(1)
    anywhere = pl.BlockSpec(memory_space=pl.ANY)
    whole = lambda g: (0, 0)
    turn = lambda g: (jnp.maximum(g - feeds - 1, 0) + pairs // 2) % pairs
    per_pair = lambda g: (0, turn(g))
    tile = pl.BlockSpec((seq_len, PAIR), per_pair)
    weight = pl.BlockSpec((width, PAIR), per_pair)

    def chunk(g):
        at = jnp.minimum(g, feeds - 1)
        return (1 - at % 2) * (feeds // 2) + at // 2

    side = lambda g: (0, chunk(g))
    keep = lambda shape: pl.BlockSpec(shape, whole, pipeline_mode=once)
    return pl.pallas_call(
        functools.partial(backward_body, dp_size),
        out_shape=(
            jax.ShapeDtypeStruct((COUNT, width, cols), low),
            jax.ShapeDtypeStruct((small_rows, cols), jnp.float32),
            jax.ShapeDtypeStruct((2, ROWS, width), low),
            jax.ShapeDtypeStruct((2, ROWS, width), low),
            jax.ShapeDtypeStruct((2, ROWS, width), low),
        ),
        grid_spec=pltpu.PrefetchScalarGridSpec(
            num_scalar_prefetch=0,
            grid=(feeds + 1 + pairs,),
            in_specs=[
                keep((seq_len, PAIR)),
                tile, tile, tile, tile,
                pl.BlockSpec((2 * seq_len, PAIR), per_pair),
                pl.BlockSpec((3, PAIR), per_pair),
                pl.BlockSpec((2, PAIR), per_pair),
                pl.BlockSpec((None, 2, 2, seq_len, seq_len), lambda g: (turn(g), 0, 0, 0, 0)),
                weight, weight, weight,
                keep((seq_len, width)), keep((seq_len, width)),
                keep((width, seq_len)), keep((width, seq_len)), keep((width, 2 * seq_len)),
                keep((width, width)),
                pl.BlockSpec((rows, cols), side), pl.BlockSpec((rows, cols), side),
                pl.BlockSpec((width, cols), side), pl.BlockSpec((cols, width), lambda g: (chunk(g), 0)),
                keep((rows, width)), keep((width, rows)), keep((width, rows)), keep((rows, width)),
                keep((rows, 1)), keep((8, width)), keep((8, width)),
                anywhere, anywhere,
            ],
            out_specs=[
                anywhere,
                pl.BlockSpec((small_rows, cols), whole),
                anywhere, anywhere, anywhere,
            ],
            scratch_shapes=[
                pltpu.VMEM((PAIR, seq_len), low),
                pltpu.VMEM((PAIR, seq_len), jnp.float32),
                pltpu.VMEM((PAIR, seq_len), jnp.float32),
                pltpu.VMEM((PAIR, 2 * seq_len), jnp.float32),
                pltpu.VMEM((rows, width), jnp.float32),
                pltpu.VMEM((rows, width), low),
                pltpu.VMEM((rows, cols), low),
                pltpu.VMEM((COUNT, width, cols), low),
                pltpu.VMEM((COUNT, width, cols), low),
                pltpu.VMEM((COUNT, width, cols), low),
                pltpu.VMEM((max(1, more - 1), COUNT if dp_size > 32 else 1, width >> FOLDS, cols), low),
                pltpu.VMEM((tiny + 1, small_rows, cols), jnp.float32),
                pltpu.VMEM((small_rows, cols), jnp.float32),
                pltpu.VMEM((tiny, small_rows, cols), jnp.float32),
                dma((COUNT,)), dma((COUNT,)), dma((COUNT,)),
                dma((FOLDS, COUNT)), dma((FOLDS, COUNT)), dma((FOLDS, COUNT)), dma((FOLDS, COUNT)),
                dma((more, COUNT)), dma((more, COUNT)), dma((tiny,)), dma((tiny,)),
                dma, dma((2,)), dma((4,)), dma((4,)),
            ],
        ),
        compiler_params=pltpu.CompilerParams(
            collective_id=0, has_side_effects=True, vmem_limit_bytes=67043328
        ),
        name="backward",
    )(
        seg_hot, proj_c, proj_q, keys, values, rel_keys, bias, embed, prob, query_w, key_w, value_w,
        vec_c, vec_q, content_t, query_t, table_t, out_w, act, slope, up_w, down_w, low_rows, low_t, first_t,
        normal, scale, norms, sums, grad, rows_in,
    )


def finish_body(
    piece_ref, rows_ref, rows_came, keep_ref, grad_came,
    content_out, query_out, content_grad, query_grad, down_ref, up_ref, out_ref, query_ref, key_ref, value_ref, rel_ref,
):
    at = pl.program_id(0)
    core = lax.axis_index("mp")
    cols = piece_ref.shape[1]
    feeds = 8

    @pl.when((at < feeds) & (at % 2 == 0))
    def _():
        down_ref[...] = jnp.transpose(piece_ref[...].astype(jnp.float32))

    @pl.when((at < feeds) & (at % 2 == 1))
    def _():
        up_ref[...] = piece_ref[...].astype(jnp.float32)

    @pl.when(at == feeds)
    def _():
        out_ref[...] = jnp.transpose(piece_ref[...].astype(jnp.float32))

    for turn in range(3):
        lanes = slice(turn * PAIR, (turn + 1) * PAIR)

        @pl.when(at == EARLY + turn)
        def _():
            query_ref[:, lanes] = piece_ref[:, :PAIR].astype(jnp.float32)
            key_ref[:, lanes] = piece_ref[:, PAIR : 2 * PAIR].astype(jnp.float32)
            value_ref[:, lanes] = piece_ref[:, 2 * PAIR :].astype(jnp.float32)

    @pl.when(at == EARLY + 3)
    def _():
        rel_ref[...] = piece_ref[...].astype(jnp.float32)

    @pl.when(at == 0)
    def _():
        content_out[core] = rows_ref[core]
        content_out[1 - core] = rows_came[0]
        query_out[core] = rows_ref[2 + core]
        query_out[1 - core] = rows_came[1]
        content_grad[core] = keep_ref[0]
        content_grad[1 - core] = grad_came[0]
        query_grad[core] = keep_ref[1]
        query_grad[1 - core] = grad_came[1]


def finish(pieces, rows_out, rows_came, keep_rows, grad_came, half_ff):
    count, rows, cols = pieces.shape
    feeds = 2 * (half_ff // cols)
    square = jax.ShapeDtypeStruct((rows, cols), jnp.float32)
    pair = jax.ShapeDtypeStruct(rows_came.shape, jnp.bfloat16)
    whole = lambda p: (0, 0)
    block = pl.BlockSpec((rows, cols), whole)
    lead = lambda p: (0, 0, 0)
    once = pl.Buffered(1)
    token = pl.BlockSpec(rows_came.shape, lead)
    token_in = pl.BlockSpec(rows_came.shape, lead, pipeline_mode=once)
    at_chunk = lambda p: jnp.minimum(p // 2, feeds // 2 - 1)
    return pl.pallas_call(
        finish_body,
        out_shape=(
            pair, pair, pair, pair,
            jax.ShapeDtypeStruct((half_ff, rows), jnp.float32),
            jax.ShapeDtypeStruct((rows, half_ff), jnp.float32),
            jax.ShapeDtypeStruct((cols, rows), jnp.float32),
            square, square, square, square,
        ),
        grid=(count,),
        in_specs=[
            pl.BlockSpec((None, rows, cols), lambda p: (p, 0, 0)),
            pl.BlockSpec(rows_out.shape, lead, pipeline_mode=once),
            token_in, token_in, token_in,
        ],
        out_specs=[
            token, token, token, token,
            pl.BlockSpec((cols, rows), lambda p: (at_chunk(p), 0)),
            pl.BlockSpec((rows, cols), lambda p: (0, at_chunk(p))),
            pl.BlockSpec((cols, rows), whole),
            block, block, block, block,
        ],
        compiler_params=pltpu.CompilerParams(vmem_limit_bytes=48 << 20),
        name="finish",
    )(pieces, rows_out, rows_came, keep_rows, grad_came)


def position_table(seq_len, width):
    distance = seq_len - 1.0 - np.arange(2 * seq_len - 1, dtype=np.float32)
    freq_exp = np.arange(0, width, 2).astype(np.float32) / np.float32(width)
    inverse = np.float32(1.0) / np.float32(10000.0) ** freq_exp
    angle = (distance[:, None] * inverse[None, :]).astype(np.float32)
    table = np.concatenate([np.sin(angle), np.cos(angle)], axis=1)
    table = np.concatenate([table, np.zeros((1, width), np.float32)], axis=0)
    return table.astype(ml_dtypes.bfloat16)


def on_device(
    dp_size,
    content_in,
    query_in,
    doc_lengths,
    order_ranks,
    segment_ids,
    target_flags,
    query_weight,
    key_weight,
    value_weight,
    out_weight,
    rel_weight,
    content_bias,
    position_bias,
    segment_bias,
    segment_embed,
    first_gain,
    first_shift,
    up_weight,
    up_bias,
    down_weight,
    down_bias,
    second_gain,
    second_shift,
    content_cot,
    query_cot,
):
    docs_dev, half, width = content_in.shape
    seq_len = order_ranks.shape[1]
    mine = lax.axis_index("mp")
    wide_f = lambda value: value.astype(jnp.float32)
    low_f = lambda value: value.astype(jnp.bfloat16)

    def swap(value):
        return lax.ppermute(value, "mp", [(0, 1), (1, 0)])

    def gather_doc(value):
        keep = lax.dynamic_index_in_dim(value, mine, 0, keepdims=False)
        came = swap(lax.dynamic_index_in_dim(value, 1 - mine, 0, keepdims=False))
        head = jnp.where(mine == 0, keep, came)
        tail = jnp.where(mine == 0, came, keep)
        return jnp.concatenate([head, tail], axis=0)

    def both(value, axis):
        return jnp.concatenate([value, swap(value)], axis=axis)

    content = gather_doc(content_in)
    query = gather_doc(query_in)
    query_use = both(query_weight, 1)
    key_use = both(key_weight, 1)
    value_use = both(value_weight, 1)
    rel_use = both(rel_weight, 1)
    vectors = both(
        jnp.concatenate(
            [
                wide_f(content_bias)[None],
                wide_f(position_bias)[None],
                wide_f(segment_bias)[None],
                wide_f(segment_embed),
            ],
            axis=0,
        ),
        1,
    )
    bias, embed = vectors[:3], vectors[3:]
    out_use = both(out_weight, 0)
    up_use = both(up_weight, 1)
    down_use = both(down_weight, 0)
    up_bias_use = both(wide_f(up_bias)[None], 1)
    cot_c = gather_doc(content_cot)
    cot_q = gather_doc(query_cot)

    lengths = lax.dynamic_slice_in_dim(doc_lengths, mine, 1, 0)
    ranks = lax.dynamic_slice_in_dim(order_ranks, mine, 1, 0)
    segments = lax.dynamic_slice_in_dim(segment_ids, mine, 1, 0)
    targets = lax.dynamic_slice_in_dim(target_flags, mine, 1, 0)
    live = targets * (jnp.arange(seq_len) >= 2).astype(jnp.int32)[None]
    lanes = jnp.arange(PAIR)
    seg_hot = low_f((segments[:, :, None] == lanes % 4) & (lanes < 8))
    table = jnp.asarray(position_table(seq_len, width))
    rel_keys = low_f(nn(table, rel_use))
    proj_c = nn(content, query_use)[None]
    proj_q = nn(query, query_use)[None]
    keys = low_f(nn(content, key_use))[None]
    values = low_f(nn(content, value_use))[None]
    vec_c, vec_q, prob = attend_forward(
        lengths, ranks[:, :, None], ranks[:, None, :], live[:, None, :], seg_hot,
        proj_c, proj_q, keys, values, rel_keys, bias, embed,
    )
    norms = jnp.stack(
        [first_gain, first_shift, second_gain, second_shift, down_bias, down_bias, down_bias, down_bias]
    ).astype(jnp.float32)
    first_t, normal, scale, act, slope, grad, low_rows, low_t, rows_out, sums = feed_forward(
        vec_c[0], vec_q[0], content, query, cot_c, cot_q, out_use, up_use, down_use, up_bias_use, norms
    )
    pieces, tiny, keep_rows, rows_came, grad_came = backward(
        dp_size, seg_hot[0], proj_c[0], proj_q[0], keys[0], values[0], rel_keys, bias, embed, prob[0],
        query_use, key_use, value_use, vec_c[0], vec_q[0], jnp.transpose(content), jnp.transpose(query),
        jnp.asarray(position_table(seq_len, width).T), out_use, act, slope, up_use, down_use,
        low_rows, low_t, first_t, normal, scale, norms, sums, grad, rows_out,
    )
    ff = up_weight.shape[1]
    cols = query_weight.shape[1]
    (
        content_out, query_out, content_grad, query_grad,
        down_sum, up_sum, out_sum, query_sum, key_sum, value_sum, rel_sum,
    ) = finish(pieces, rows_out.reshape(4, half, width), rows_came, keep_rows, grad_came, ff)
    split_rows = 5 + ff // cols
    same_part = tiny[split_rows : split_rows + 10].reshape(5, width)
    split_part = tiny[:5]
    return (
        content_out,
        query_out,
        content_grad,
        query_grad,
        query_sum,
        key_sum,
        value_sum,
        out_sum,
        rel_sum,
        split_part[0],
        split_part[1],
        split_part[2],
        split_part[3:5],
        same_part[0],
        same_part[1],
        up_sum,
        tiny[5:split_rows].reshape(ff),
        down_sum,
        same_part[4],
        same_part[2],
        same_part[3],
    )


def solution(mesh):
    placed = (
        P("dp", "mp", None),
        P("dp", "mp", None),
        P("dp"),
        P("dp", None),
        P("dp", None),
        P("dp", None),
        P(None, "mp"),
        P(None, "mp"),
        P(None, "mp"),
        P("mp", None),
        P(None, "mp"),
        P("mp"),
        P("mp"),
        P("mp"),
        P(None, "mp"),
        P(),
        P(),
        P(None, "mp"),
        P("mp"),
        P("mp", None),
        P(),
        P(),
        P(),
        P("dp", "mp", None),
        P("dp", "mp", None),
    )
    return jax.shard_map(
        functools.partial(on_device, mesh.shape["dp"]),
        mesh=mesh,
        in_specs=placed,
        out_specs=(
            P("dp", "mp", None),
            P("dp", "mp", None),
            P("dp", "mp", None),
            P("dp", "mp", None),
            P(None, "mp"),
            P(None, "mp"),
            P(None, "mp"),
            P("mp", None),
            P(None, "mp"),
            P("mp"),
            P("mp"),
            P("mp"),
            P(None, "mp"),
            P(),
            P(),
            P(None, "mp"),
            P("mp"),
            P("mp", None),
            P(),
            P(),
            P(),
        ),
        check_vma=False,
    )
```

```python
import functools

import jax
import jax.numpy as jnp
import ml_dtypes
import numpy as np
from jax import lax
from jax.experimental import pallas as pl
from jax.experimental.pallas import tpu as pltpu
from jax.sharding import PartitionSpec as P

epsilon = 1e-06
DH = 64
PAIR = 2 * DH
ROWS = 256
NEG = -1e30
MESH = pl.DeviceIdType.MESH


def nt(left_op, right_op):
    return lax.dot_general(
        left_op, right_op, (((1,), (1,)), ((), ())), preferred_element_type=jnp.float32
    )


def nn(left_op, right_op):
    return jnp.dot(left_op, right_op, preferred_element_type=jnp.float32)


def lane_ids(rows):
    return lax.broadcasted_iota(jnp.int32, (rows, PAIR), 1)


def forward_body(
    content_in, query_in, content_cot, query_cot, query_w, key_w, value_w, rel_w, out_w, up_w, down_w,
    meta_ref, vector_ref, table_ref,
    vec_c, vec_q, prob_ref, proj_c, proj_q, key_ref, value_ref, rel_ref, hot_ref, content_t, query_t, vectors_out,
    content_out, query_out, cots_out, square_out, out_all, up_all, down_all,
    tokens, squares, vectors, bounce_up, bounce_down, bounce_out, bounce_cot, mask_scr, ext_scr, rank_scr,
    token_sem, token_send, token_recv, square_sem, square_send, square_recv,
    bulk_load, bulk_store, bulk_send, bulk_recv, vector_send, vector_recv,
):
    step = pl.program_id(0)
    core = lax.axis_index("mp")
    seq_len = proj_c.shape[0]
    half = seq_len // 2
    cols = query_w.shape[1]
    feed = up_w.shape[1]
    blocks = seq_len // ROWS
    wide = seq_len + ROWS
    other = {"mp": 1 - core}
    mine = pl.ds(pl.multiple_of(core * half, half), half)

    def remote(source, target, send, recv):
        return pltpu.make_async_remote_copy(
            src_ref=source, dst_ref=target, send_sem=send, recv_sem=recv,
            device_id=other, device_id_type=MESH,
        )

    token_in = (content_in, query_in)
    square_in = (query_w, key_w, value_w, rel_w)
    token_load = [
        pltpu.make_async_copy(token_in[at].at[core], tokens.at[at, mine], token_sem.at[at]) for at in range(2)
    ]
    token_swap = [
        remote(token_in[at].at[1 - core], tokens.at[at, mine], token_send.at[at], token_recv.at[at])
        for at in range(2)
    ]
    square_load = [
        pltpu.make_async_copy(square_in[at], squares.at[at, :, :cols], square_sem.at[at]) for at in range(4)
    ]
    square_swap = [
        remote(square_in[at], squares.at[at, :, cols:], square_send.at[at], square_recv.at[at])
        for at in range(4)
    ]
    vector_swap = remote(vector_ref, vectors, vector_send, vector_recv)
    cot_in = (content_cot, query_cot)
    bulk_loads = [
        pltpu.make_async_copy(out_w, bounce_out, bulk_load.at[0]),
        pltpu.make_async_copy(up_w, bounce_up, bulk_load.at[1]),
        pltpu.make_async_copy(down_w, bounce_down, bulk_load.at[2]),
    ] + [
        pltpu.make_async_copy(cot_in[at].at[core], bounce_cot.at[at], bulk_load.at[3 + at]) for at in range(2)
    ]
    bulk_stores = [
        pltpu.make_async_copy(bounce_out, out_all.at[:cols], bulk_store.at[0]),
        pltpu.make_async_copy(bounce_up, up_all.at[:, :feed], bulk_store.at[1]),
        pltpu.make_async_copy(bounce_down, down_all.at[:feed], bulk_store.at[2]),
    ] + [
        pltpu.make_async_copy(bounce_cot.at[at], cots_out.at[at, mine], bulk_store.at[3 + at]) for at in range(2)
    ]
    bulk_swaps = [
        remote(out_w, out_all.at[cols:], bulk_send.at[0], bulk_recv.at[0]),
        remote(up_w, up_all.at[:, feed:], bulk_send.at[1], bulk_recv.at[1]),
        remote(down_w, down_all.at[feed:], bulk_send.at[2], bulk_recv.at[2]),
    ] + [
        remote(cot_in[at].at[1 - core], cots_out.at[at, mine], bulk_send.at[3 + at], bulk_recv.at[3 + at])
        for at in range(2)
    ]
    token_store = [
        pltpu.make_async_copy(tokens.at[at], (content_out, query_out)[at], bulk_store.at[5 + at]) for at in range(2)
    ]
    square_store = [
        pltpu.make_async_copy(squares.at[at], square_out.at[at], bulk_store.at[7 + at]) for at in range(3)
    ]

    @pl.when(step == 0)
    def _():
        for copy in token_load + square_load:
            copy.start()
        barrier = pltpu.get_barrier_semaphore()
        pl.semaphore_signal(barrier, inc=1, device_id=other, device_id_type=MESH)
        pl.semaphore_wait(barrier, 1)
        for copy in token_swap + [vector_swap] + square_swap + bulk_swaps + bulk_loads:
            copy.start()
        vectors_out[:, :cols] = vector_ref[...]
        place_j = lax.broadcasted_iota(jnp.int32, (1, seq_len), 1)
        ranks = meta_ref[pl.ds(core, 1), :]
        segments = meta_ref[pl.ds(2 + core, 1), :]
        targets = meta_ref[pl.ds(4 + core, 1), :]
        length = meta_ref[pl.ds(6 + core, 1), :]
        live = jnp.where(place_j >= 2, targets, 0.0)
        rank_scr[...] = jnp.transpose(jnp.broadcast_to(ranks, (PAIR, seq_len)))
        lane = lane_ids(seq_len)
        seg_turn = jnp.transpose(jnp.broadcast_to(segments, (PAIR, seq_len)))
        hot = (seg_turn == (lane % 4).astype(jnp.float32)) & (lane < 8)
        hot_ref[...] = jnp.where(hot, 1.0, 0.0).astype(jnp.bfloat16)
        base = jnp.where(place_j.astype(jnp.float32) < length, 0.0, NEG)
        for block in range(blocks):
            rows = slice(block * ROWS, (block + 1) * ROWS)
            rank_i = jnp.concatenate([rank_scr[rows, :]] * (seq_len // PAIR), axis=1)
            seen = jnp.where((live == 0.0) | (ranks < rank_i), base, NEG)
            column = lax.broadcasted_iota(jnp.int32, (ROWS, seq_len), 1)
            line = lax.broadcasted_iota(jnp.int32, (ROWS, seq_len), 0) + block * ROWS
            diagonal = column == line
            mask_scr[0, rows, :] = jnp.where(diagonal, 0.0, seen)
            mask_scr[1, rows, :] = jnp.where(diagonal, NEG, seen)
        for copy in token_load + square_load:
            copy.wait()
        for copy in token_swap:
            copy.wait_recv()
        for copy in token_store:
            copy.start()

    @pl.when(step == 1)
    def _():
        for copy in bulk_loads:
            copy.wait()
        for copy in bulk_stores:
            copy.start()
        content_t[...] = jnp.transpose(tokens[0])
        query_t[...] = jnp.transpose(tokens[1])

    @pl.when(step == pl.num_programs(0) // 2)
    def _():
        for copy in square_swap + [vector_swap]:
            copy.wait_recv()
        for copy in square_store:
            copy.start()
        vectors_out[:, cols:] = vectors[...]

    pair_lanes = pl.ds(pl.multiple_of(step * PAIR, PAIR), PAIR)
    lines = vectors_out[:, pair_lanes]
    triple_w = jnp.concatenate([squares[at, :, pair_lanes] for at in range(3)], axis=1)
    for block in range(blocks):
        rows = slice(block * ROWS, (block + 1) * ROWS)
        triple = nn(tokens[0, rows, :], triple_w)
        proj_c[rows, :] = triple[:, :PAIR]
        key_ref[rows, :] = triple[:, PAIR : 2 * PAIR].astype(jnp.bfloat16)
        value_ref[rows, :] = triple[:, 2 * PAIR :].astype(jnp.bfloat16)
        proj_q[rows, :] = nn(tokens[1, rows, :], squares[0, :, pair_lanes])
    for block in range(2 * blocks):
        rows = slice(block * ROWS, (block + 1) * ROWS)
        rel_ref[rows, :] = nn(table_ref[rows, :], squares[3, :, pair_lanes]).astype(jnp.bfloat16)
    ext_scr[:, :PAIR] = key_ref[...]
    ext_scr[:, PAIR:] = hot_ref[...]
    lane = lane_ids(ROWS)
    diff = lines[3:4, :] - lines[4:5, :]
    for stream in range(2):
        proj_ref = (proj_c, proj_q)[stream]
        vec_ref = (vec_c, vec_q)[stream]
        for block in range(blocks):
            rows = pl.ds(block * ROWS, ROWS)
            proj = proj_ref[rows, :]
            query_c = ((proj + lines[0:1, :]) * 0.125).astype(jnp.bfloat16)
            query_p = ((proj + lines[1:2, :]) * 0.125).astype(jnp.bfloat16)
            seg_gap = (proj + lines[2:3, :]) * (diff * 0.125)
            hot = hot_ref[rows, :].astype(jnp.float32)
            window = rel_ref[pl.ds(seq_len - (block + 1) * ROWS, wide), :]
            vec_pair = None
            for head in range(2):
                own = (lane >= DH) if head else (lane < DH)
                zero = jnp.zeros((), jnp.bfloat16)
                gap = jnp.sum(jnp.where(own, seg_gap, 0.0), axis=1, keepdims=True)
                gap_high = gap.astype(jnp.bfloat16).astype(jnp.float32)
                seg_part = (jnp.where(lane < 4, gap_high, gap - gap_high) * hot).astype(jnp.bfloat16)
                left = jnp.concatenate([jnp.where(own, query_c, zero), seg_part], axis=1)
                scores = nt(left, ext_scr[...])
                table = nt(jnp.where(own, query_p, zero), window)
                table = pltpu.roll(table, 1, 1, stride=1, stride_axis=0)
                scores = scores + table[:, ROWS:] + mask_scr[stream, rows, :]
                top = jnp.max(scores, axis=1, keepdims=True)
                terms = jnp.exp(scores - top)
                total = jnp.sum(terms, axis=1, keepdims=True)
                prob = (terms * (1.0 / total)).astype(jnp.bfloat16)
                prob_ref[stream, head, rows, :] = prob
                part = nn(prob, value_ref[...])
                vec_pair = part if head == 0 else jnp.where(own, part, vec_pair)
            vec_ref[rows, :] = vec_pair.astype(jnp.bfloat16)

    @pl.when(step == pl.num_programs(0) - 1)
    def _():
        for copy in token_swap + square_swap + [vector_swap]:
            copy.wait_send()
        for copy in bulk_swaps:
            copy.wait()
        for copy in bulk_stores + token_store + square_store:
            copy.wait()


def forward(content_in, query_in, content_cot, query_cot, query_w, key_w, value_w, rel_w, out_w, up_w, down_w, meta, vectors, table):
    docs, half, width = content_in.shape
    seq_len = 2 * half
    pairs = width // PAIR
    cols = query_w.shape[1]
    feed = up_w.shape[1]
    lines = vectors.shape[0]
    low = jnp.bfloat16
    dma = pltpu.SemaphoreType.DMA
    whole = lambda p: (0, 0)
    once = pl.Buffered(1)
    anywhere = pl.BlockSpec(memory_space=pl.ANY)
    tile = pl.BlockSpec((seq_len, PAIR), lambda p: (0, p))
    low_tokens = jax.ShapeDtypeStruct((seq_len, width), low)
    turned = jax.ShapeDtypeStruct((width, seq_len), low)
    return pl.pallas_call(
        forward_body,
        out_shape=(
            low_tokens, low_tokens,
            jax.ShapeDtypeStruct((pairs, 2, 2, seq_len, seq_len), low),
            jax.ShapeDtypeStruct((seq_len, width), jnp.float32),
            jax.ShapeDtypeStruct((seq_len, width), jnp.float32),
            low_tokens, low_tokens,
            jax.ShapeDtypeStruct((2 * seq_len, width), low),
            jax.ShapeDtypeStruct((seq_len, PAIR), low),
            turned, turned,
            jax.ShapeDtypeStruct((lines, width), jnp.float32),
            low_tokens, low_tokens,
            jax.ShapeDtypeStruct((2, seq_len, width), low),
            jax.ShapeDtypeStruct((3, width, width), low),
            jax.ShapeDtypeStruct((width, width), low),
            jax.ShapeDtypeStruct((width, 2 * feed), low),
            jax.ShapeDtypeStruct((2 * feed, width), low),
        ),
        grid_spec=pltpu.PrefetchScalarGridSpec(
            num_scalar_prefetch=0,
            grid=(pairs,),
            in_specs=[anywhere] * 11
            + [
                pl.BlockSpec(meta.shape, whole, pipeline_mode=once),
                pl.BlockSpec(vectors.shape, whole, pipeline_mode=once),
                pl.BlockSpec((2 * seq_len, width), whole, pipeline_mode=once),
            ],
            out_specs=[
                tile, tile,
                pl.BlockSpec((None, 2, 2, seq_len, seq_len), lambda p: (p, 0, 0, 0, 0)),
                tile, tile, tile, tile,
                pl.BlockSpec((2 * seq_len, PAIR), lambda p: (0, p)),
                pl.BlockSpec((seq_len, PAIR), whole),
                pl.BlockSpec((width, seq_len), whole),
                pl.BlockSpec((width, seq_len), whole),
                pl.BlockSpec((lines, width), whole),
            ]
            + [anywhere] * 7,
            scratch_shapes=[
                pltpu.VMEM((2, seq_len, width), low),
                pltpu.VMEM((4, width, width), low),
                pltpu.VMEM(vectors.shape, jnp.float32),
                pltpu.VMEM((width, feed), low),
                pltpu.VMEM((feed, width), low),
                pltpu.VMEM((cols, width), low),
                pltpu.VMEM((2, half, width), low),
                pltpu.VMEM((2, seq_len, seq_len), jnp.float32),
                pltpu.VMEM((seq_len, 2 * PAIR), low),
                pltpu.VMEM((seq_len, PAIR), jnp.float32),
                dma((2,)), dma((2,)), dma((2,)), dma((4,)), dma((4,)), dma((4,)),
                dma((5,)), dma((10,)), dma((5,)), dma((5,)), dma, dma,
            ],
        ),
        compiler_params=pltpu.CompilerParams(
            collective_id=1, has_side_effects=True, vmem_limit_bytes=60 << 20
        ),
        name="attend_forward",
    )(content_in, query_in, content_cot, query_cot, query_w, key_w, value_w, rel_w, out_w, up_w, down_w, meta, vectors, table)


GELU_A = 0.7978845608028654
GELU_B = 0.044715


def norm_parts(value_in):
    center = value_in - jnp.mean(value_in, axis=1, keepdims=True)
    scale = lax.rsqrt(jnp.mean(center * center, axis=1, keepdims=True) + epsilon)
    return center * scale, scale


def norm_pull(normal, scale, grad):
    return scale * (
        grad
        - jnp.mean(grad, axis=1, keepdims=True)
        - normal * jnp.mean(grad * normal, axis=1, keepdims=True)
    )


def feed_forward_body(
    vec_c, vec_q, content, query, cots, out_ref, up_ref, down_ref, up_bias, norms,
    first_t, normal_ref, scale_ref, act_ref, slope_ref, grad_ref, low_ref, low_t, rows_ref, sums_ref,
    first_scr, total_scr,
):
    step = pl.program_id(0)
    half_rows = vec_c.shape[0]
    chunks = [(s, at) for s in range(2) for at in range(0, half_rows, ROWS)]

    @pl.when(step == 0)
    def _():
        for stream, at in chunks:
            here = pl.ds(at, ROWS)
            there = slice(stream * half_rows + at, stream * half_rows + at + ROWS)
            mixed = nn((vec_c, vec_q)[stream][here, :], out_ref[...])
            mixed = mixed + (content, query)[stream][here, :].astype(jnp.float32)
            normal, scale = norm_parts(mixed)
            first = (normal * norms[0:1, :] + norms[1:2, :]).astype(jnp.bfloat16)
            first_scr[there, :] = first
            first_t[:, there] = jnp.transpose(first)
            normal_ref[there, :] = normal.astype(jnp.bfloat16)
            scale_ref[there, :] = scale
            total_scr[there, :] = first.astype(jnp.float32) + norms[4:5, :]

    for stream, at in chunks:
        there = slice(stream * half_rows + at, stream * half_rows + at + ROWS)
        value = nn(first_scr[there, :], up_ref[...]) + up_bias[...]
        square = value * value
        half = 0.5 + 0.5 * jnp.tanh(value * (GELU_A + (GELU_A * GELU_B) * square))
        wide = value * half
        act = wide.astype(jnp.bfloat16)
        slope = half + (wide * (1.0 - half)) * ((2.0 * GELU_A) + (6.0 * GELU_A * GELU_B) * square)
        act_ref[there, :] = act
        slope_ref[there, :] = slope.astype(jnp.bfloat16)
        total_scr[there, :] += nn(act, down_ref[...])

    @pl.when(step == pl.num_programs(0) - 1)
    def _():
        sums = [jnp.zeros((1, content.shape[1]), jnp.float32) for _ in range(3)]
        for stream, at in chunks:
            here = pl.ds(at, ROWS)
            there = slice(stream * half_rows + at, stream * half_rows + at + ROWS)
            normal, scale = norm_parts(total_scr[there, :])
            rows_ref[there, :] = (normal * norms[2:3, :] + norms[3:4, :]).astype(jnp.bfloat16)
            cot = cots[stream, here, :].astype(jnp.float32)
            grad = norm_pull(normal, scale, cot * norms[2:3, :])
            grad_ref[there, :] = grad
            low = grad.astype(jnp.bfloat16)
            low_ref[there, :] = low
            low_t[:, there] = jnp.transpose(low)
            for at_sum, term in enumerate((cot * normal, cot, grad)):
                sums[at_sum] = sums[at_sum] + jnp.sum(term, axis=0, keepdims=True)
        sums_ref[...] = jnp.concatenate(sums + [jnp.zeros((5, content.shape[1]), jnp.float32)], axis=0)


def feed_forward(vec_c, vec_q, content, query, cots, out_use, up_use, down_use, up_bias, norms):
    seq_len, width = content.shape
    hidden = up_use.shape[1]
    cols = width // 2
    rows = 2 * seq_len
    low = jnp.bfloat16
    once = pl.Buffered(1)
    whole = lambda f: (0, 0)
    side = lambda f: (0, f)
    keep = lambda shape: pl.BlockSpec(shape, whole, pipeline_mode=once)
    stream = keep((seq_len, width))
    return pl.pallas_call(
        feed_forward_body,
        out_shape=(
            jax.ShapeDtypeStruct((width, rows), low),
            jax.ShapeDtypeStruct((rows, width), low),
            jax.ShapeDtypeStruct((rows, 1), jnp.float32),
            jax.ShapeDtypeStruct((rows, hidden), low),
            jax.ShapeDtypeStruct((rows, hidden), low),
            jax.ShapeDtypeStruct((rows, width), jnp.float32),
            jax.ShapeDtypeStruct((rows, width), low),
            jax.ShapeDtypeStruct((width, rows), low),
            jax.ShapeDtypeStruct((rows, width), low),
            jax.ShapeDtypeStruct((8, width), jnp.float32),
        ),
        grid=(hidden // cols,),
        in_specs=[
            stream, stream, stream, stream,
            pl.BlockSpec(cots.shape, lambda f: (0, 0, 0), pipeline_mode=once),
            keep((width, width)),
            pl.BlockSpec((width, cols), side),
            pl.BlockSpec((cols, width), lambda f: (f, 0)),
            pl.BlockSpec((1, cols), side),
            keep((8, width)),
        ],
        out_specs=[
            pl.BlockSpec((width, rows), whole),
            pl.BlockSpec((rows, width), whole),
            pl.BlockSpec((rows, 1), whole),
            pl.BlockSpec((rows, cols), side),
            pl.BlockSpec((rows, cols), side),
            pl.BlockSpec((rows, width), whole),
            pl.BlockSpec((rows, width), whole),
            pl.BlockSpec((width, rows), whole),
            pl.BlockSpec((rows, width), whole),
            pl.BlockSpec((8, width), whole),
        ],
        scratch_shapes=[
            pltpu.VMEM((rows, width), low),
            pltpu.VMEM((rows, width), jnp.float32),
        ],
        compiler_params=pltpu.CompilerParams(vmem_limit_bytes=60 << 20),
        name="feed_forward",
    )(vec_c, vec_q, content, query, cots, out_use, up_use, down_use, up_bias, norms)


FOLDS = 4
LAG = 2
EARLY = 9
COUNT = 13


def shear_left(value_in):
    rows, wide = value_in.shape
    pack = 16
    groups = []
    for group in range(rows // pack):
        piece = value_in[group * pack : (group + 1) * pack]
        groups.append(pltpu.roll(piece, wide - 1 - group * pack, 1))
    moved = jnp.concatenate(groups, axis=0)
    place = lax.broadcasted_iota(jnp.int32, (rows, wide), 0)
    step = 1
    while step < pack:
        moved = jnp.where((place & step) != 0, pltpu.roll(moved, wide - step, 1), moved)
        step = step * 2
    return moved


def backward_body(dp_size, *refs):
    (
        seg_hot, proj_c, proj_q, key_ref, value_ref, rel_ref, bias_ref, prob_ref,
        square_w, vec_c, vec_q, content_t, query_t, table_t, out_w,
        act_ref, slope_ref, up_ref, down_ref, low_ref, low_t, first_t, normal_ref, scale_ref,
        norms, sums_in, grad_in, rows_in,
        sum_out, small_out, keep_out, rows_came, grad_came,
        vt_scr, key_acc, value_acc, rel_acc, total, vec_grad, hid_scr,
        work, swapped, landed, extra, small_work, small_far, small_land,
        store_sem, swap_send, swap_recv, fold_send, fold_recv, spread_send, spread_recv,
        more_send, more_recv, tiny_send, tiny_recv, grad_sem, keep_sem, back_send, back_recv,
    ) = refs
    gproj_c = hid_scr.at[: key_ref.shape[0], :]
    gproj_q = hid_scr.at[key_ref.shape[0] :, :PAIR]
    ext_scr = hid_scr.at[key_ref.shape[0] :, PAIR:]
    grid_at = pl.program_id(0)
    feeds = 8
    pairs = 6
    half_pairs = pairs // 2
    last = pl.num_programs(0) - 1
    rows, cols = work.shape[1:]
    seq_len = key_ref.shape[0]
    place = lax.axis_index("dp")
    core = lax.axis_index("mp")
    strides = [1 + core, 2 - core, 4, 8]
    more = [16 << step for step in range(8) if (16 << step) < dp_size]
    bits = [(place // stride) % 2 for stride in strides]
    partners = [place + (1 - 2 * bit) * stride for bit, stride in zip(bits, strides)]
    more_partners = [place + (1 - 2 * ((place // stride) % 2)) * stride for stride in more]
    lengths = [rows >> (fold + 1) for fold in range(FOLDS)]
    starts, begin = [], 0
    for bit, length in zip(bits, lengths):
        begin = begin + bit * length
        starts.append(begin)
    land_at = [rows - 2 * length for length in lengths]
    offsets = [number * LAG for number in range(2 * FOLDS + 1)]
    final_slot = 20

    def kept(fold):
        return pl.ds(pl.multiple_of(starts[fold], 16), lengths[fold])

    def given(fold):
        return pl.ds(pl.multiple_of(starts[fold] + (1 - 2 * bits[fold]) * lengths[fold], 16), lengths[fold])

    def remote(source, target, send, recv, device):
        return pltpu.make_async_remote_copy(
            src_ref=source, dst_ref=target, send_sem=send, recv_sem=recv,
            device_id=device, device_id_type=MESH,
        )

    def swap_copy(piece):
        return remote(
            work.at[piece], swapped.at[piece], swap_send.at[piece], swap_recv.at[piece], {"mp": 1 - core}
        )

    def fold_copy(fold, piece):
        return remote(
            work.at[piece, given(fold)],
            landed.at[piece, pl.ds(land_at[fold], lengths[fold])],
            fold_send.at[fold, piece], fold_recv.at[fold, piece], {"dp": partners[fold]},
        )

    def spread_copy(fold, piece):
        return remote(
            swapped.at[piece, kept(fold)],
            swapped.at[piece, kept(fold)],
            spread_send.at[fold, piece], spread_recv.at[fold, piece], {"dp": partners[fold]},
        )

    def extra_ref(step, piece):
        if step == 0:
            return landed.at[piece, pl.ds(rows - lengths[-1], lengths[-1])]
        return extra.at[step - 1, piece]

    def more_copy(step, piece):
        return remote(
            work.at[piece, kept(FOLDS - 1)],
            extra_ref(step, piece),
            more_send.at[step, piece], more_recv.at[step, piece], {"dp": more_partners[step]},
        )

    def store(piece):
        return pltpu.make_async_copy(swapped.at[piece], sum_out.at[piece], store_sem.at[piece])

    def add_rows(piece, where, other):
        mine = work[piece, where, :].astype(jnp.float32)
        work[piece, where, :] = (mine + other.astype(jnp.float32)).astype(jnp.bfloat16)

    tiny_devices = [{"mp": 1 - core}] + [{"dp": partner} for partner in partners + more_partners]

    def tiny_copy(step):
        return remote(
            small_far if step == 0 else small_work.at[step],
            small_land.at[step], tiny_send.at[step], tiny_recv.at[step], tiny_devices[step],
        )

    far_rows = (1 - core) * ROWS

    def rows_copy(stream):
        return remote(
            rows_in.at[pl.ds(pl.multiple_of(stream * seq_len + far_rows, ROWS), ROWS)], rows_came.at[stream],
            back_send.at[stream], back_recv.at[stream], {"mp": 1 - core},
        )

    def grad_copy(stream):
        return remote(
            vec_grad.at[pl.ds(pl.multiple_of(stream * seq_len + far_rows, ROWS), ROWS)], grad_came.at[stream],
            back_send.at[2 + stream], back_recv.at[2 + stream], {"mp": 1 - core},
        )

    def keep_copy(stream):
        return pltpu.make_async_copy(
            vec_grad.at[pl.ds(pl.multiple_of(stream * seq_len + core * ROWS, ROWS), ROWS)],
            keep_out.at[stream], keep_sem.at[stream],
        )

    grad_load = pltpu.make_async_copy(grad_in, total, grad_sem)

    def stage(number, piece):
        if number == 0:
            fold_copy(0, piece).start()
        elif number <= FOLDS:
            fold = number - 1
            fold_copy(fold, piece).wait_recv()
            add_rows(piece, kept(fold), landed[piece, pl.ds(land_at[fold], lengths[fold]), :])
            if fold + 1 < FOLDS:
                fold_copy(fold + 1, piece).start()
                return
            for step in range(len(more)):
                more_copy(step, piece).start()
                more_copy(step, piece).wait()
                add_rows(piece, kept(fold), extra_ref(step, piece)[...])
            swapped[piece, kept(fold), :] = work[piece, kept(fold), :]
            spread_copy(fold, piece).start()
        else:
            fold = 2 * FOLDS - number
            remote(
                swapped.at[piece, kept(fold)], swapped.at[piece, given(fold)],
                spread_send.at[fold, piece], spread_recv.at[fold, piece], {"dp": partners[fold]},
            ).wait_recv()
            if fold > 0:
                spread_copy(fold - 1, piece).start()
            else:
                store(piece).start()

    def advance(tick):
        for number in reversed(range(2 * FOLDS + 1)):
            slot = tick - offsets[number]
            piece = jnp.where(slot < EARLY, slot, EARLY + (slot - 14) // 2)

            @pl.when(
                (slot >= 0)
                & ((slot < EARLY) | (slot == 15) | (slot == 17) | (slot == 19) | (slot == final_slot))
            )
            def _():
                stage(number, piece)

    def settle(piece):
        swap_copy(piece).wait_recv()
        add_rows(piece, pl.ds(0, rows), swapped[piece])

    @pl.when(grid_at == 0)
    def _():
        barrier = pltpu.get_barrier_semaphore()
        for device in tiny_devices:
            pl.semaphore_signal(barrier, inc=1, device_id=device, device_id_type=MESH)
        pl.semaphore_wait(barrier, len(tiny_devices))
        grad_load.start()
        rows_copy(0).start()
        rows_copy(1).start()
        small_work[0] = jnp.zeros_like(small_work[0])
        small_far[...] = jnp.zeros_like(small_far)
        for at in range(3):
            for side in range(2):
                line = sums_in[at : at + 1, side * cols : (side + 1) * cols]
                spot = slice(13 + 2 * at + side, 14 + 2 * at + side)
                small_work[0, spot, :] = line
                small_far[spot, :] = line
        grad_load.wait()

    @pl.when(grid_at < feeds)
    def _():
        chunk = grid_at // 2
        near = grid_at % 2 == 1
        bias_sum = jnp.zeros((1, cols), jnp.float32)
        for at in range(0, total.shape[0], ROWS):
            here = slice(at, at + ROWS)
            grad_act = nt(low_ref[here, :], down_ref[...])
            hid = (grad_act * slope_ref[here, :].astype(jnp.float32)).astype(jnp.bfloat16)
            hid_scr[here, :] = hid
            bias_sum = bias_sum + jnp.sum(hid.astype(jnp.float32), axis=0, keepdims=True)
            total[here, :] += nt(hid, up_ref[...])

        @pl.when(near)
        def _():
            swap_copy(2 * chunk).wait_send()
            swap_copy(2 * chunk + 1).wait_send()

        for at in range(0, rows, ROWS):
            here = slice(at, at + ROWS)
            work[2 * chunk, here, :] = nn(low_t[here, :], act_ref[...]).astype(jnp.bfloat16)
            work[2 * chunk + 1, here, :] = nn(first_t[here, :], hid_scr[...]).astype(jnp.bfloat16)

        @pl.when(near)
        def _():
            small_work[0, pl.ds(5 + chunk, 1), :] = bias_sum
            settle(2 * chunk)
            settle(2 * chunk + 1)

        @pl.when(jnp.logical_not(near))
        def _():
            small_far[pl.ds(5 + chunk, 1), :] = bias_sum
            swap_copy(2 * chunk).start()
            swap_copy(2 * chunk + 1).start()

    @pl.when(grid_at == feeds)
    def _():
        sums = [jnp.zeros((1, 2 * cols), jnp.float32) for _ in range(2)]
        out_piece = EARLY - 1
        near_sum = jnp.zeros((rows, cols), jnp.float32)
        far_sum = jnp.zeros((rows, cols), jnp.float32)
        for at in range(0, total.shape[0], ROWS):
            here = slice(at, at + ROWS)
            normal = normal_ref[here, :].astype(jnp.float32)
            grad = total[here, :]
            sums[0] = sums[0] + jnp.sum(grad * normal, axis=0, keepdims=True)
            sums[1] = sums[1] + jnp.sum(grad, axis=0, keepdims=True)
            grad = norm_pull(normal, scale_ref[here, :], grad * norms[0:1, :])
            total[here, :] = grad
            low = grad.astype(jnp.bfloat16)
            hid_scr[here, :] = low[:, :cols]
            vec_grad[here, :] = low
        for at in range(0, total.shape[0], ROWS):
            here = slice(at, at + ROWS)
            low = vec_grad[here, :]
            low_turn = jnp.transpose(low)
            vec = (vec_c, vec_q)[at // seq_len][at % seq_len : at % seq_len + ROWS, :]
            far_sum = far_sum + nn(low_turn, vec[:, cols:])
            near_sum = near_sum + nn(low_turn, vec[:, :cols])
            vec_grad[here, :] = nt(low, out_w[...]).astype(jnp.bfloat16)
        work[out_piece] = far_sum.astype(jnp.bfloat16)
        swap_copy(out_piece).start()
        for at in range(2):
            for side in range(2):
                line = sums[at][:, side * cols : (side + 1) * cols]
                spot = slice(9 + 2 * at + side, 10 + 2 * at + side)
                small_work[0, spot, :] = line
                small_far[spot, :] = line
        swap_copy(out_piece).wait()
        work[out_piece] = (near_sum + swapped[out_piece].astype(jnp.float32)).astype(jnp.bfloat16)

    @pl.when(grid_at > feeds)
    def _():
        turn = grid_at - feeds - 1
        pair = (turn + half_pairs) % pairs
        pair_lanes = pl.ds(pl.multiple_of(pair * PAIR, PAIR), PAIR)
        blocks = seq_len // ROWS
        wide = seq_len + ROWS
        ext_scr[:, :PAIR] = (key_ref[...].astype(jnp.float32) * 0.125).astype(jnp.bfloat16)
        ext_scr[:, PAIR:] = (seg_hot[...].astype(jnp.float32) * 0.125).astype(jnp.bfloat16)
        vt_scr[...] = jnp.transpose(value_ref[...])
        key_acc[...] = jnp.zeros_like(key_acc)
        value_acc[...] = jnp.zeros_like(value_acc)
        rel_acc[...] = jnp.zeros_like(rel_acc)
        lane = lane_ids(ROWS)
        first = lane < DH
        sums = [jnp.zeros((1, PAIR), jnp.float32) for _ in range(5)]
        for stream in range(2):
            proj_ref = (proj_c, proj_q)[stream]
            vec_ref = (vec_c, vec_q)[stream]
            gproj_ref = (gproj_c, gproj_q)[stream]
            for block in range(blocks):
                where = pl.ds(block * ROWS, ROWS)
                start = seq_len - (block + 1) * ROWS
                proj = proj_ref[where, :]
                query_ct = jnp.transpose(((proj + bias_ref[0:1, :]) * 0.125).astype(jnp.bfloat16))
                query_pt = jnp.transpose(((proj + bias_ref[1:2, :]) * 0.125).astype(jnp.bfloat16))
                query_s = proj + bias_ref[2:3, :]
                hot = jnp.where(lane < 4, seg_hot[where, :].astype(jnp.float32), 0.0)
                grad = vec_grad[pl.ds(stream * seq_len + block * ROWS, ROWS), pair_lanes]
                grad_t = jnp.transpose(grad)
                inner = grad.astype(jnp.float32) * vec_ref[where, pair_lanes].astype(jnp.float32)
                window = (rel_ref[pl.ds(start, wide), :].astype(jnp.float32) * 0.125).astype(jnp.bfloat16)
                parts = []
                for head in range(2):
                    own = (lane >= DH) if head else first
                    low, high = head * DH, (head + 1) * DH
                    prob = prob_ref[stream, head, where, :]
                    grad_prob = nn(jnp.where(own, grad, jnp.zeros((), jnp.bfloat16)), vt_scr[...])
                    row_inner = jnp.sum(jnp.where(own, inner, 0.0), axis=1, keepdims=True)
                    gscore = (prob.astype(jnp.float32) * (grad_prob - row_inner)).astype(jnp.bfloat16)
                    value_acc[low:high, :] += nn(grad_t[low:high, :], prob)
                    key_acc[low:high, :] += nn(query_ct[low:high, :], gscore)
                    both = nn(gscore, ext_scr[...])
                    table = jnp.concatenate([jnp.zeros((ROWS, ROWS), jnp.bfloat16), gscore], axis=1)
                    table = shear_left(table)
                    gpos = nn(table, window)
                    rel_acc[low:high, start : start + wide] += nn(query_pt[low:high, :], table)
                    tail = both[:, PAIR:]
                    tail = jnp.where(lane < 4, tail, 0.0)
                    g_same = jnp.sum(tail * hot, axis=1, keepdims=True)
                    g_other = jnp.sum(tail, axis=1, keepdims=True) - g_same
                    parts.append((both[:, :PAIR], gpos, g_same, g_other))
                g_content = jnp.where(first, parts[0][0], parts[1][0])
                g_position = jnp.where(first, parts[0][1], parts[1][1])
                g_same = jnp.where(first, parts[0][2], parts[1][2])
                g_other = jnp.where(first, parts[0][3], parts[1][3])
                g_segment = g_same * bias_ref[3:4, :] + g_other * bias_ref[4:5, :]
                gproj_ref[where, :PAIR] = (g_content + g_position + g_segment).astype(jnp.bfloat16)
                terms = (g_content, g_position, g_segment, g_same * query_s, g_other * query_s)
                sums = [old + jnp.sum(term, axis=0, keepdims=True) for old, term in zip(sums, terms)]
            if stream == 0:
                advance(2 * grid_at - 10)
        gproj_c[:, PAIR : 2 * PAIR] = jnp.transpose(key_acc[...]).astype(jnp.bfloat16)
        gproj_c[:, 2 * PAIR :] = jnp.transpose(value_acc[...]).astype(jnp.bfloat16)
        triple = nn(content_t[...], gproj_c[...])
        g_query = triple[:, :PAIR] + nn(query_t[...], gproj_q[...])
        g_rel = nt(table_t[...], rel_acc[...].astype(jnp.bfloat16))
        vectors = jnp.concatenate(sums, axis=0)
        weights = jnp.concatenate([square_w[0], square_w[1], square_w[2]], axis=1)
        total[:seq_len, :] += nt(gproj_c[...], weights)
        total[seq_len:, :] += nt(gproj_q[...], square_w[0])
        late = turn % half_pairs
        piece = EARLY + late
        rel_piece = EARLY + half_pairs
        lanes = pl.ds(pl.multiple_of(late * PAIR, PAIR), PAIR)

        @pl.when(turn >= half_pairs)
        def _():
            swap_copy(piece).wait_send()

            @pl.when(turn == half_pairs)
            def _():
                swap_copy(rel_piece).wait_send()

        work[piece, :, :PAIR] = g_query.astype(jnp.bfloat16)
        work[piece, :, PAIR:] = triple[:, PAIR:].astype(jnp.bfloat16)
        work[rel_piece, :, lanes] = g_rel.astype(jnp.bfloat16)

        @pl.when(turn < half_pairs)
        def _():
            small_far[0:5, lanes] = vectors
            swap_copy(piece).start()

            @pl.when(turn == half_pairs - 1)
            def _():
                swap_copy(rel_piece).start()
                tiny_copy(0).start()

        @pl.when(turn >= half_pairs)
        def _():
            small_work[0, 0:5, lanes] = vectors
            settle(piece)

            @pl.when(turn == pairs - 1)
            def _():
                settle(rel_piece)

    advance(grid_at - 1 + (grid_at // (feeds + 1)) * (grid_at - feeds))

    @pl.when(grid_at == last)
    def _():
        for at in range(0, total.shape[0], ROWS):
            vec_grad[at : at + ROWS, :] = total[at : at + ROWS, :].astype(jnp.bfloat16)
        begin_tick = final_slot

        def finish_tick(tick, carry):
            for step in range(len(tiny_devices)):
                @pl.when(tick == begin_tick + 1 + step)
                def _():
                    tiny_copy(step).wait_recv()
                    small_work[step + 1] = small_work[step] + small_land[step]
                    if step + 1 < len(tiny_devices):
                        tiny_copy(step + 1).start()

            advance(tick)

            @pl.when(tick == begin_tick)
            def _():
                grad_copy(0).start()
                grad_copy(1).start()
                keep_copy(0).start()
                keep_copy(1).start()

            return carry

        lax.fori_loop(begin_tick, final_slot + 1 + offsets[-1], finish_tick, 0)
        small_out[...] = small_work[len(tiny_devices)]
        for step in range(len(tiny_devices)):
            tiny_copy(step).wait_send()
        for stream in range(2):
            rows_copy(stream).wait()
            grad_copy(stream).wait()
            keep_copy(stream).wait()

        def drain(piece, carry):
            for fold in range(FOLDS):
                fold_copy(fold, piece).wait_send()
                spread_copy(fold, piece).wait_send()
            store(piece).wait()
            return carry

        lax.fori_loop(0, COUNT, drain, 0)


def backward(
    dp_size, seg_hot, proj_c, proj_q, keys, values, rel_keys, lines, prob, squares,
    vec_c, vec_q, content_t, query_t, table_t, out_w, act, slope, up_w, down_w, low_rows, low_t, first_t,
    normal, scale, norms, sums, grad, rows_in,
):
    seq_len, width = proj_c.shape
    pairs = width // PAIR
    cols = width // 2
    feeds = up_w.shape[1] // cols
    rows = 2 * seq_len
    small_rows = 24
    more = max(1, dp_size.bit_length() - 1 - FOLDS)
    tiny = dp_size.bit_length()
    low = jnp.bfloat16
    dma = pltpu.SemaphoreType.DMA
    once = pl.Buffered(1)
    anywhere = pl.BlockSpec(memory_space=pl.ANY)
    whole = lambda g: (0, 0)
    turn = lambda g: (jnp.maximum(g - feeds - 1, 0) + pairs // 2) % pairs
    per_pair = lambda g: (0, turn(g))
    tile = pl.BlockSpec((seq_len, PAIR), per_pair)

    def chunk(g):
        at = jnp.minimum(g, feeds - 1)
        return (1 - at % 2) * (feeds // 2) + at // 2

    side = lambda g: (0, chunk(g))
    keep = lambda shape: pl.BlockSpec(shape, whole, pipeline_mode=once)
    return pl.pallas_call(
        functools.partial(backward_body, dp_size),
        out_shape=(
            jax.ShapeDtypeStruct((COUNT, width, cols), low),
            jax.ShapeDtypeStruct((small_rows, cols), jnp.float32),
            jax.ShapeDtypeStruct((2, ROWS, width), low),
            jax.ShapeDtypeStruct((2, ROWS, width), low),
            jax.ShapeDtypeStruct((2, ROWS, width), low),
        ),
        grid_spec=pltpu.PrefetchScalarGridSpec(
            num_scalar_prefetch=0,
            grid=(feeds + 1 + pairs,),
            in_specs=[
                keep((seq_len, PAIR)),
                tile, tile, tile, tile,
                pl.BlockSpec((2 * seq_len, PAIR), per_pair),
                pl.BlockSpec((lines.shape[0], PAIR), per_pair),
                pl.BlockSpec((None, 2, 2, seq_len, seq_len), lambda g: (turn(g), 0, 0, 0, 0)),
                pl.BlockSpec((3, width, PAIR), lambda g: (0, 0, turn(g))),
                keep((seq_len, width)), keep((seq_len, width)),
                keep((width, seq_len)), keep((width, seq_len)), keep((width, 2 * seq_len)),
                keep((width, width)),
                pl.BlockSpec((rows, cols), side), pl.BlockSpec((rows, cols), side),
                pl.BlockSpec((width, cols), side), pl.BlockSpec((cols, width), lambda g: (chunk(g), 0)),
                keep((rows, width)), keep((width, rows)), keep((width, rows)), keep((rows, width)),
                keep((rows, 1)), keep((8, width)), keep((8, width)),
                anywhere, anywhere,
            ],
            out_specs=[
                anywhere,
                pl.BlockSpec((small_rows, cols), whole),
                anywhere, anywhere, anywhere,
            ],
            scratch_shapes=[
                pltpu.VMEM((PAIR, seq_len), low),
                pltpu.VMEM((PAIR, seq_len), jnp.float32),
                pltpu.VMEM((PAIR, seq_len), jnp.float32),
                pltpu.VMEM((PAIR, 2 * seq_len), jnp.float32),
                pltpu.VMEM((rows, width), jnp.float32),
                pltpu.VMEM((rows, width), low),
                pltpu.VMEM((rows, cols), low),
                pltpu.VMEM((COUNT, width, cols), low),
                pltpu.VMEM((COUNT, width, cols), low),
                pltpu.VMEM((COUNT, width, cols), low),
                pltpu.VMEM((max(1, more - 1), COUNT if dp_size > 32 else 1, width >> FOLDS, cols), low),
                pltpu.VMEM((tiny + 1, small_rows, cols), jnp.float32),
                pltpu.VMEM((small_rows, cols), jnp.float32),
                pltpu.VMEM((tiny, small_rows, cols), jnp.float32),
                dma((COUNT,)), dma((COUNT,)), dma((COUNT,)),
                dma((FOLDS, COUNT)), dma((FOLDS, COUNT)), dma((FOLDS, COUNT)), dma((FOLDS, COUNT)),
                dma((more, COUNT)), dma((more, COUNT)), dma((tiny,)), dma((tiny,)),
                dma, dma((2,)), dma((4,)), dma((4,)),
            ],
        ),
        compiler_params=pltpu.CompilerParams(
            collective_id=0, has_side_effects=True, vmem_limit_bytes=67043328
        ),
        name="backward",
    )(
        seg_hot, proj_c, proj_q, keys, values, rel_keys, lines, prob, squares,
        vec_c, vec_q, content_t, query_t, table_t, out_w, act, slope, up_w, down_w, low_rows, low_t, first_t,
        normal, scale, norms, sums, grad, rows_in,
    )


def finish_body(
    piece_ref, rows_ref, rows_came, keep_ref, grad_came,
    content_out, query_out, content_grad, query_grad, down_ref, up_ref, out_ref, query_ref, key_ref, value_ref, rel_ref,
):
    at = pl.program_id(0)
    core = lax.axis_index("mp")
    cols = piece_ref.shape[1]
    feeds = 8

    @pl.when((at < feeds) & (at % 2 == 0))
    def _():
        down_ref[...] = jnp.transpose(piece_ref[...].astype(jnp.float32))

    @pl.when((at < feeds) & (at % 2 == 1))
    def _():
        up_ref[...] = piece_ref[...].astype(jnp.float32)

    @pl.when(at == feeds)
    def _():
        out_ref[...] = jnp.transpose(piece_ref[...].astype(jnp.float32))

    for turn in range(3):
        lanes = slice(turn * PAIR, (turn + 1) * PAIR)

        @pl.when(at == EARLY + turn)
        def _():
            query_ref[:, lanes] = piece_ref[:, :PAIR].astype(jnp.float32)
            key_ref[:, lanes] = piece_ref[:, PAIR : 2 * PAIR].astype(jnp.float32)
            value_ref[:, lanes] = piece_ref[:, 2 * PAIR :].astype(jnp.float32)

    @pl.when(at == EARLY + 3)
    def _():
        rel_ref[...] = piece_ref[...].astype(jnp.float32)

    @pl.when(at == 0)
    def _():
        content_out[core] = rows_ref[core]
        content_out[1 - core] = rows_came[0]
        query_out[core] = rows_ref[2 + core]
        query_out[1 - core] = rows_came[1]
        content_grad[core] = keep_ref[0]
        content_grad[1 - core] = grad_came[0]
        query_grad[core] = keep_ref[1]
        query_grad[1 - core] = grad_came[1]


def finish(pieces, rows_out, rows_came, keep_rows, grad_came, half_ff):
    count, rows, cols = pieces.shape
    feeds = 2 * (half_ff // cols)
    square = jax.ShapeDtypeStruct((rows, cols), jnp.float32)
    pair = jax.ShapeDtypeStruct(rows_came.shape, jnp.bfloat16)
    whole = lambda p: (0, 0)
    block = pl.BlockSpec((rows, cols), whole)
    lead = lambda p: (0, 0, 0)
    once = pl.Buffered(1)
    token = pl.BlockSpec(rows_came.shape, lead)
    token_in = pl.BlockSpec(rows_came.shape, lead, pipeline_mode=once)
    at_chunk = lambda p: jnp.minimum(p // 2, feeds // 2 - 1)
    return pl.pallas_call(
        finish_body,
        out_shape=(
            pair, pair, pair, pair,
            jax.ShapeDtypeStruct((half_ff, rows), jnp.float32),
            jax.ShapeDtypeStruct((rows, half_ff), jnp.float32),
            jax.ShapeDtypeStruct((cols, rows), jnp.float32),
            square, square, square, square,
        ),
        grid=(count,),
        in_specs=[
            pl.BlockSpec((None, rows, cols), lambda p: (p, 0, 0)),
            pl.BlockSpec(rows_out.shape, lead, pipeline_mode=once),
            token_in, token_in, token_in,
        ],
        out_specs=[
            token, token, token, token,
            pl.BlockSpec((cols, rows), lambda p: (at_chunk(p), 0)),
            pl.BlockSpec((rows, cols), lambda p: (0, at_chunk(p))),
            pl.BlockSpec((cols, rows), whole),
            block, block, block, block,
        ],
        compiler_params=pltpu.CompilerParams(vmem_limit_bytes=48 << 20),
        name="finish",
    )(pieces, rows_out, rows_came, keep_rows, grad_came)


def position_table(seq_len, width):
    distance = seq_len - 1.0 - np.arange(2 * seq_len - 1, dtype=np.float32)
    freq_exp = np.arange(0, width, 2).astype(np.float32) / np.float32(width)
    inverse = np.float32(1.0) / np.float32(10000.0) ** freq_exp
    angle = (distance[:, None] * inverse[None, :]).astype(np.float32)
    table = np.concatenate([np.sin(angle), np.cos(angle)], axis=1)
    table = np.concatenate([table, np.zeros((1, width), np.float32)], axis=0)
    return table.astype(ml_dtypes.bfloat16)


def on_device(
    dp_size,
    content_in,
    query_in,
    doc_lengths,
    order_ranks,
    segment_ids,
    target_flags,
    query_weight,
    key_weight,
    value_weight,
    out_weight,
    rel_weight,
    content_bias,
    position_bias,
    segment_bias,
    segment_embed,
    first_gain,
    first_shift,
    up_weight,
    up_bias,
    down_weight,
    down_bias,
    second_gain,
    second_shift,
    content_cot,
    query_cot,
):
    half, width = content_in.shape[1:]
    seq_len = order_ranks.shape[1]
    cols = query_weight.shape[1]
    ff = up_weight.shape[1]
    wide_f = lambda value: value.astype(jnp.float32)
    meta = jnp.concatenate(
        [order_ranks, segment_ids, target_flags, jnp.broadcast_to(doc_lengths[:, None], order_ranks.shape)], axis=0
    ).astype(jnp.float32)
    up_rows = ff // cols
    vectors = jnp.concatenate(
        [
            content_bias[None], position_bias[None], segment_bias[None], segment_embed,
            up_bias.reshape(up_rows, cols), jnp.zeros(((-5 - up_rows) % 8, cols), jnp.bfloat16),
        ],
        axis=0,
    ).astype(jnp.float32)
    table = position_table(seq_len, width)
    (
        vec_c, vec_q, prob, proj_c, proj_q, keys, values, rel_keys, seg_hot, content_t, query_t, lines,
        content, query, cots, squares, out_use, up_use, down_use,
    ) = forward(
        content_in, query_in, content_cot, query_cot, query_weight, key_weight, value_weight, rel_weight,
        out_weight, up_weight, down_weight, meta, vectors, jnp.asarray(table),
    )
    up_bias_use = jnp.concatenate(
        [lines[5 : 5 + up_rows, :cols].reshape(1, ff), lines[5 : 5 + up_rows, cols:].reshape(1, ff)], axis=1
    )
    norms = jnp.stack(
        [first_gain, first_shift, second_gain, second_shift, down_bias, down_bias, down_bias, down_bias]
    ).astype(jnp.float32)
    first_t, normal, scale, act, slope, grad, low_rows, low_t, rows_out, sums = feed_forward(
        vec_c, vec_q, content, query, cots, out_use, up_use, down_use, up_bias_use, norms
    )
    pieces, tiny, keep_rows, rows_came, grad_came = backward(
        dp_size, seg_hot, proj_c, proj_q, keys, values, rel_keys, lines, prob, squares,
        vec_c, vec_q, content_t, query_t, jnp.asarray(table.T), out_use, act, slope, up_use, down_use,
        low_rows, low_t, first_t, normal, scale, norms, sums, grad, rows_out,
    )
    (
        content_out, query_out, content_grad, query_grad,
        down_sum, up_sum, out_sum, query_sum, key_sum, value_sum, rel_sum,
    ) = finish(pieces, rows_out.reshape(4, half, width), rows_came, keep_rows, grad_came, ff)
    split_rows = 5 + ff // cols
    same_part = tiny[split_rows : split_rows + 10].reshape(5, width)
    split_part = tiny[:5]
    return (
        content_out,
        query_out,
        content_grad,
        query_grad,
        query_sum,
        key_sum,
        value_sum,
        out_sum,
        rel_sum,
        split_part[0],
        split_part[1],
        split_part[2],
        split_part[3:5],
        same_part[0],
        same_part[1],
        up_sum,
        tiny[5:split_rows].reshape(ff),
        down_sum,
        same_part[4],
        same_part[2],
        same_part[3],
    )


def solution(mesh):
    placed = (
        P("dp", "mp", None),
        P("dp", "mp", None),
        P("dp"),
        P("dp", None),
        P("dp", None),
        P("dp", None),
        P(None, "mp"),
        P(None, "mp"),
        P(None, "mp"),
        P("mp", None),
        P(None, "mp"),
        P("mp"),
        P("mp"),
        P("mp"),
        P(None, "mp"),
        P(),
        P(),
        P(None, "mp"),
        P("mp"),
        P("mp", None),
        P(),
        P(),
        P(),
        P("dp", "mp", None),
        P("dp", "mp", None),
    )
    return jax.shard_map(
        functools.partial(on_device, mesh.shape["dp"]),
        mesh=mesh,
        in_specs=placed,
        out_specs=(
            P("dp", "mp", None),
            P("dp", "mp", None),
            P("dp", "mp", None),
            P("dp", "mp", None),
            P(None, "mp"),
            P(None, "mp"),
            P(None, "mp"),
            P("mp", None),
            P(None, "mp"),
            P("mp"),
            P("mp"),
            P("mp"),
            P(None, "mp"),
            P(),
            P(),
            P(None, "mp"),
            P("mp"),
            P("mp", None),
            P(),
            P(),
            P(),
        ),
        check_vma=False,
    )
```

```python
import functools

import jax
import jax.numpy as jnp
import ml_dtypes
import numpy as np
from jax import lax
from jax.experimental import pallas as pl
from jax.experimental.pallas import tpu as pltpu
from jax.sharding import PartitionSpec as P

epsilon = 1e-06
DH = 64
PAIR = 2 * DH
ROWS = 256
NEG = -1e30
MESH = pl.DeviceIdType.MESH


def nt(left_op, right_op):
    return lax.dot_general(
        left_op, right_op, (((1,), (1,)), ((), ())), preferred_element_type=jnp.float32
    )


def nn(left_op, right_op):
    return jnp.dot(left_op, right_op, preferred_element_type=jnp.float32)


def lane_ids(rows):
    return lax.broadcasted_iota(jnp.int32, (rows, PAIR), 1)


def forward_body(
    content_in, query_in, content_cot, query_cot, query_w, key_w, value_w, rel_w, out_w, up_w, down_w,
    length_ref, order_ref, segment_ref, target_ref, cbias_ref, pbias_ref, sbias_ref, embed_ref, ubias_ref, table_ref,
    vec_c, vec_q, prob_ref, proj_c, proj_q, key_ref, value_ref, rel_ref, hot_ref, content_t, query_t, vectors_out, ubias_out,
    content_out, query_out, cots_out, square_out, out_all, up_all, down_all,
    tokens, squares, near_pack, far_pack, bounce_up, bounce_down, bounce_out, bounce_cot, mask_scr, ext_scr, rank_scr,
    token_sem, token_send, token_recv, square_sem, square_send, square_recv,
    bulk_load, bulk_store, bulk_send, bulk_recv, vector_send, vector_recv,
):
    step = pl.program_id(0)
    core = lax.axis_index("mp")
    seq_len = proj_c.shape[0]
    half = seq_len // 2
    cols = query_w.shape[1]
    feed = up_w.shape[1]
    blocks = seq_len // ROWS
    wide = seq_len + ROWS
    other = {"mp": 1 - core}
    mine = pl.ds(pl.multiple_of(core * half, half), half)

    def remote(source, target, send, recv):
        return pltpu.make_async_remote_copy(
            src_ref=source, dst_ref=target, send_sem=send, recv_sem=recv,
            device_id=other, device_id_type=MESH,
        )

    token_in = (content_in, query_in)
    square_in = (query_w, key_w, value_w, rel_w)
    token_load = [
        pltpu.make_async_copy(token_in[at].at[core], tokens.at[at, mine], token_sem.at[at]) for at in range(2)
    ]
    token_swap = [
        remote(token_in[at].at[1 - core], tokens.at[at, mine], token_send.at[at], token_recv.at[at])
        for at in range(2)
    ]
    square_load = [
        pltpu.make_async_copy(square_in[at], squares.at[at, :, :cols], square_sem.at[at]) for at in range(4)
    ]
    square_swap = [
        remote(square_in[at], squares.at[at, :, cols:], square_send.at[at], square_recv.at[at])
        for at in range(4)
    ]
    vector_swap = remote(near_pack, far_pack, vector_send, vector_recv)
    cot_in = (content_cot, query_cot)
    bulk_loads = [
        pltpu.make_async_copy(out_w, bounce_out, bulk_load.at[0]),
        pltpu.make_async_copy(up_w, bounce_up, bulk_load.at[1]),
        pltpu.make_async_copy(down_w, bounce_down, bulk_load.at[2]),
    ] + [
        pltpu.make_async_copy(cot_in[at].at[core], bounce_cot.at[at], bulk_load.at[3 + at]) for at in range(2)
    ]
    bulk_stores = [
        pltpu.make_async_copy(bounce_out, out_all.at[:cols], bulk_store.at[0]),
        pltpu.make_async_copy(bounce_up, up_all.at[:, :feed], bulk_store.at[1]),
        pltpu.make_async_copy(bounce_down, down_all.at[:feed], bulk_store.at[2]),
    ] + [
        pltpu.make_async_copy(bounce_cot.at[at], cots_out.at[at, mine], bulk_store.at[3 + at]) for at in range(2)
    ]
    bulk_swaps = [
        remote(out_w, out_all.at[cols:], bulk_send.at[0], bulk_recv.at[0]),
        remote(up_w, up_all.at[:, feed:], bulk_send.at[1], bulk_recv.at[1]),
        remote(down_w, down_all.at[feed:], bulk_send.at[2], bulk_recv.at[2]),
    ] + [
        remote(cot_in[at].at[1 - core], cots_out.at[at, mine], bulk_send.at[3 + at], bulk_recv.at[3 + at])
        for at in range(2)
    ]
    token_store = [
        pltpu.make_async_copy(tokens.at[at], (content_out, query_out)[at], bulk_store.at[5 + at]) for at in range(2)
    ]
    square_store = [
        pltpu.make_async_copy(squares.at[at], square_out.at[at], bulk_store.at[7 + at]) for at in range(3)
    ]

    @pl.when(step == 0)
    def _():
        for copy in token_load + square_load:
            copy.start()
        near_pack[...] = jnp.zeros_like(near_pack)
        for at, part in enumerate((cbias_ref, pbias_ref, sbias_ref)):
            near_pack[at : at + 1, :cols] = part[...].astype(jnp.float32).reshape(1, cols)
        near_pack[3:5, :cols] = embed_ref[...].astype(jnp.float32)
        near_pack[5:6, :] = ubias_ref[...].astype(jnp.float32).reshape(1, feed)
        vectors_out[:, :cols] = near_pack[:, :cols]
        ubias_out[:, :feed] = near_pack[5:6, :]
        barrier = pltpu.get_barrier_semaphore()
        pl.semaphore_signal(barrier, inc=1, device_id=other, device_id_type=MESH)
        pl.semaphore_wait(barrier, 1)
        for copy in token_swap + [vector_swap] + square_swap + bulk_swaps + bulk_loads:
            copy.start()
        place_j = lax.broadcasted_iota(jnp.int32, (1, seq_len), 1)
        ranks = order_ref[pl.ds(core, 1), :].astype(jnp.float32)
        segments = segment_ref[pl.ds(core, 1), :].astype(jnp.float32)
        targets = target_ref[pl.ds(core, 1), :].astype(jnp.float32)
        length = length_ref[core]
        live = jnp.where(place_j >= 2, targets, 0.0)
        rank_scr[...] = jnp.transpose(jnp.broadcast_to(ranks, (PAIR, seq_len)))
        lane = lane_ids(seq_len)
        seg_turn = jnp.transpose(jnp.broadcast_to(segments, (PAIR, seq_len)))
        hot = (seg_turn == (lane % 4).astype(jnp.float32)) & (lane < 8)
        hot_ref[...] = jnp.where(hot, 1.0, 0.0).astype(jnp.bfloat16)
        base = jnp.where(place_j < length, 0.0, NEG)
        for block in range(blocks):
            rows = slice(block * ROWS, (block + 1) * ROWS)
            rank_i = jnp.concatenate([rank_scr[rows, :]] * (seq_len // PAIR), axis=1)
            seen = jnp.where((live == 0.0) | (ranks < rank_i), base, NEG)
            column = lax.broadcasted_iota(jnp.int32, (ROWS, seq_len), 1)
            line = lax.broadcasted_iota(jnp.int32, (ROWS, seq_len), 0) + block * ROWS
            diagonal = column == line
            mask_scr[0, rows, :] = jnp.where(diagonal, 0.0, seen)
            mask_scr[1, rows, :] = jnp.where(diagonal, NEG, seen)
        for copy in token_load + square_load:
            copy.wait()
        for copy in token_swap:
            copy.wait_recv()
        for copy in token_store:
            copy.start()

    @pl.when(step == 1)
    def _():
        for copy in bulk_loads:
            copy.wait()
        for copy in bulk_stores:
            copy.start()
        content_t[...] = jnp.transpose(tokens[0])
        query_t[...] = jnp.transpose(tokens[1])

    @pl.when(step == pl.num_programs(0) // 2)
    def _():
        for copy in square_swap + [vector_swap]:
            copy.wait_recv()
        for copy in square_store:
            copy.start()
        vectors_out[:, cols:] = far_pack[:, :cols]
        ubias_out[:, feed:] = far_pack[5:6, :]

    pair_lanes = pl.ds(pl.multiple_of(step * PAIR, PAIR), PAIR)
    lines = vectors_out[:, pair_lanes]
    triple_w = jnp.concatenate([squares[at, :, pair_lanes] for at in range(3)], axis=1)
    for block in range(blocks):
        rows = slice(block * ROWS, (block + 1) * ROWS)
        triple = nn(tokens[0, rows, :], triple_w)
        proj_c[rows, :] = triple[:, :PAIR]
        key_ref[rows, :] = triple[:, PAIR : 2 * PAIR].astype(jnp.bfloat16)
        value_ref[rows, :] = triple[:, 2 * PAIR :].astype(jnp.bfloat16)
        proj_q[rows, :] = nn(tokens[1, rows, :], squares[0, :, pair_lanes])
    for block in range(2 * blocks):
        rows = slice(block * ROWS, (block + 1) * ROWS)
        rel_ref[rows, :] = nn(table_ref[rows, :], squares[3, :, pair_lanes]).astype(jnp.bfloat16)
    ext_scr[:, :PAIR] = key_ref[...]
    ext_scr[:, PAIR:] = hot_ref[...]
    lane = lane_ids(ROWS)
    diff = lines[3:4, :] - lines[4:5, :]
    for stream in range(2):
        proj_ref = (proj_c, proj_q)[stream]
        vec_ref = (vec_c, vec_q)[stream]
        for block in range(blocks):
            rows = pl.ds(block * ROWS, ROWS)
            proj = proj_ref[rows, :]
            query_c = ((proj + lines[0:1, :]) * 0.125).astype(jnp.bfloat16)
            query_p = ((proj + lines[1:2, :]) * 0.125).astype(jnp.bfloat16)
            seg_gap = (proj + lines[2:3, :]) * (diff * 0.125)
            hot = hot_ref[rows, :].astype(jnp.float32)
            window = rel_ref[pl.ds(seq_len - (block + 1) * ROWS, wide), :]
            vec_pair = None
            for head in range(2):
                own = (lane >= DH) if head else (lane < DH)
                zero = jnp.zeros((), jnp.bfloat16)
                gap = jnp.sum(jnp.where(own, seg_gap, 0.0), axis=1, keepdims=True)
                gap_high = gap.astype(jnp.bfloat16).astype(jnp.float32)
                seg_part = (jnp.where(lane < 4, gap_high, gap - gap_high) * hot).astype(jnp.bfloat16)
                left = jnp.concatenate([jnp.where(own, query_c, zero), seg_part], axis=1)
                scores = nt(left, ext_scr[...])
                table = nt(jnp.where(own, query_p, zero), window)
                table = pltpu.roll(table, 1, 1, stride=1, stride_axis=0)
                scores = scores + table[:, ROWS:] + mask_scr[stream, rows, :]
                top = jnp.max(scores, axis=1, keepdims=True)
                terms = jnp.exp(scores - top)
                total = jnp.sum(terms, axis=1, keepdims=True)
                prob = (terms * (1.0 / total)).astype(jnp.bfloat16)
                prob_ref[stream, head, rows, :] = prob
                part = nn(prob, value_ref[...])
                vec_pair = part if head == 0 else jnp.where(own, part, vec_pair)
            vec_ref[rows, :] = vec_pair.astype(jnp.bfloat16)

    @pl.when(step == pl.num_programs(0) - 1)
    def _():
        for copy in token_swap + square_swap + [vector_swap]:
            copy.wait_send()
        for copy in bulk_swaps:
            copy.wait()
        for copy in bulk_stores + token_store + square_store:
            copy.wait()


def forward(
    content_in, query_in, content_cot, query_cot, query_w, key_w, value_w, rel_w, out_w, up_w, down_w,
    lengths, orders, segments, targets, cbias, pbias, sbias, embed, ubias, table,
):
    once = pl.Buffered(1)
    half, width = content_in.shape[1:]
    seq_len = 2 * half
    pairs = width // PAIR
    cols = query_w.shape[1]
    feed = up_w.shape[1]
    lines = 8
    keep = lambda shape: pl.BlockSpec(shape, lambda p: (0,) * len(shape), pipeline_mode=once)
    low = jnp.bfloat16
    dma = pltpu.SemaphoreType.DMA
    whole = lambda p: (0, 0)
    anywhere = pl.BlockSpec(memory_space=pl.ANY)
    tile = pl.BlockSpec((seq_len, PAIR), lambda p: (0, p))
    low_tokens = jax.ShapeDtypeStruct((seq_len, width), low)
    turned = jax.ShapeDtypeStruct((width, seq_len), low)
    return pl.pallas_call(
        forward_body,
        out_shape=(
            low_tokens, low_tokens,
            jax.ShapeDtypeStruct((pairs, 2, 2, seq_len, seq_len), low),
            jax.ShapeDtypeStruct((seq_len, width), jnp.float32),
            jax.ShapeDtypeStruct((seq_len, width), jnp.float32),
            low_tokens, low_tokens,
            jax.ShapeDtypeStruct((2 * seq_len, width), low),
            jax.ShapeDtypeStruct((seq_len, PAIR), low),
            turned, turned,
            jax.ShapeDtypeStruct((lines, width), jnp.float32),
            jax.ShapeDtypeStruct((1, 2 * feed), jnp.float32),
            low_tokens, low_tokens,
            jax.ShapeDtypeStruct((2, seq_len, width), low),
            jax.ShapeDtypeStruct((3, width, width), low),
            jax.ShapeDtypeStruct((width, width), low),
            jax.ShapeDtypeStruct((width, 2 * feed), low),
            jax.ShapeDtypeStruct((2 * feed, width), low),
        ),
        grid_spec=pltpu.PrefetchScalarGridSpec(
            num_scalar_prefetch=0,
            grid=(pairs,),
            in_specs=[anywhere] * 11
            + [
                pl.BlockSpec(memory_space=pltpu.SMEM),
                keep(orders.shape), keep(orders.shape), keep(orders.shape),
                keep(cbias.shape), keep(cbias.shape), keep(cbias.shape), keep(embed.shape), keep(ubias.shape),
                keep((2 * seq_len, width)),
            ],
            out_specs=[
                tile, tile,
                pl.BlockSpec((None, 2, 2, seq_len, seq_len), lambda p: (p, 0, 0, 0, 0)),
                tile, tile, tile, tile,
                pl.BlockSpec((2 * seq_len, PAIR), lambda p: (0, p)),
                pl.BlockSpec((seq_len, PAIR), whole),
                pl.BlockSpec((width, seq_len), whole),
                pl.BlockSpec((width, seq_len), whole),
                pl.BlockSpec((lines, width), whole),
                pl.BlockSpec((1, 2 * feed), whole),
            ]
            + [anywhere] * 7,
            scratch_shapes=[
                pltpu.VMEM((2, seq_len, width), low),
                pltpu.VMEM((4, width, width), low),
                pltpu.VMEM((lines, feed), jnp.float32),
                pltpu.VMEM((lines, feed), jnp.float32),
                pltpu.VMEM((width, feed), low),
                pltpu.VMEM((feed, width), low),
                pltpu.VMEM((cols, width), low),
                pltpu.VMEM((2, half, width), low),
                pltpu.VMEM((2, seq_len, seq_len), jnp.float32),
                pltpu.VMEM((seq_len, 2 * PAIR), low),
                pltpu.VMEM((seq_len, PAIR), jnp.float32),
                dma((2,)), dma((2,)), dma((2,)), dma((4,)), dma((4,)), dma((4,)),
                dma((5,)), dma((10,)), dma((5,)), dma((5,)), dma, dma,
            ],
        ),
        compiler_params=pltpu.CompilerParams(
            collective_id=1, has_side_effects=True, vmem_limit_bytes=60 << 20
        ),
        name="attend_forward",
    )(
        content_in, query_in, content_cot, query_cot, query_w, key_w, value_w, rel_w, out_w, up_w, down_w,
        lengths, orders, segments, targets, cbias, pbias, sbias, embed, ubias, table,
    )


GELU_A = 0.7978845608028654
GELU_B = 0.044715


def norm_parts(value_in):
    center = value_in - jnp.mean(value_in, axis=1, keepdims=True)
    scale = lax.rsqrt(jnp.mean(center * center, axis=1, keepdims=True) + epsilon)
    return center * scale, scale


def norm_pull(normal, scale, grad):
    return scale * (
        grad
        - jnp.mean(grad, axis=1, keepdims=True)
        - normal * jnp.mean(grad * normal, axis=1, keepdims=True)
    )


def feed_forward_body(
    vec_c, vec_q, content, query, cots, out_ref, up_ref, down_ref, up_bias,
    gain1_ref, shift1_ref, gain2_ref, shift2_ref, dbias_ref,
    first_t, normal_ref, scale_ref, act_ref, slope_ref, grad_ref, low_ref, low_t, rows_ref, sums_ref, norms,
    first_scr, total_scr,
):
    step = pl.program_id(0)
    half_rows = vec_c.shape[0]
    chunks = [(s, at) for s in range(2) for at in range(0, half_rows, ROWS)]

    @pl.when(step == 0)
    def _():
        norms[...] = jnp.zeros_like(norms)
        for at, part in enumerate((gain1_ref, shift1_ref, gain2_ref, shift2_ref, dbias_ref)):
            norms[at : at + 1, :] = part[...].astype(jnp.float32).reshape(1, part.shape[0])
        for stream, at in chunks:
            here = pl.ds(at, ROWS)
            there = slice(stream * half_rows + at, stream * half_rows + at + ROWS)
            mixed = nn((vec_c, vec_q)[stream][here, :], out_ref[...])
            mixed = mixed + (content, query)[stream][here, :].astype(jnp.float32)
            normal, scale = norm_parts(mixed)
            first = (normal * norms[0:1, :] + norms[1:2, :]).astype(jnp.bfloat16)
            first_scr[there, :] = first
            first_t[:, there] = jnp.transpose(first)
            normal_ref[there, :] = normal.astype(jnp.bfloat16)
            scale_ref[there, :] = scale
            total_scr[there, :] = first.astype(jnp.float32) + norms[4:5, :]

    for stream, at in chunks:
        there = slice(stream * half_rows + at, stream * half_rows + at + ROWS)
        value = nn(first_scr[there, :], up_ref[...]) + up_bias[...]
        square = value * value
        half = 0.5 + 0.5 * jnp.tanh(value * (GELU_A + (GELU_A * GELU_B) * square))
        wide = value * half
        act = wide.astype(jnp.bfloat16)
        slope = half + (wide * (1.0 - half)) * ((2.0 * GELU_A) + (6.0 * GELU_A * GELU_B) * square)
        act_ref[there, :] = act
        slope_ref[there, :] = slope.astype(jnp.bfloat16)
        total_scr[there, :] += nn(act, down_ref[...])

    @pl.when(step == pl.num_programs(0) - 1)
    def _():
        sums = [jnp.zeros((1, content.shape[1]), jnp.float32) for _ in range(3)]
        for stream, at in chunks:
            here = pl.ds(at, ROWS)
            there = slice(stream * half_rows + at, stream * half_rows + at + ROWS)
            normal, scale = norm_parts(total_scr[there, :])
            rows_ref[there, :] = (normal * norms[2:3, :] + norms[3:4, :]).astype(jnp.bfloat16)
            cot = cots[stream, here, :].astype(jnp.float32)
            grad = norm_pull(normal, scale, cot * norms[2:3, :])
            grad_ref[there, :] = grad
            low = grad.astype(jnp.bfloat16)
            low_ref[there, :] = low
            low_t[:, there] = jnp.transpose(low)
            for at_sum, term in enumerate((cot * normal, cot, grad)):
                sums[at_sum] = sums[at_sum] + jnp.sum(term, axis=0, keepdims=True)
        sums_ref[...] = jnp.concatenate(sums + [jnp.zeros((5, content.shape[1]), jnp.float32)], axis=0)


def feed_forward(vec_c, vec_q, content, query, cots, out_use, up_use, down_use, up_bias, vectors):
    seq_len, width = content.shape
    hidden = up_use.shape[1]
    cols = 512
    rows = 2 * seq_len
    low = jnp.bfloat16
    once = pl.Buffered(1)
    whole = lambda f: (0, 0)
    side = lambda f: (0, f)
    keep = lambda shape: pl.BlockSpec(shape, whole, pipeline_mode=once)
    stream = keep((seq_len, width))
    return pl.pallas_call(
        feed_forward_body,
        out_shape=(
            jax.ShapeDtypeStruct((width, rows), low),
            jax.ShapeDtypeStruct((rows, width), low),
            jax.ShapeDtypeStruct((rows, 1), jnp.float32),
            jax.ShapeDtypeStruct((rows, hidden), low),
            jax.ShapeDtypeStruct((rows, hidden), low),
            jax.ShapeDtypeStruct((rows, width), jnp.float32),
            jax.ShapeDtypeStruct((rows, width), low),
            jax.ShapeDtypeStruct((width, rows), low),
            jax.ShapeDtypeStruct((rows, width), low),
            jax.ShapeDtypeStruct((8, width), jnp.float32),
            jax.ShapeDtypeStruct((8, width), jnp.float32),
        ),
        grid=(hidden // cols,),
        in_specs=[
            stream, stream, stream, stream,
            pl.BlockSpec(cots.shape, lambda f: (0, 0, 0), pipeline_mode=once),
            keep((width, width)),
            pl.BlockSpec((width, cols), side),
            pl.BlockSpec((cols, width), lambda f: (f, 0)),
            pl.BlockSpec((1, cols), side),
            pl.BlockSpec((width,), lambda f: (0,)), pl.BlockSpec((width,), lambda f: (0,)), pl.BlockSpec((width,), lambda f: (0,)),
            pl.BlockSpec((width,), lambda f: (0,)), pl.BlockSpec((width,), lambda f: (0,)),
        ],
        out_specs=[
            pl.BlockSpec((width, rows), whole),
            pl.BlockSpec((rows, width), whole),
            pl.BlockSpec((rows, 1), whole),
            pl.BlockSpec((rows, cols), side),
            pl.BlockSpec((rows, cols), side),
            pl.BlockSpec((rows, width), whole),
            pl.BlockSpec((rows, width), whole),
            pl.BlockSpec((width, rows), whole),
            pl.BlockSpec((rows, width), whole),
            pl.BlockSpec((8, width), whole),
            pl.BlockSpec((8, width), whole),
        ],
        scratch_shapes=[
            pltpu.VMEM((rows, width), low),
            pltpu.VMEM((rows, width), jnp.float32),
        ],
        compiler_params=pltpu.CompilerParams(vmem_limit_bytes=60 << 20),
        name="feed_forward",
    )(vec_c, vec_q, content, query, cots, out_use, up_use, down_use, up_bias, *vectors)


FOLDS = 4
EARLY = 7
COUNT = 10
CHUNK = 512


def backward_body(dp_size, *refs):
    (
        seg_hot, proj_c, proj_q, key_ref, value_ref, rel_ref, bias_ref, prob_ref,
        square_w, vec_c, vec_q, out_w, act_ref, slope_ref, up_ref, down_ref, low_ref, scale_ref, norms, sums_in,
        content_t, query_t, table_t, low_t, first_t, normal_in, grad_in, rows_in,
        sum_out, small_out, keep_out, rows_came, grad_came,
        vt_scr, key_acc, value_acc, rel_acc, total, vec_grad, hid_scr, turn_a, turn_b, flip_scr,
        work, swapped, landed, extra, small_work, small_far, small_land,
        store_sem, swap_send, swap_recv, fold_send, fold_recv, spread_send, spread_recv,
        more_send, more_recv, tiny_send, tiny_recv, side_sem, keep_sem, back_send, back_recv,
    ) = refs
    seq_len = key_ref.shape[0]
    gproj_c = hid_scr.at[:seq_len, : 3 * PAIR]
    gproj_q = hid_scr.at[seq_len:, :PAIR]
    ext_scr = hid_scr.at[seq_len:, PAIR : 3 * PAIR]
    grid_at = pl.program_id(0)
    feeds = 6
    pairs = 6
    half_pairs = pairs // 2
    last = pl.num_programs(0) - 1
    rows, width = total.shape[1], work.shape[2]
    cols = rows // 2
    place = lax.axis_index("dp")
    core = lax.axis_index("mp")
    strides = [1 + core, 2 - core, 4, 8]
    more = [16 << step for step in range(8) if (16 << step) < dp_size]
    bits = [(place // stride) % 2 for stride in strides]
    partners = [place + (1 - 2 * bit) * stride for bit, stride in zip(bits, strides)]
    more_partners = [place + (1 - 2 * ((place // stride) % 2)) * stride for stride in more]
    lengths = [rows >> (fold + 1) for fold in range(FOLDS)]
    starts, begin = [], 0
    for bit, length in zip(bits, lengths):
        begin = begin + bit * length
        starts.append(begin)
    land_at = [rows - 2 * length for length in lengths]
    offsets = [0, 3, 5, 7, 9, 11, 13, 15, 18]
    final_slot = 25

    def kept(fold):
        return pl.ds(pl.multiple_of(starts[fold], 16), lengths[fold])

    def given(fold):
        return pl.ds(pl.multiple_of(starts[fold] + (1 - 2 * bits[fold]) * lengths[fold], 16), lengths[fold])

    def remote(source, target, send, recv, device):
        return pltpu.make_async_remote_copy(
            src_ref=source, dst_ref=target, send_sem=send, recv_sem=recv,
            device_id=device, device_id_type=MESH,
        )

    def swap_copy(piece):
        return remote(
            work.at[piece], swapped.at[piece], swap_send.at[piece], swap_recv.at[piece], {"mp": 1 - core}
        )

    def fold_copy(fold, piece):
        return remote(
            work.at[piece, given(fold)],
            landed.at[piece, pl.ds(land_at[fold], lengths[fold])],
            fold_send.at[fold, piece], fold_recv.at[fold, piece], {"dp": partners[fold]},
        )

    def spread_copy(fold, piece):
        return remote(
            swapped.at[piece, kept(fold)],
            swapped.at[piece, kept(fold)],
            spread_send.at[fold, piece], spread_recv.at[fold, piece], {"dp": partners[fold]},
        )

    def extra_ref(step, piece):
        if step == 0:
            return landed.at[piece, pl.ds(rows - lengths[-1], lengths[-1])]
        return extra.at[step - 1, piece]

    def more_copy(step, piece):
        return remote(
            work.at[piece, kept(FOLDS - 1)],
            extra_ref(step, piece),
            more_send.at[step, piece], more_recv.at[step, piece], {"dp": more_partners[step]},
        )

    def store(piece):
        return pltpu.make_async_copy(swapped.at[piece], sum_out.at[piece], store_sem.at[piece])

    def add_rows(piece, where, other):
        mine = work[piece, where, :].astype(jnp.float32)
        work[piece, where, :] = (mine + other.astype(jnp.float32)).astype(jnp.bfloat16)

    tiny_devices = [{"mp": 1 - core}] + [{"dp": partner} for partner in partners + more_partners]

    def tiny_copy(step):
        return remote(
            small_far if step == 0 else small_work.at[step],
            small_land.at[step], tiny_send.at[step], tiny_recv.at[step], tiny_devices[step],
        )

    far_rows = (1 - core) * ROWS

    def rows_copy(stream):
        return remote(
            rows_in.at[pl.ds(pl.multiple_of(stream * seq_len + far_rows, ROWS), ROWS)], rows_came.at[stream],
            back_send.at[stream], back_recv.at[stream], {"mp": 1 - core},
        )

    def grad_copy(stream):
        return remote(
            vec_grad.at[pl.ds(pl.multiple_of(stream * seq_len + far_rows, ROWS), ROWS)], grad_came.at[stream],
            back_send.at[2 + stream], back_recv.at[2 + stream], {"mp": 1 - core},
        )

    def keep_copy(stream):
        return pltpu.make_async_copy(
            vec_grad.at[pl.ds(pl.multiple_of(stream * seq_len + core * ROWS, ROWS), ROWS)],
            keep_out.at[stream], keep_sem.at[stream],
        )

    side_loads = [
        pltpu.make_async_copy(source, target, side_sem.at[at])
        for at, (source, target) in enumerate(
            (
                (grad_in, total),
                (first_t, turn_a),
                (low_t, turn_b),
                (normal_in, vec_grad),
                (table_t, turn_a),
                (content_t, turn_b.at[:, :seq_len]),
                (query_t, turn_b.at[:, seq_len:]),
            )
        )
    ]

    def stage(number, piece):
        if number == 0:
            fold_copy(0, piece).start()
        elif number <= FOLDS:
            fold = number - 1
            fold_copy(fold, piece).wait_recv()
            add_rows(piece, kept(fold), landed[piece, pl.ds(land_at[fold], lengths[fold]), :])
            if fold + 1 < FOLDS:
                fold_copy(fold + 1, piece).start()
                return
            for step in range(len(more)):
                more_copy(step, piece).start()
                more_copy(step, piece).wait()
                add_rows(piece, kept(fold), extra_ref(step, piece)[...])
            swapped[piece, kept(fold), :] = work[piece, kept(fold), :]
            spread_copy(fold, piece).start()
        else:
            fold = 2 * FOLDS - number
            remote(
                swapped.at[piece, kept(fold)], swapped.at[piece, given(fold)],
                spread_send.at[fold, piece], spread_recv.at[fold, piece], {"dp": partners[fold]},
            ).wait_recv()
            if fold > 0:
                spread_copy(fold - 1, piece).start()
            else:
                store(piece).start()

    def advance(tick):
        for number in reversed(range(2 * FOLDS + 1)):
            slot = tick - offsets[number]
            early = (slot == 3) | (slot == 4) | (slot == 7) | (slot == 8) | (slot == 11) | (slot == 12)
            late = (slot == 13) | (slot == 17) | (slot == 21) | (slot == final_slot)
            piece = jnp.where(slot < 13, 2 * ((slot - 3) // 4) + (slot - 3) % 4, EARLY - 1 + (slot - 13) // 4)

            @pl.when(early | late)
            def _():
                stage(number, piece)

    def settle(piece):
        swap_copy(piece).wait_recv()
        add_rows(piece, pl.ds(0, rows), swapped[piece])

    @pl.when(grid_at == 0)
    def _():
        barrier = pltpu.get_barrier_semaphore()
        for device in tiny_devices:
            pl.semaphore_signal(barrier, inc=1, device_id=device, device_id_type=MESH)
        pl.semaphore_wait(barrier, len(tiny_devices))
        for copy in side_loads[:4]:
            copy.start()
        rows_copy(0).start()
        rows_copy(1).start()
        small_work[0] = jnp.zeros_like(small_work[0])
        small_far[...] = jnp.zeros_like(small_far)
        for at in range(3):
            for side in range(2):
                line = sums_in[at : at + 1, side * cols : (side + 1) * cols]
                spot = slice(12 + 2 * at + side, 13 + 2 * at + side)
                small_work[0, spot, :cols] = line
                small_far[spot, :cols] = line
        line_at = lax.broadcasted_iota(jnp.int32, (ROWS, ROWS), 0)
        lane_at = lax.broadcasted_iota(jnp.int32, (ROWS, ROWS), 1)
        flip_scr[...] = jnp.where(line_at + lane_at == ROWS - 1, 1.0, 0.0).astype(jnp.bfloat16)
        for copy in side_loads[:3]:
            copy.wait()

    @pl.when(grid_at < feeds)
    def _():
        chunk = grid_at // 2
        near = grid_at % 2 == 1
        bias_sum = jnp.zeros((1, width), jnp.float32)
        for at in range(0, total.shape[0], ROWS):
            here = slice(at, at + ROWS)
            grad_act = nt(low_ref[here, :], down_ref[...])
            hid = (grad_act * slope_ref[here, :].astype(jnp.float32)).astype(jnp.bfloat16)
            hid_scr[here, :] = hid
            bias_sum = bias_sum + jnp.sum(hid.astype(jnp.float32), axis=0, keepdims=True)
            total[here, :] += nt(hid, up_ref[...])

        advance(2 * grid_at)

        @pl.when(near)
        def _():
            swap_copy(2 * chunk).wait_send()
            swap_copy(2 * chunk + 1).wait_send()

        for at in range(0, rows, ROWS):
            here = slice(at, at + ROWS)
            work[2 * chunk, here, :] = nn(turn_b[here, :], act_ref[...]).astype(jnp.bfloat16)
            work[2 * chunk + 1, here, :] = nn(turn_a[here, :], hid_scr[...]).astype(jnp.bfloat16)

        @pl.when(near)
        def _():
            small_work[0, pl.ds(5 + chunk, 1), :] = bias_sum
            settle(2 * chunk)
            settle(2 * chunk + 1)

        @pl.when(jnp.logical_not(near))
        def _():
            small_far[pl.ds(5 + chunk, 1), :] = bias_sum
            swap_copy(2 * chunk).start()
            swap_copy(2 * chunk + 1).start()

    @pl.when(grid_at == feeds)
    def _():
        advance(2 * grid_at)
        for copy in side_loads[4:]:
            copy.start()
        side_loads[3].wait()
        sums = [jnp.zeros((1, rows), jnp.float32) for _ in range(2)]
        out_piece = EARLY - 1
        near_sum = jnp.zeros((rows, cols), jnp.float32)
        far_sum = jnp.zeros((rows, cols), jnp.float32)
        for at in range(0, total.shape[0], ROWS):
            here = slice(at, at + ROWS)
            normal = vec_grad[here, :].astype(jnp.float32)
            grad = total[here, :]
            sums[0] = sums[0] + jnp.sum(grad * normal, axis=0, keepdims=True)
            sums[1] = sums[1] + jnp.sum(grad, axis=0, keepdims=True)
            grad = norm_pull(normal, scale_ref[here, :], grad * norms[0:1, :])
            total[here, :] = grad
            vec_grad[here, :] = grad.astype(jnp.bfloat16)
        for at in range(0, total.shape[0], ROWS):
            here = slice(at, at + ROWS)
            low = vec_grad[here, :]
            low_turn = jnp.transpose(low)
            vec = (vec_c, vec_q)[at // seq_len][at % seq_len : at % seq_len + ROWS, :]
            far_sum = far_sum + nn(low_turn, vec[:, cols:])
            near_sum = near_sum + nn(low_turn, vec[:, :cols])
            vec_grad[here, :] = nt(low, out_w[...]).astype(jnp.bfloat16)
        work[out_piece, :, :cols] = far_sum.astype(jnp.bfloat16)
        work[out_piece, :, cols:] = jnp.zeros((rows, width - cols), jnp.bfloat16)
        swap_copy(out_piece).start()
        for at in range(2):
            for side in range(2):
                line = sums[at][:, side * cols : (side + 1) * cols]
                spot = slice(8 + 2 * at + side, 9 + 2 * at + side)
                small_work[0, spot, :cols] = line
                small_far[spot, :cols] = line
        swap_copy(out_piece).wait()
        near_sum = near_sum + swapped[out_piece, :, :cols].astype(jnp.float32)
        work[out_piece, :, :cols] = near_sum.astype(jnp.bfloat16)

    @pl.when(grid_at > feeds)
    def _():
        turn = grid_at - feeds - 1
        late = turn // 2
        near = turn % 2 == 1
        pair = late + (1 - turn % 2) * half_pairs

        @pl.when(turn == 0)
        def _():
            for copy in side_loads[4:]:
                copy.wait()

        pair_lanes = pl.ds(pl.multiple_of(pair * PAIR, PAIR), PAIR)
        blocks = seq_len // ROWS
        wide = seq_len + ROWS
        ext_scr[:, :PAIR] = (key_ref[...].astype(jnp.float32) * 0.125).astype(jnp.bfloat16)
        ext_scr[:, PAIR:] = (seg_hot[...].astype(jnp.float32) * 0.125).astype(jnp.bfloat16)
        vt_scr[...] = jnp.transpose(value_ref[...])
        key_acc[...] = jnp.zeros_like(key_acc)
        value_acc[...] = jnp.zeros_like(value_acc)
        rel_acc[...] = jnp.zeros_like(rel_acc)
        lane = lane_ids(ROWS)
        first = lane < DH
        sums = [jnp.zeros((1, PAIR), jnp.float32) for _ in range(5)]
        for stream in range(2):
            proj_ref = (proj_c, proj_q)[stream]
            vec_ref = (vec_c, vec_q)[stream]
            gproj_ref = (gproj_c, gproj_q)[stream]
            for block in range(blocks):
                where = pl.ds(block * ROWS, ROWS)
                start = seq_len - (block + 1) * ROWS
                proj = proj_ref[where, :]
                query_ct = jnp.transpose(((proj + bias_ref[0:1, :]) * 0.125).astype(jnp.bfloat16))
                query_p = ((proj + bias_ref[1:2, :]) * 0.125).astype(jnp.bfloat16)
                query_pt = jnp.transpose(nn(flip_scr[...], query_p).astype(jnp.bfloat16))
                query_s = proj + bias_ref[2:3, :]
                hot = jnp.where(lane < 4, seg_hot[where, :].astype(jnp.float32), 0.0)
                grad = vec_grad[pl.ds(stream * seq_len + block * ROWS, ROWS), pair_lanes]
                grad_t = jnp.transpose(grad)
                inner = grad.astype(jnp.float32) * vec_ref[where, pair_lanes].astype(jnp.float32)
                window = (rel_ref[pl.ds(start, wide), :].astype(jnp.float32) * 0.125).astype(jnp.bfloat16)
                parts = []
                for head in range(2):
                    own = (lane >= DH) if head else first
                    low, high = head * DH, (head + 1) * DH
                    prob = prob_ref[stream, head, where, :]
                    grad_prob = nn(jnp.where(own, grad, jnp.zeros((), jnp.bfloat16)), vt_scr[...])
                    row_inner = jnp.sum(jnp.where(own, inner, 0.0), axis=1, keepdims=True)
                    gscore = (prob.astype(jnp.float32) * (grad_prob - row_inner)).astype(jnp.bfloat16)
                    value_acc[low:high, :] += nn(grad_t[low:high, :], prob)
                    key_acc[low:high, :] += nn(query_ct[low:high, :], gscore)
                    both = nn(gscore, ext_scr[...])
                    table = nn(flip_scr[...], gscore).astype(jnp.bfloat16)
                    table = jnp.concatenate([table, jnp.zeros((ROWS, ROWS), jnp.bfloat16)], axis=1)
                    table = pltpu.roll(table, 0, 1, stride=1, stride_axis=0)
                    gpos = nn(table, window)
                    rel_acc[low:high, start : start + wide] += nn(query_pt[low:high, :], table)
                    tail = both[:, PAIR:]
                    tail = jnp.where(lane < 4, tail, 0.0)
                    g_same = jnp.sum(tail * hot, axis=1, keepdims=True)
                    g_other = jnp.sum(tail, axis=1, keepdims=True) - g_same
                    parts.append((both[:, :PAIR], gpos, g_same, g_other))
                g_content = jnp.where(first, parts[0][0], parts[1][0])
                g_position = jnp.where(first, parts[0][1], parts[1][1]).astype(jnp.bfloat16)
                g_position = nn(flip_scr[...], g_position)
                g_same = jnp.where(first, parts[0][2], parts[1][2])
                g_other = jnp.where(first, parts[0][3], parts[1][3])
                g_segment = g_same * bias_ref[3:4, :] + g_other * bias_ref[4:5, :]
                gproj_ref[where, :PAIR] = (g_content + g_position + g_segment).astype(jnp.bfloat16)
                terms = (g_content, g_position, g_segment, g_same * query_s, g_other * query_s)
                sums = [old + jnp.sum(term, axis=0, keepdims=True) for old, term in zip(sums, terms)]
            if stream == 0:
                advance(2 * grid_at)
        gproj_c[:, PAIR : 2 * PAIR] = jnp.transpose(key_acc[...]).astype(jnp.bfloat16)
        gproj_c[:, 2 * PAIR :] = jnp.transpose(value_acc[...]).astype(jnp.bfloat16)
        triple = nn(turn_b[:, :seq_len], gproj_c[...])
        g_query = triple[:, :PAIR] + nn(turn_b[:, seq_len:], gproj_q[...])
        g_rel = nt(turn_a[...], rel_acc[...].astype(jnp.bfloat16))
        vectors = jnp.concatenate(sums, axis=0)
        piece = EARLY + late
        lanes = pl.ds(pl.multiple_of(late * PAIR, PAIR), PAIR)

        @pl.when(near)
        def _():
            swap_copy(piece).wait_send()

        work[piece, :, :PAIR] = g_query.astype(jnp.bfloat16)
        work[piece, :, PAIR : 3 * PAIR] = triple[:, PAIR:].astype(jnp.bfloat16)
        work[piece, :, 3 * PAIR :] = g_rel.astype(jnp.bfloat16)

        @pl.when(jnp.logical_not(near))
        def _():
            small_far[0:5, lanes] = vectors
            swap_copy(piece).start()

            @pl.when(turn == pairs - 2)
            def _():
                tiny_copy(0).start()

        @pl.when(near)
        def _():
            small_work[0, 0:5, lanes] = vectors
            settle(piece)

        weights = jnp.concatenate([square_w[0], square_w[1], square_w[2]], axis=1)
        total[:seq_len, :] += nt(gproj_c[...], weights)
        total[seq_len:, :] += nt(gproj_q[...], square_w[0])

    advance(2 * grid_at + 1)

    @pl.when(grid_at == last)
    def _():
        for at in range(0, total.shape[0], ROWS):
            vec_grad[at : at + ROWS, :] = total[at : at + ROWS, :].astype(jnp.bfloat16)
        begin_tick = final_slot + 1

        def finish_tick(tick, carry):
            for step in range(len(tiny_devices)):
                @pl.when(tick == begin_tick + step)
                def _():
                    tiny_copy(step).wait_recv()
                    small_work[step + 1] = small_work[step] + small_land[step]
                    if step + 1 < len(tiny_devices):
                        tiny_copy(step + 1).start()

            advance(tick)

            @pl.when(tick == begin_tick)
            def _():
                grad_copy(0).start()
                grad_copy(1).start()
                keep_copy(0).start()
                keep_copy(1).start()

            return carry

        lax.fori_loop(begin_tick, final_slot + 1 + offsets[-1], finish_tick, 0)
        small_out[...] = small_work[len(tiny_devices)]
        for step in range(len(tiny_devices)):
            tiny_copy(step).wait_send()
        for stream in range(2):
            rows_copy(stream).wait()
            grad_copy(stream).wait()
            keep_copy(stream).wait()

        def drain(piece, carry):
            for fold in range(FOLDS):
                fold_copy(fold, piece).wait_send()
                spread_copy(fold, piece).wait_send()
            store(piece).wait()
            return carry

        lax.fori_loop(0, COUNT, drain, 0)


def backward(
    dp_size, seg_hot, proj_c, proj_q, keys, values, rel_keys, lines, prob, squares,
    vec_c, vec_q, content_t, query_t, table_t, out_w, act, slope, up_w, down_w, low_rows, low_t, first_t,
    normal, scale, norms, sums, grad, rows_in,
):
    seq_len, width = proj_c.shape
    pairs = width // PAIR
    feeds = up_w.shape[1] // CHUNK
    rows = 2 * seq_len
    small_rows = 24
    more = max(1, dp_size.bit_length() - 1 - FOLDS)
    tiny = dp_size.bit_length()
    low = jnp.bfloat16
    dma = pltpu.SemaphoreType.DMA
    once = pl.Buffered(1)
    anywhere = pl.BlockSpec(memory_space=pl.ANY)
    whole = lambda g: (0, 0)

    def turn(g):
        at = jnp.maximum(g - feeds - 1, 0)
        return at // 2 + (1 - at % 2) * (pairs // 2)

    def chunk(g):
        at = jnp.minimum(g, feeds - 1)
        return (1 - at % 2) * (feeds // 2) + at // 2

    per_pair = lambda g: (0, turn(g))
    tile = pl.BlockSpec((seq_len, PAIR), per_pair)
    side = lambda g: (0, chunk(g))
    keep = lambda shape: pl.BlockSpec(shape, whole, pipeline_mode=once)
    pieces = pltpu.VMEM((COUNT, width, CHUNK), low)
    return pl.pallas_call(
        functools.partial(backward_body, dp_size),
        out_shape=(
            jax.ShapeDtypeStruct((COUNT, width, CHUNK), low),
            jax.ShapeDtypeStruct((small_rows, CHUNK), jnp.float32),
            jax.ShapeDtypeStruct((2, ROWS, width), low),
            jax.ShapeDtypeStruct((2, ROWS, width), low),
            jax.ShapeDtypeStruct((2, ROWS, width), low),
        ),
        grid_spec=pltpu.PrefetchScalarGridSpec(
            num_scalar_prefetch=0,
            grid=(feeds + 1 + pairs,),
            in_specs=[
                keep((seq_len, PAIR)),
                tile, tile, tile, tile,
                pl.BlockSpec((2 * seq_len, PAIR), per_pair),
                pl.BlockSpec((lines.shape[0], PAIR), per_pair),
                pl.BlockSpec((None, 2, 2, seq_len, seq_len), lambda g: (turn(g), 0, 0, 0, 0)),
                pl.BlockSpec((3, width, PAIR), lambda g: (0, 0, turn(g))),
                keep((seq_len, width)), keep((seq_len, width)), keep((width, width)),
                pl.BlockSpec((rows, CHUNK), side), pl.BlockSpec((rows, CHUNK), side),
                pl.BlockSpec((width, CHUNK), side), pl.BlockSpec((CHUNK, width), lambda g: (chunk(g), 0)),
                keep((rows, width)), keep((rows, 1)), keep((8, width)), keep((8, width)),
            ]
            + [anywhere] * 8,
            out_specs=[
                anywhere,
                pl.BlockSpec((small_rows, CHUNK), whole),
                anywhere, anywhere, anywhere,
            ],
            scratch_shapes=[
                pltpu.VMEM((PAIR, seq_len), low),
                pltpu.VMEM((PAIR, seq_len), jnp.float32),
                pltpu.VMEM((PAIR, seq_len), jnp.float32),
                pltpu.VMEM((PAIR, 2 * seq_len), jnp.float32),
                pltpu.VMEM((rows, width), jnp.float32),
                pltpu.VMEM((rows, width), low),
                pltpu.VMEM((rows, CHUNK), low),
                pltpu.VMEM((width, rows), low),
                pltpu.VMEM((width, rows), low),
                pltpu.VMEM((ROWS, ROWS), low),
                pieces, pieces, pieces,
                pltpu.VMEM((max(1, more - 1), COUNT if dp_size > 32 else 1, width >> FOLDS, CHUNK), low),
                pltpu.VMEM((tiny + 1, small_rows, CHUNK), jnp.float32),
                pltpu.VMEM((small_rows, CHUNK), jnp.float32),
                pltpu.VMEM((tiny, small_rows, CHUNK), jnp.float32),
                dma((COUNT,)), dma((COUNT,)), dma((COUNT,)),
                dma((FOLDS, COUNT)), dma((FOLDS, COUNT)), dma((FOLDS, COUNT)), dma((FOLDS, COUNT)),
                dma((more, COUNT)), dma((more, COUNT)), dma((tiny,)), dma((tiny,)),
                dma((7,)), dma((2,)), dma((4,)), dma((4,)),
            ],
        ),
        compiler_params=pltpu.CompilerParams(
            collective_id=0, has_side_effects=True, vmem_limit_bytes=67043328
        ),
        name="backward",
    )(
        seg_hot, proj_c, proj_q, keys, values, rel_keys, lines, prob, squares,
        vec_c, vec_q, out_w, act, slope, up_w, down_w, low_rows, scale, norms, sums,
        content_t, query_t, table_t, low_t, first_t, normal, grad, rows_in,
    )


def finish_body(
    piece_ref, rows_ref, rows_came, keep_ref, grad_came, tiny_ref,
    content_out, query_out, content_grad, query_grad, down_ref, up_ref, out_ref, query_ref, key_ref, value_ref,
    rel_ref, cbias_ref, pbias_ref, sbias_ref, embed_ref, gain1_ref, shift1_ref, ubias_ref, dbias_ref,
    gain2_ref, shift2_ref,
):
    at = pl.program_id(0)
    core = lax.axis_index("mp")
    cols = out_ref.shape[0]

    @pl.when((at < EARLY - 1) & (at % 2 == 0))
    def _():
        down_ref[...] = jnp.transpose(piece_ref[...]).astype(jnp.float32)

    @pl.when((at < EARLY - 1) & (at % 2 == 1))
    def _():
        up_ref[...] = piece_ref[...].astype(jnp.float32)

    @pl.when(at == EARLY - 1)
    def _():
        out_ref[...] = jnp.transpose(piece_ref[:, :cols]).astype(jnp.float32)

    @pl.when(at >= EARLY)
    def _():
        for turn, target in enumerate((query_ref, key_ref, value_ref, rel_ref)):
            target[...] = piece_ref[:, turn * PAIR : (turn + 1) * PAIR].astype(jnp.float32)

    @pl.when(at == 0)
    def _():
        content_out[core] = rows_ref[core]
        content_out[1 - core] = rows_came[0]
        query_out[core] = rows_ref[2 + core]
        query_out[1 - core] = rows_came[1]
        content_grad[core] = keep_ref[0]
        content_grad[1 - core] = grad_came[0]
        query_grad[core] = keep_ref[1]
        query_grad[1 - core] = grad_came[1]
        for line, target in enumerate((cbias_ref, pbias_ref, sbias_ref)):
            target[...] = tiny_ref[line : line + 1, :cols].reshape(cols)
        embed_ref[...] = tiny_ref[3:5, :cols]
        for line in range(ubias_ref.shape[0] // CHUNK):
            ubias_ref[line * CHUNK : (line + 1) * CHUNK] = tiny_ref[5 + line : 6 + line, :].reshape(CHUNK)
        for line, target in enumerate((gain1_ref, shift1_ref, gain2_ref, shift2_ref, dbias_ref)):
            for side in range(2):
                spot = 8 + 2 * line + side
                target[side * cols : (side + 1) * cols] = tiny_ref[spot : spot + 1, :cols].reshape(cols)


def finish(pieces, rows_out, rows_came, keep_rows, grad_came, tiny, half_ff):
    count, rows, chunk = pieces.shape
    cols = rows // 2
    flat = lambda size: jax.ShapeDtypeStruct((size,), jnp.float32)
    square = jax.ShapeDtypeStruct((rows, cols), jnp.float32)
    pair = jax.ShapeDtypeStruct(rows_came.shape, jnp.bfloat16)
    whole = lambda p: (0, 0)
    lead = lambda p: (0, 0, 0)
    flat_at = lambda size: pl.BlockSpec((size,), lambda p: (0,))
    once = pl.Buffered(1)
    token = pl.BlockSpec(rows_came.shape, lead)
    token_in = pl.BlockSpec(rows_came.shape, lead, pipeline_mode=once)
    at_chunk = lambda p: jnp.minimum(p // 2, half_ff // chunk - 1)
    thin = pl.BlockSpec((rows, PAIR), lambda p: (0, jnp.maximum(p - EARLY, 0)))
    return pl.pallas_call(
        finish_body,
        out_shape=(
            pair, pair, pair, pair,
            jax.ShapeDtypeStruct((half_ff, rows), jnp.float32),
            jax.ShapeDtypeStruct((rows, half_ff), jnp.float32),
            jax.ShapeDtypeStruct((cols, rows), jnp.float32),
            square, square, square, square,
            flat(cols), flat(cols), flat(cols), jax.ShapeDtypeStruct((2, cols), jnp.float32),
            flat(rows), flat(rows), flat(half_ff), flat(rows), flat(rows), flat(rows),
        ),
        grid=(count,),
        in_specs=[
            pl.BlockSpec((None, rows, chunk), lambda p: (p, 0, 0)),
            pl.BlockSpec(rows_out.shape, lead, pipeline_mode=once),
            token_in, token_in, token_in,
            pl.BlockSpec(tiny.shape, whole, pipeline_mode=once),
        ],
        out_specs=[
            token, token, token, token,
            pl.BlockSpec((chunk, rows), lambda p: (at_chunk(p), 0)),
            pl.BlockSpec((rows, chunk), lambda p: (0, at_chunk(p))),
            pl.BlockSpec((cols, rows), whole),
            thin, thin, thin, thin,
            flat_at(cols), flat_at(cols), flat_at(cols), pl.BlockSpec((2, cols), whole),
            flat_at(rows), flat_at(rows), flat_at(half_ff), flat_at(rows), flat_at(rows), flat_at(rows),
        ],
        compiler_params=pltpu.CompilerParams(vmem_limit_bytes=60 << 20),
        name="finish",
    )(pieces, rows_out, rows_came, keep_rows, grad_came, tiny)


def position_table(seq_len, width):
    distance = seq_len - 1.0 - np.arange(2 * seq_len - 1, dtype=np.float32)
    freq_exp = np.arange(0, width, 2).astype(np.float32) / np.float32(width)
    inverse = np.float32(1.0) / np.float32(10000.0) ** freq_exp
    angle = (distance[:, None] * inverse[None, :]).astype(np.float32)
    table = np.concatenate([np.sin(angle), np.cos(angle)], axis=1)
    table = np.concatenate([table, np.zeros((1, width), np.float32)], axis=0)
    return table.astype(ml_dtypes.bfloat16)


def on_device(
    dp_size,
    content_in,
    query_in,
    doc_lengths,
    order_ranks,
    segment_ids,
    target_flags,
    query_weight,
    key_weight,
    value_weight,
    out_weight,
    rel_weight,
    content_bias,
    position_bias,
    segment_bias,
    segment_embed,
    first_gain,
    first_shift,
    up_weight,
    up_bias,
    down_weight,
    down_bias,
    second_gain,
    second_shift,
    content_cot,
    query_cot,
):
    half, width = content_in.shape[1:]
    seq_len = order_ranks.shape[1]
    ff = up_weight.shape[1]
    table = position_table(seq_len, width)
    (
        vec_c, vec_q, prob, proj_c, proj_q, keys, values, rel_keys, seg_hot, content_t, query_t, lines, up_bias_use,
        content, query, cots, squares, out_use, up_use, down_use,
    ) = forward(
        content_in, query_in, content_cot, query_cot, query_weight, key_weight, value_weight, rel_weight,
        out_weight, up_weight, down_weight, doc_lengths, order_ranks, segment_ids, target_flags,
        content_bias, position_bias, segment_bias, segment_embed, up_bias, jnp.asarray(table),
    )
    first_t, normal, scale, act, slope, grad, low_rows, low_t, rows_out, sums, norms = feed_forward(
        vec_c, vec_q, content, query, cots, out_use, up_use, down_use, up_bias_use,
        (first_gain, first_shift, second_gain, second_shift, down_bias),
    )
    pieces, tiny, keep_rows, rows_came, grad_came = backward(
        dp_size, seg_hot, proj_c, proj_q, keys, values, rel_keys, lines, prob, squares,
        vec_c, vec_q, content_t, query_t, jnp.asarray(table.T), out_use, act, slope, up_use, down_use,
        low_rows, low_t, first_t, normal, scale, norms, sums, grad, rows_out,
    )
    (
        content_out, query_out, content_grad, query_grad, down_sum, up_sum, out_sum,
        query_sum, key_sum, value_sum, rel_sum, cbias_sum, pbias_sum, sbias_sum, embed_sum,
        gain1_sum, shift1_sum, ubias_sum, dbias_sum, gain2_sum, shift2_sum,
    ) = finish(pieces, rows_out.reshape(4, half, width), rows_came, keep_rows, grad_came, tiny, ff)
    return (
        content_out, query_out, content_grad, query_grad,
        query_sum, key_sum, value_sum, out_sum, rel_sum, cbias_sum, pbias_sum, sbias_sum, embed_sum,
        gain1_sum, shift1_sum, up_sum, ubias_sum, down_sum, dbias_sum, gain2_sum, shift2_sum,
    )


def solution(mesh):
    placed = (
        P("dp", "mp", None),
        P("dp", "mp", None),
        P("dp"),
        P("dp", None),
        P("dp", None),
        P("dp", None),
        P(None, "mp"),
        P(None, "mp"),
        P(None, "mp"),
        P("mp", None),
        P(None, "mp"),
        P("mp"),
        P("mp"),
        P("mp"),
        P(None, "mp"),
        P(),
        P(),
        P(None, "mp"),
        P("mp"),
        P("mp", None),
        P(),
        P(),
        P(),
        P("dp", "mp", None),
        P("dp", "mp", None),
    )
    return jax.shard_map(
        functools.partial(on_device, mesh.shape["dp"]),
        mesh=mesh,
        in_specs=placed,
        out_specs=(
            P("dp", "mp", None),
            P("dp", "mp", None),
            P("dp", "mp", None),
            P("dp", "mp", None),
            P(None, "mp"),
            P(None, "mp"),
            P(None, "mp"),
            P("mp", None),
            P(None, "mp"),
            P("mp"),
            P("mp"),
            P("mp"),
            P(None, "mp"),
            P(),
            P(),
            P(None, "mp"),
            P("mp"),
            P("mp", None),
            P(),
            P(),
            P(),
        ),
        check_vma=False,
    )
```

```python
import functools

import jax
import jax.numpy as jnp
import ml_dtypes
import numpy as np
from jax import lax
from jax.experimental import pallas as pl
from jax.experimental.pallas import tpu as pltpu
from jax.sharding import PartitionSpec as P

epsilon = 1e-06
DH = 64
PAIR = 2 * DH
ROWS = 256
NEG = -1e30
MESH = pl.DeviceIdType.MESH


def nt(left_op, right_op):
    return lax.dot_general(
        left_op, right_op, (((1,), (1,)), ((), ())), preferred_element_type=jnp.float32
    )


def nn(left_op, right_op):
    return jnp.dot(left_op, right_op, preferred_element_type=jnp.float32)


def lane_ids(rows):
    return lax.broadcasted_iota(jnp.int32, (rows, PAIR), 1)


def forward_body(
    content_in, query_in, content_cot, query_cot, query_w, key_w, value_w, rel_w, out_w, up_w, down_w,
    length_ref, order_ref, segment_ref, target_ref, cbias_ref, pbias_ref, sbias_ref, embed_ref, ubias_ref, table_ref,
    vec_c, vec_q, prob_ref, proj_c, proj_q, key_ref, value_ref, rel_ref, hot_ref, content_t, query_t, vectors_out, ubias_out,
    content_out, query_out, cots_out, square_out, out_all, up_all, down_all,
    tokens, squares, near_pack, far_pack, bounce_up, bounce_down, bounce_out, bounce_cot, mask_scr, ext_scr, rank_scr, proj_next, low_next, rel_next,
    token_sem, token_send, token_recv, square_sem, square_send, square_recv,
    bulk_load, bulk_store, bulk_send, bulk_recv, vector_send, vector_recv,
):
    step = pl.program_id(0)
    core = lax.axis_index("mp")
    seq_len = proj_c.shape[0]
    half = seq_len // 2
    cols = query_w.shape[1]
    feed = up_w.shape[1]
    blocks = seq_len // ROWS
    wide = seq_len + ROWS
    other = {"mp": 1 - core}
    mine = pl.ds(pl.multiple_of(core * half, half), half)

    def remote(source, target, send, recv):
        return pltpu.make_async_remote_copy(
            src_ref=source, dst_ref=target, send_sem=send, recv_sem=recv,
            device_id=other, device_id_type=MESH,
        )

    token_in = (content_in, query_in)
    square_in = (query_w, key_w, value_w, rel_w)
    token_load = [
        pltpu.make_async_copy(token_in[at].at[core], tokens.at[at, mine], token_sem.at[at]) for at in range(2)
    ]
    token_swap = [
        remote(token_in[at].at[1 - core], tokens.at[at, mine], token_send.at[at], token_recv.at[at])
        for at in range(2)
    ]
    square_load = [
        pltpu.make_async_copy(square_in[at], squares.at[at, :, :cols], square_sem.at[at]) for at in range(4)
    ]
    square_swap = [
        remote(square_in[at], squares.at[at, :, cols:], square_send.at[at], square_recv.at[at])
        for at in range(4)
    ]
    vector_swap = remote(near_pack, far_pack, vector_send, vector_recv)
    cot_in = (content_cot, query_cot)
    bulk_loads = [
        pltpu.make_async_copy(out_w, bounce_out, bulk_load.at[0]),
        pltpu.make_async_copy(up_w, bounce_up, bulk_load.at[1]),
        pltpu.make_async_copy(down_w, bounce_down, bulk_load.at[2]),
    ] + [
        pltpu.make_async_copy(cot_in[at].at[core], bounce_cot.at[at], bulk_load.at[3 + at]) for at in range(2)
    ]
    bulk_stores = [
        pltpu.make_async_copy(bounce_out, out_all.at[:cols], bulk_store.at[0]),
        pltpu.make_async_copy(bounce_up, up_all.at[:, :feed], bulk_store.at[1]),
        pltpu.make_async_copy(bounce_down, down_all.at[:feed], bulk_store.at[2]),
    ] + [
        pltpu.make_async_copy(bounce_cot.at[at], cots_out.at[at, mine], bulk_store.at[3 + at]) for at in range(2)
    ]
    bulk_swaps = [
        remote(out_w, out_all.at[cols:], bulk_send.at[0], bulk_recv.at[0]),
        remote(up_w, up_all.at[:, feed:], bulk_send.at[1], bulk_recv.at[1]),
        remote(down_w, down_all.at[feed:], bulk_send.at[2], bulk_recv.at[2]),
    ] + [
        remote(cot_in[at].at[1 - core], cots_out.at[at, mine], bulk_send.at[3 + at], bulk_recv.at[3 + at])
        for at in range(2)
    ]
    token_store = [
        pltpu.make_async_copy(tokens.at[at], (content_out, query_out)[at], bulk_store.at[5 + at]) for at in range(2)
    ]
    square_store = [
        pltpu.make_async_copy(squares.at[at], square_out.at[at], bulk_store.at[7 + at]) for at in range(3)
    ]

    @pl.when(step == 0)
    def _():
        for copy in token_load + square_load:
            copy.start()
        near_pack[...] = jnp.zeros_like(near_pack)
        for at, part in enumerate((cbias_ref, pbias_ref, sbias_ref)):
            near_pack[at : at + 1, :cols] = part[...].astype(jnp.float32).reshape(1, cols)
        near_pack[3:5, :cols] = embed_ref[...].astype(jnp.float32)
        near_pack[5:6, :] = ubias_ref[...].astype(jnp.float32).reshape(1, feed)
        vectors_out[:, :cols] = near_pack[:, :cols]
        ubias_out[:, :feed] = near_pack[5:6, :]
        barrier = pltpu.get_barrier_semaphore()
        pl.semaphore_signal(barrier, inc=1, device_id=other, device_id_type=MESH)
        pl.semaphore_wait(barrier, 1)
        for copy in token_swap + [vector_swap] + square_swap + bulk_swaps + bulk_loads:
            copy.start()
        place_j = lax.broadcasted_iota(jnp.int32, (1, seq_len), 1)
        ranks = order_ref[pl.ds(core, 1), :].astype(jnp.float32)
        segments = segment_ref[pl.ds(core, 1), :].astype(jnp.float32)
        targets = target_ref[pl.ds(core, 1), :].astype(jnp.float32)
        length = length_ref[core]
        live = jnp.where(place_j >= 2, targets, 0.0)
        rank_scr[...] = jnp.transpose(jnp.broadcast_to(ranks, (PAIR, seq_len)))
        lane = lane_ids(seq_len)
        seg_turn = jnp.transpose(jnp.broadcast_to(segments, (PAIR, seq_len)))
        hot = (seg_turn == (lane % 4).astype(jnp.float32)) & (lane < 8)
        hot_ref[...] = jnp.where(hot, 1.0, 0.0).astype(jnp.bfloat16)
        base = jnp.where(place_j < length, 0.0, NEG)
        for block in range(blocks):
            rows = slice(block * ROWS, (block + 1) * ROWS)
            rank_i = jnp.concatenate([rank_scr[rows, :]] * (seq_len // PAIR), axis=1)
            seen = jnp.where((live == 0.0) | (ranks < rank_i), base, NEG)
            column = lax.broadcasted_iota(jnp.int32, (ROWS, seq_len), 1)
            line = lax.broadcasted_iota(jnp.int32, (ROWS, seq_len), 0) + block * ROWS
            diagonal = column == line
            mask_scr[0, rows, :] = jnp.where(diagonal, 0.0, seen)
            mask_scr[1, rows, :] = jnp.where(diagonal, NEG, seen)
        for copy in token_load + square_load:
            copy.wait()
        for copy in token_swap:
            copy.wait_recv()
        for copy in token_store:
            copy.start()

    @pl.when(step == 1)
    def _():
        for copy in bulk_loads:
            copy.wait()
        for copy in bulk_stores:
            copy.start()
        content_t[...] = jnp.transpose(tokens[0])
        query_t[...] = jnp.transpose(tokens[1])

    @pl.when(step == pl.num_programs(0) // 2 - 1)
    def _():
        for copy in square_swap + [vector_swap]:
            copy.wait_recv()
        for copy in square_store:
            copy.start()
        vectors_out[:, cols:] = far_pack[:, :cols]
        ubias_out[:, feed:] = far_pack[5:6, :]

    pair_lanes = pl.ds(pl.multiple_of(step * PAIR, PAIR), PAIR)
    lines = vectors_out[:, pair_lanes]
    double = pl.ds(pl.multiple_of((step // 2) * 2 * PAIR, 2 * PAIR), 2 * PAIR)

    @pl.when(step % 2 == 0)
    def _():
        six_w = jnp.concatenate([squares[at, :, double] for at in range(3)], axis=1)
        for block in range(blocks):
            rows = slice(block * ROWS, (block + 1) * ROWS)
            six = nn(tokens[0, rows, :], six_w)
            proj_c[rows, :] = six[:, :PAIR]
            proj_next[0, rows, :] = six[:, PAIR : 2 * PAIR]
            key_ref[rows, :] = six[:, 2 * PAIR : 3 * PAIR].astype(jnp.bfloat16)
            low_next[0, rows, :] = six[:, 3 * PAIR : 4 * PAIR].astype(jnp.bfloat16)
            value_ref[rows, :] = six[:, 4 * PAIR : 5 * PAIR].astype(jnp.bfloat16)
            low_next[1, rows, :] = six[:, 5 * PAIR :].astype(jnp.bfloat16)
            two = nn(tokens[1, rows, :], squares[0, :, double])
            proj_q[rows, :] = two[:, :PAIR]
            proj_next[1, rows, :] = two[:, PAIR:]
        for block in range(2 * blocks):
            rows = slice(block * ROWS, (block + 1) * ROWS)
            two = nn(table_ref[rows, :], squares[3, :, double]).astype(jnp.bfloat16)
            rel_ref[rows, :] = two[:, :PAIR]
            rel_next[rows, :] = two[:, PAIR:]

    @pl.when(step % 2 == 1)
    def _():
        proj_c[...] = proj_next[0]
        proj_q[...] = proj_next[1]
        key_ref[...] = low_next[0]
        value_ref[...] = low_next[1]
        rel_ref[...] = rel_next[...]

    ext_scr[:, :PAIR] = key_ref[...]
    ext_scr[:, PAIR:] = hot_ref[...]
    lane = lane_ids(ROWS)
    diff = lines[3:4, :] - lines[4:5, :]
    zero = jnp.zeros((), jnp.bfloat16)

    def rough(stream, block, head):
        rows = pl.ds(block * ROWS, ROWS)
        own = (lane >= DH) if head else (lane < DH)
        proj = (proj_c, proj_q)[stream][rows, :]
        query_c = ((proj + lines[0:1, :]) * 0.125).astype(jnp.bfloat16)
        query_p = ((proj + lines[1:2, :]) * 0.125).astype(jnp.bfloat16)
        seg_gap = (proj + lines[2:3, :]) * (diff * 0.125)
        gap = jnp.sum(jnp.where(own, seg_gap, 0.0), axis=1, keepdims=True)
        gap_high = gap.astype(jnp.bfloat16).astype(jnp.float32)
        seg_part = jnp.where(lane < 4, gap_high, gap - gap_high) * hot_ref[rows, :].astype(jnp.float32)
        left = jnp.concatenate([jnp.where(own, query_c, zero), seg_part.astype(jnp.bfloat16)], axis=1)
        window = rel_ref[pl.ds(seq_len - (block + 1) * ROWS, wide), :]
        scores = nt(left, ext_scr[...])
        table = nt(jnp.where(own, query_p, zero), window)
        return scores, table

    def settle(stream, block, head, scores, table):
        rows = pl.ds(block * ROWS, ROWS)
        table = pltpu.roll(table, 1, 1, stride=1, stride_axis=0)
        scores = scores + table[:, ROWS:] + mask_scr[stream, rows, :]
        top = jnp.max(scores, axis=1, keepdims=True)
        terms = jnp.exp(scores - top)
        total = jnp.sum(terms, axis=1, keepdims=True)
        prob = (terms * (1.0 / total)).astype(jnp.bfloat16)
        prob_ref[stream, head, rows, :] = prob
        return nn(prob, value_ref[...])

    turns = [(stream, block, head) for stream in range(2) for block in range(blocks) for head in range(2)]
    ahead = rough(*turns[0])
    part_first = None
    for at, (stream, block, head) in enumerate(turns):
        now = ahead
        if at + 1 < len(turns):
            ahead = rough(*turns[at + 1])
        part = settle(stream, block, head, *now)
        if head == 0:
            part_first = part
        else:
            rows = pl.ds(block * ROWS, ROWS)
            (vec_c, vec_q)[stream][rows, :] = jnp.where(lane < DH, part_first, part).astype(jnp.bfloat16)

    @pl.when(step == pl.num_programs(0) - 1)
    def _():
        for copy in token_swap + square_swap + [vector_swap]:
            copy.wait_send()
        for copy in bulk_swaps:
            copy.wait()
        for copy in bulk_stores + token_store + square_store:
            copy.wait()


def forward(
    content_in, query_in, content_cot, query_cot, query_w, key_w, value_w, rel_w, out_w, up_w, down_w,
    lengths, orders, segments, targets, cbias, pbias, sbias, embed, ubias, table,
):
    once = pl.Buffered(1)
    half, width = content_in.shape[1:]
    seq_len = 2 * half
    pairs = width // PAIR
    cols = query_w.shape[1]
    feed = up_w.shape[1]
    lines = 8
    keep = lambda shape: pl.BlockSpec(shape, lambda p: (0,) * len(shape), pipeline_mode=once)
    low = jnp.bfloat16
    dma = pltpu.SemaphoreType.DMA
    whole = lambda p: (0, 0)
    anywhere = pl.BlockSpec(memory_space=pl.ANY)
    tile = pl.BlockSpec((seq_len, PAIR), lambda p: (0, p))
    low_tokens = jax.ShapeDtypeStruct((seq_len, width), low)
    turned = jax.ShapeDtypeStruct((width, seq_len), low)
    return pl.pallas_call(
        forward_body,
        out_shape=(
            low_tokens, low_tokens,
            jax.ShapeDtypeStruct((pairs, 2, 2, seq_len, seq_len), low),
            jax.ShapeDtypeStruct((seq_len, width), jnp.float32),
            jax.ShapeDtypeStruct((seq_len, width), jnp.float32),
            low_tokens, low_tokens,
            jax.ShapeDtypeStruct((2 * seq_len, width), low),
            jax.ShapeDtypeStruct((seq_len, PAIR), low),
            turned, turned,
            jax.ShapeDtypeStruct((lines, width), jnp.float32),
            jax.ShapeDtypeStruct((1, 2 * feed), jnp.float32),
            low_tokens, low_tokens,
            jax.ShapeDtypeStruct((2, seq_len, width), low),
            jax.ShapeDtypeStruct((3, width, width), low),
            jax.ShapeDtypeStruct((width, width), low),
            jax.ShapeDtypeStruct((width, 2 * feed), low),
            jax.ShapeDtypeStruct((2 * feed, width), low),
        ),
        grid_spec=pltpu.PrefetchScalarGridSpec(
            num_scalar_prefetch=0,
            grid=(pairs,),
            in_specs=[anywhere] * 11
            + [
                pl.BlockSpec(memory_space=pltpu.SMEM),
                keep(orders.shape), keep(orders.shape), keep(orders.shape),
                keep(cbias.shape), keep(cbias.shape), keep(cbias.shape), keep(embed.shape), keep(ubias.shape),
                keep((2 * seq_len, width)),
            ],
            out_specs=[
                tile, tile,
                pl.BlockSpec((None, 2, 2, seq_len, seq_len), lambda p: (p, 0, 0, 0, 0)),
                tile, tile, tile, tile,
                pl.BlockSpec((2 * seq_len, PAIR), lambda p: (0, p)),
                pl.BlockSpec((seq_len, PAIR), whole),
                pl.BlockSpec((width, seq_len), whole),
                pl.BlockSpec((width, seq_len), whole),
                pl.BlockSpec((lines, width), whole),
                pl.BlockSpec((1, 2 * feed), whole),
            ]
            + [anywhere] * 7,
            scratch_shapes=[
                pltpu.VMEM((2, seq_len, width), low),
                pltpu.VMEM((4, width, width), low),
                pltpu.VMEM((lines, feed), jnp.float32),
                pltpu.VMEM((lines, feed), jnp.float32),
                pltpu.VMEM((width, feed), low),
                pltpu.VMEM((feed, width), low),
                pltpu.VMEM((cols, width), low),
                pltpu.VMEM((2, half, width), low),
                pltpu.VMEM((2, seq_len, seq_len), jnp.float32),
                pltpu.VMEM((seq_len, 2 * PAIR), low),
                pltpu.VMEM((seq_len, PAIR), jnp.float32),
                pltpu.VMEM((2, seq_len, PAIR), jnp.float32),
                pltpu.VMEM((2, seq_len, PAIR), low),
                pltpu.VMEM((2 * seq_len, PAIR), low),
                dma((2,)), dma((2,)), dma((2,)), dma((4,)), dma((4,)), dma((4,)),
                dma((5,)), dma((10,)), dma((5,)), dma((5,)), dma, dma,
            ],
        ),
        compiler_params=pltpu.CompilerParams(
            collective_id=1, has_side_effects=True, vmem_limit_bytes=60 << 20
        ),
        name="attend_forward",
    )(
        content_in, query_in, content_cot, query_cot, query_w, key_w, value_w, rel_w, out_w, up_w, down_w,
        lengths, orders, segments, targets, cbias, pbias, sbias, embed, ubias, table,
    )


GELU_A = 0.7978845608028654
GELU_B = 0.044715


def norm_parts(value_in):
    center = value_in - jnp.mean(value_in, axis=1, keepdims=True)
    scale = lax.rsqrt(jnp.mean(center * center, axis=1, keepdims=True) + epsilon)
    return center * scale, scale


def norm_pull(normal, scale, grad):
    return scale * (
        grad
        - jnp.mean(grad, axis=1, keepdims=True)
        - normal * jnp.mean(grad * normal, axis=1, keepdims=True)
    )


def feed_forward_body(
    vec_c, vec_q, content, query, out_ref, up_ref, down_ref, up_bias,
    gain1_ref, shift1_ref, gain2_ref, shift2_ref, dbias_ref, cots_in,
    act_ref, slope_ref, scale_ref, sums_ref, norms,
    first_t_out, normal_out, grad_out, low_out, low_t_out, rows_out,
    first_scr, total_scr, cots, first_t, normal_ref, grad_ref, low_ref, low_t, rows_ref, cot_sem, out_sem,
):
    step = pl.program_id(0)
    half_rows = vec_c.shape[0]
    last = pl.num_programs(0) - 1
    cot_copy = pltpu.make_async_copy(cots_in, cots, cot_sem)

    def lines_copy(at, source, target, start):
        here = pl.ds(start, ROWS)
        return pltpu.make_async_copy(source.at[here], target.at[here], out_sem.at[at, start // ROWS])

    first_copies = [pltpu.make_async_copy(first_t, first_t_out, out_sem.at[0, 0])] + [
        lines_copy(1, normal_ref, normal_out, start) for start in range(0, 2 * half_rows, ROWS)
    ]
    late_copies = [
        [
            lines_copy(2, grad_ref, grad_out, start),
            lines_copy(3, low_ref, low_out, start),
            lines_copy(4, rows_ref, rows_out, start),
            pltpu.make_async_copy(
                low_t.at[:, pl.ds(start, ROWS)], low_t_out.at[:, pl.ds(start, ROWS)], out_sem.at[5, start // ROWS]
            ),
        ]
        for start in range(0, 2 * half_rows, ROWS)
    ]
    chunks = [(s, at) for s in range(2) for at in range(0, half_rows, ROWS)]

    @pl.when(step == 0)
    def _():
        cot_copy.start()
        norms[...] = jnp.zeros_like(norms)
        for at, part in enumerate((gain1_ref, shift1_ref, gain2_ref, shift2_ref, dbias_ref)):
            norms[at : at + 1, :] = part[...].astype(jnp.float32).reshape(1, part.shape[0])
        for stream, at in chunks:
            here = pl.ds(at, ROWS)
            there = slice(stream * half_rows + at, stream * half_rows + at + ROWS)
            mixed = nn((vec_c, vec_q)[stream][here, :], out_ref[...])
            mixed = mixed + (content, query)[stream][here, :].astype(jnp.float32)
            normal, scale = norm_parts(mixed)
            first = (normal * norms[0:1, :] + norms[1:2, :]).astype(jnp.bfloat16)
            first_scr[there, :] = first
            first_t[:, there] = jnp.transpose(first)
            normal_ref[there, :] = normal.astype(jnp.bfloat16)
            scale_ref[there, :] = scale
            total_scr[there, :] = first.astype(jnp.float32) + norms[4:5, :]
        for copy in first_copies:
            copy.start()

    for stream, at in chunks:
        there = slice(stream * half_rows + at, stream * half_rows + at + ROWS)
        value = nn(first_scr[there, :], up_ref[...]) + up_bias[...]
        square = value * value
        half = 0.5 + 0.5 * jnp.tanh(value * (GELU_A + (GELU_A * GELU_B) * square))
        wide = value * half
        act = wide.astype(jnp.bfloat16)
        slope = half + (wide * (1.0 - half)) * ((2.0 * GELU_A) + (6.0 * GELU_A * GELU_B) * square)
        act_ref[there, :] = act
        slope_ref[there, :] = slope.astype(jnp.bfloat16)
        total_scr[there, :] += nn(act, down_ref[...])

    @pl.when(step == last)
    def _():
        cot_copy.wait()
        sums = [jnp.zeros((1, content.shape[1]), jnp.float32) for _ in range(3)]
        for stream, at in chunks:
            here = pl.ds(at, ROWS)
            there = slice(stream * half_rows + at, stream * half_rows + at + ROWS)
            normal, scale = norm_parts(total_scr[there, :])
            rows_ref[there, :] = (normal * norms[2:3, :] + norms[3:4, :]).astype(jnp.bfloat16)
            cot = cots[stream, here, :].astype(jnp.float32)
            grad = norm_pull(normal, scale, cot * norms[2:3, :])
            grad_ref[there, :] = grad
            low = grad.astype(jnp.bfloat16)
            low_ref[there, :] = low
            low_t[:, there] = jnp.transpose(low)
            for at_sum, term in enumerate((cot * normal, cot, grad)):
                sums[at_sum] = sums[at_sum] + jnp.sum(term, axis=0, keepdims=True)
            for copy in late_copies[(stream * half_rows + at) // ROWS]:
                copy.start()
        sums_ref[...] = jnp.concatenate(sums + [jnp.zeros((5, content.shape[1]), jnp.float32)], axis=0)
        for copy in first_copies + sum(late_copies, []):
            copy.wait()


def feed_forward(vec_c, vec_q, content, query, cots, out_use, up_use, down_use, up_bias, vectors):
    seq_len, width = content.shape
    hidden = up_use.shape[1]
    cols = 512
    rows = 2 * seq_len
    low = jnp.bfloat16
    once = pl.Buffered(1)
    whole = lambda f: (0, 0)
    side = lambda f: (0, f)
    keep = lambda shape: pl.BlockSpec(shape, whole, pipeline_mode=once)
    stream = keep((seq_len, width))
    flat = pl.BlockSpec((width,), lambda f: (0,))
    anywhere = pl.BlockSpec(memory_space=pl.ANY)
    return pl.pallas_call(
        feed_forward_body,
        out_shape=(
            jax.ShapeDtypeStruct((rows, hidden), low),
            jax.ShapeDtypeStruct((rows, hidden), low),
            jax.ShapeDtypeStruct((rows, 1), jnp.float32),
            jax.ShapeDtypeStruct((8, width), jnp.float32),
            jax.ShapeDtypeStruct((8, width), jnp.float32),
            jax.ShapeDtypeStruct((width, rows), low),
            jax.ShapeDtypeStruct((rows, width), low),
            jax.ShapeDtypeStruct((rows, width), jnp.float32),
            jax.ShapeDtypeStruct((rows, width), low),
            jax.ShapeDtypeStruct((width, rows), low),
            jax.ShapeDtypeStruct((rows, width), low),
        ),
        grid=(hidden // cols,),
        in_specs=[
            stream, stream, stream, stream,
            keep((width, width)),
            pl.BlockSpec((width, cols), side),
            pl.BlockSpec((cols, width), lambda f: (f, 0)),
            pl.BlockSpec((1, cols), side),
            flat, flat, flat, flat, flat,
            anywhere,
        ],
        out_specs=[
            pl.BlockSpec((rows, cols), side),
            pl.BlockSpec((rows, cols), side),
            pl.BlockSpec((rows, 1), whole),
            pl.BlockSpec((8, width), whole),
            pl.BlockSpec((8, width), whole),
        ]
        + [anywhere] * 6,
        scratch_shapes=[
            pltpu.VMEM((rows, width), low),
            pltpu.VMEM((rows, width), jnp.float32),
            pltpu.VMEM(cots.shape, low),
            pltpu.VMEM((width, rows), low),
            pltpu.VMEM((rows, width), low),
            pltpu.VMEM((rows, width), jnp.float32),
            pltpu.VMEM((rows, width), low),
            pltpu.VMEM((width, rows), low),
            pltpu.VMEM((rows, width), low),
            pltpu.SemaphoreType.DMA,
            pltpu.SemaphoreType.DMA((6, rows // ROWS)),
        ],
        compiler_params=pltpu.CompilerParams(vmem_limit_bytes=60 << 20),
        name="feed_forward",
    )(vec_c, vec_q, content, query, out_use, up_use, down_use, up_bias, *vectors, cots)


FOLDS = 4
EARLY = 7
COUNT = 10
CHUNK = 512


def backward_body(dp_size, *refs):
    (
        seg_hot, proj_c, proj_q, key_ref, value_ref, rel_ref, bias_ref, prob_ref,
        square_w, act_ref, slope_ref, up_ref, down_ref, low_ref, scale_ref, norms, sums_in,
        content_t, query_t, table_t, low_t, first_t, normal_in, grad_in, rows_in, vec_c_in, vec_q_in, out_in,
        sum_out, small_out, keep_out, rows_came, grad_came,
        vt_scr, key_acc, value_acc, rel_acc, total, vec_grad, hid_scr, turn_a, turn_b, flip_scr, vec_c, vec_q, out_w,
        work, swapped, landed, extra, small_work, small_far, small_land,
        store_sem, swap_send, swap_recv, fold_send, fold_recv, spread_send, spread_recv,
        more_send, more_recv, tiny_send, tiny_recv, side_sem, keep_sem, back_send, back_recv,
    ) = refs
    seq_len = key_ref.shape[0]
    gproj_c = hid_scr.at[:seq_len, : 3 * PAIR]
    gproj_q = hid_scr.at[seq_len:, :PAIR]
    ext_scr = hid_scr.at[seq_len:, PAIR : 3 * PAIR]
    grid_at = pl.program_id(0)
    feeds = 6
    pairs = 6
    half_pairs = pairs // 2
    last = pl.num_programs(0) - 1
    rows, width = total.shape[1], work.shape[2]
    cols = rows // 2
    place = lax.axis_index("dp")
    core = lax.axis_index("mp")
    strides = [1 + core, 2 - core, 4, 8]
    more = [16 << step for step in range(8) if (16 << step) < dp_size]
    bits = [(place // stride) % 2 for stride in strides]
    partners = [place + (1 - 2 * bit) * stride for bit, stride in zip(bits, strides)]
    more_partners = [place + (1 - 2 * ((place // stride) % 2)) * stride for stride in more]
    lengths = [rows >> (fold + 1) for fold in range(FOLDS)]
    starts, begin = [], 0
    for bit, length in zip(bits, lengths):
        begin = begin + bit * length
        starts.append(begin)
    land_at = [rows - 2 * length for length in lengths]
    offsets = [0, 3, 6, 8, 10, 12, 14, 16, 19]
    final_slot = 25

    def kept(fold):
        return pl.ds(pl.multiple_of(starts[fold], 16), lengths[fold])

    def given(fold):
        return pl.ds(pl.multiple_of(starts[fold] + (1 - 2 * bits[fold]) * lengths[fold], 16), lengths[fold])

    def remote(source, target, send, recv, device):
        return pltpu.make_async_remote_copy(
            src_ref=source, dst_ref=target, send_sem=send, recv_sem=recv,
            device_id=device, device_id_type=MESH,
        )

    def swap_copy(piece):
        return remote(
            work.at[piece], swapped.at[piece], swap_send.at[piece], swap_recv.at[piece], {"mp": 1 - core}
        )

    def fold_copy(fold, piece):
        return remote(
            work.at[piece, given(fold)],
            landed.at[piece, pl.ds(land_at[fold], lengths[fold])],
            fold_send.at[fold, piece], fold_recv.at[fold, piece], {"dp": partners[fold]},
        )

    def spread_copy(fold, piece):
        return remote(
            swapped.at[piece, kept(fold)],
            swapped.at[piece, kept(fold)],
            spread_send.at[fold, piece], spread_recv.at[fold, piece], {"dp": partners[fold]},
        )

    def extra_ref(step, piece):
        if step == 0:
            return landed.at[piece, pl.ds(rows - lengths[-1], lengths[-1])]
        return extra.at[step - 1, piece]

    def more_copy(step, piece):
        return remote(
            work.at[piece, kept(FOLDS - 1)],
            extra_ref(step, piece),
            more_send.at[step, piece], more_recv.at[step, piece], {"dp": more_partners[step]},
        )

    def store(piece):
        return pltpu.make_async_copy(swapped.at[piece], sum_out.at[piece], store_sem.at[piece])

    def add_rows(piece, where, other):
        mine = work[piece, where, :].astype(jnp.float32)
        work[piece, where, :] = (mine + other.astype(jnp.float32)).astype(jnp.bfloat16)

    tiny_devices = [{"mp": 1 - core}] + [{"dp": partner} for partner in partners + more_partners]

    def tiny_copy(step):
        return remote(
            small_far if step == 0 else small_work.at[step],
            small_land.at[step], tiny_send.at[step], tiny_recv.at[step], tiny_devices[step],
        )

    far_rows = (1 - core) * ROWS

    def rows_copy(stream):
        return remote(
            rows_in.at[pl.ds(pl.multiple_of(stream * seq_len + far_rows, ROWS), ROWS)], rows_came.at[stream],
            back_send.at[stream], back_recv.at[stream], {"mp": 1 - core},
        )

    def grad_copy(stream):
        return remote(
            vec_grad.at[pl.ds(pl.multiple_of(stream * seq_len + far_rows, ROWS), ROWS)], grad_came.at[stream],
            back_send.at[2 + stream], back_recv.at[2 + stream], {"mp": 1 - core},
        )

    def keep_copy(stream):
        return pltpu.make_async_copy(
            vec_grad.at[pl.ds(pl.multiple_of(stream * seq_len + core * ROWS, ROWS), ROWS)],
            keep_out.at[stream], keep_sem.at[stream],
        )

    side_loads = [
        pltpu.make_async_copy(source, target, side_sem.at[at])
        for at, (source, target) in enumerate(
            (
                (grad_in, total),
                (first_t, turn_a),
                (low_t, turn_b),
                (normal_in, vec_grad),
                (table_t, turn_a),
                (content_t, turn_b.at[:, :seq_len]),
                (query_t, turn_b.at[:, seq_len:]),
                (vec_c_in, vec_c),
                (vec_q_in, vec_q),
                (out_in, out_w),
            )
        )
    ]

    def stage(number, piece):
        if number == 0:
            fold_copy(0, piece).start()
        elif number <= FOLDS:
            fold = number - 1
            fold_copy(fold, piece).wait_recv()
            add_rows(piece, kept(fold), landed[piece, pl.ds(land_at[fold], lengths[fold]), :])
            if fold + 1 < FOLDS:
                fold_copy(fold + 1, piece).start()
                return
            for step in range(len(more)):
                more_copy(step, piece).start()
                more_copy(step, piece).wait()
                add_rows(piece, kept(fold), extra_ref(step, piece)[...])
            swapped[piece, kept(fold), :] = work[piece, kept(fold), :]
            spread_copy(fold, piece).start()
        else:
            fold = 2 * FOLDS - number
            remote(
                swapped.at[piece, kept(fold)], swapped.at[piece, given(fold)],
                spread_send.at[fold, piece], spread_recv.at[fold, piece], {"dp": partners[fold]},
            ).wait_recv()
            if fold > 0:
                spread_copy(fold - 1, piece).start()
            else:
                store(piece).start()

    def advance(tick):
        for number in reversed(range(2 * FOLDS + 1)):
            slot = tick - offsets[number]
            early = (slot == 2) | (slot == 3) | (slot == 6) | (slot == 7) | (slot == 10) | (slot == 11)
            late = (slot == 13) | (slot == 17) | (slot == 21) | (slot == final_slot)
            piece = jnp.where(slot < 13, 2 * ((slot - 2) // 4) + (slot - 2) % 4, EARLY - 1 + (slot - 13) // 4)

            @pl.when(early | late)
            def _():
                stage(number, piece)

    def settle(piece):
        swap_copy(piece).wait_recv()
        add_rows(piece, pl.ds(0, rows), swapped[piece])

    @pl.when(grid_at == 0)
    def _():
        barrier = pltpu.get_barrier_semaphore()
        for device in tiny_devices:
            pl.semaphore_signal(barrier, inc=1, device_id=device, device_id_type=MESH)
        pl.semaphore_wait(barrier, len(tiny_devices))
        for at in (2, 0, 1, 3, 7, 8, 9):
            side_loads[at].start()
        rows_copy(0).start()
        rows_copy(1).start()
        small_work[0] = jnp.zeros_like(small_work[0])
        small_far[...] = jnp.zeros_like(small_far)
        for at in range(3):
            for side in range(2):
                line = sums_in[at : at + 1, side * cols : (side + 1) * cols]
                spot = slice(12 + 2 * at + side, 13 + 2 * at + side)
                small_work[0, spot, :cols] = line
                small_far[spot, :cols] = line
        line_at = lax.broadcasted_iota(jnp.int32, (ROWS, ROWS), 0)
        lane_at = lax.broadcasted_iota(jnp.int32, (ROWS, ROWS), 1)
        flip_scr[...] = jnp.where(line_at + lane_at == ROWS - 1, 1.0, 0.0).astype(jnp.bfloat16)

    @pl.when(grid_at < feeds)
    def _():
        chunk = grid_at // 2
        near = grid_at % 2 == 1
        bias_sum = jnp.zeros((1, width), jnp.float32)

        @pl.when(near)
        def _():
            swap_copy(2 * chunk).wait_send()

        @pl.when(grid_at == 0)
        def _():
            side_loads[2].wait()

        for at in range(0, rows, ROWS):
            here = slice(at, at + ROWS)
            work[2 * chunk, here, :] = nn(turn_b[here, :], act_ref[...]).astype(jnp.bfloat16)

        @pl.when(near)
        def _():
            settle(2 * chunk)

        @pl.when(jnp.logical_not(near))
        def _():
            swap_copy(2 * chunk).start()

        @pl.when(grid_at == 0)
        def _():
            side_loads[0].wait()
            side_loads[1].wait()

        advance(2 * grid_at)
        for at in range(0, total.shape[0], ROWS):
            here = slice(at, at + ROWS)
            grad_act = nt(low_ref[here, :], down_ref[...])
            hid = (grad_act * slope_ref[here, :].astype(jnp.float32)).astype(jnp.bfloat16)
            hid_scr[here, :] = hid
            bias_sum = bias_sum + jnp.sum(hid.astype(jnp.float32), axis=0, keepdims=True)
            total[here, :] += nt(hid, up_ref[...])

        @pl.when(near)
        def _():
            swap_copy(2 * chunk + 1).wait_send()

        for at in range(0, rows, ROWS):
            here = slice(at, at + ROWS)
            work[2 * chunk + 1, here, :] = nn(turn_a[here, :], hid_scr[...]).astype(jnp.bfloat16)

        @pl.when(near)
        def _():
            small_work[0, pl.ds(5 + chunk, 1), :] = bias_sum
            settle(2 * chunk + 1)

        @pl.when(jnp.logical_not(near))
        def _():
            small_far[pl.ds(5 + chunk, 1), :] = bias_sum
            swap_copy(2 * chunk + 1).start()

    @pl.when(grid_at == feeds)
    def _():
        advance(2 * grid_at)
        for copy in side_loads[4:7]:
            copy.start()
        for at in (3, 7, 8, 9):
            side_loads[at].wait()
        sums = [jnp.zeros((1, rows), jnp.float32) for _ in range(2)]
        out_piece = EARLY - 1
        near_sum = jnp.zeros((rows, cols), jnp.float32)
        far_sum = jnp.zeros((rows, cols), jnp.float32)
        for at in range(0, total.shape[0], ROWS):
            here = slice(at, at + ROWS)
            normal = vec_grad[here, :].astype(jnp.float32)
            grad = total[here, :]
            sums[0] = sums[0] + jnp.sum(grad * normal, axis=0, keepdims=True)
            sums[1] = sums[1] + jnp.sum(grad, axis=0, keepdims=True)
            grad = norm_pull(normal, scale_ref[here, :], grad * norms[0:1, :])
            total[here, :] = grad
            vec_grad[here, :] = grad.astype(jnp.bfloat16)
        for at in range(0, total.shape[0], ROWS):
            here = slice(at, at + ROWS)
            low = vec_grad[here, :]
            low_turn = jnp.transpose(low)
            vec = (vec_c, vec_q)[at // seq_len][at % seq_len : at % seq_len + ROWS, :]
            far_sum = far_sum + nn(low_turn, vec[:, cols:])
            near_sum = near_sum + nn(low_turn, vec[:, :cols])
            vec_grad[here, :] = nt(low, out_w[...]).astype(jnp.bfloat16)
        work[out_piece, :, :cols] = far_sum.astype(jnp.bfloat16)
        work[out_piece, :, cols:] = jnp.zeros((rows, width - cols), jnp.bfloat16)
        swap_copy(out_piece).start()
        for at in range(2):
            for side in range(2):
                line = sums[at][:, side * cols : (side + 1) * cols]
                spot = slice(8 + 2 * at + side, 9 + 2 * at + side)
                small_work[0, spot, :cols] = line
                small_far[spot, :cols] = line
        swap_copy(out_piece).wait()
        near_sum = near_sum + swapped[out_piece, :, :cols].astype(jnp.float32)
        work[out_piece, :, :cols] = near_sum.astype(jnp.bfloat16)

    @pl.when(grid_at > feeds)
    def _():
        turn = grid_at - feeds - 1
        late = turn // 2
        near = turn % 2 == 1
        pair = late + (1 - turn % 2) * half_pairs

        @pl.when(turn == 0)
        def _():
            for copy in side_loads[4:7]:
                copy.wait()

        pair_lanes = pl.ds(pl.multiple_of(pair * PAIR, PAIR), PAIR)
        blocks = seq_len // ROWS
        wide = seq_len + ROWS
        ext_scr[:, :PAIR] = (key_ref[...].astype(jnp.float32) * 0.125).astype(jnp.bfloat16)
        ext_scr[:, PAIR:] = (seg_hot[...].astype(jnp.float32) * 0.125).astype(jnp.bfloat16)
        vt_scr[...] = jnp.transpose(value_ref[...])
        key_acc[...] = jnp.zeros_like(key_acc)
        value_acc[...] = jnp.zeros_like(value_acc)
        rel_acc[...] = jnp.zeros_like(rel_acc)
        lane = lane_ids(ROWS)
        first = lane < DH
        sums = [jnp.zeros((1, PAIR), jnp.float32) for _ in range(5)]
        for stream in range(2):
            proj_ref = (proj_c, proj_q)[stream]
            vec_ref = (vec_c, vec_q)[stream]
            gproj_ref = (gproj_c, gproj_q)[stream]
            for block in range(blocks):
                where = pl.ds(block * ROWS, ROWS)
                start = seq_len - (block + 1) * ROWS
                proj = proj_ref[where, :]
                query_ct = jnp.transpose(((proj + bias_ref[0:1, :]) * 0.125).astype(jnp.bfloat16))
                query_p = ((proj + bias_ref[1:2, :]) * 0.125).astype(jnp.bfloat16)
                query_pt = jnp.transpose(nn(flip_scr[...], query_p).astype(jnp.bfloat16))
                query_s = proj + bias_ref[2:3, :]
                hot = jnp.where(lane < 4, seg_hot[where, :].astype(jnp.float32), 0.0)
                grad = vec_grad[pl.ds(stream * seq_len + block * ROWS, ROWS), pair_lanes]
                grad_t = jnp.transpose(grad)
                inner = grad.astype(jnp.float32) * vec_ref[where, pair_lanes].astype(jnp.float32)
                window = (rel_ref[pl.ds(start, wide), :].astype(jnp.float32) * 0.125).astype(jnp.bfloat16)
                parts = []
                for head in range(2):
                    own = (lane >= DH) if head else first
                    low, high = head * DH, (head + 1) * DH
                    prob = prob_ref[stream, head, where, :]
                    grad_prob = nn(jnp.where(own, grad, jnp.zeros((), jnp.bfloat16)), vt_scr[...])
                    row_inner = jnp.sum(jnp.where(own, inner, 0.0), axis=1, keepdims=True)
                    gscore = (prob.astype(jnp.float32) * (grad_prob - row_inner)).astype(jnp.bfloat16)
                    value_acc[low:high, :] += nn(grad_t[low:high, :], prob)
                    key_acc[low:high, :] += nn(query_ct[low:high, :], gscore)
                    both = nn(gscore, ext_scr[...])
                    table = nn(flip_scr[...], gscore).astype(jnp.bfloat16)
                    table = jnp.concatenate([table, jnp.zeros((ROWS, ROWS), jnp.bfloat16)], axis=1)
                    table = pltpu.roll(table, 0, 1, stride=1, stride_axis=0)
                    gpos = nn(table, window)
                    rel_acc[low:high, start : start + wide] += nn(query_pt[low:high, :], table)
                    tail = both[:, PAIR:]
                    tail = jnp.where(lane < 4, tail, 0.0)
                    g_same = jnp.sum(tail * hot, axis=1, keepdims=True)
                    g_other = jnp.sum(tail, axis=1, keepdims=True) - g_same
                    parts.append((both[:, :PAIR], gpos, g_same, g_other))
                g_content = jnp.where(first, parts[0][0], parts[1][0])
                g_position = jnp.where(first, parts[0][1], parts[1][1]).astype(jnp.bfloat16)
                g_position = nn(flip_scr[...], g_position)
                g_same = jnp.where(first, parts[0][2], parts[1][2])
                g_other = jnp.where(first, parts[0][3], parts[1][3])
                g_segment = g_same * bias_ref[3:4, :] + g_other * bias_ref[4:5, :]
                gproj_ref[where, :PAIR] = (g_content + g_position + g_segment).astype(jnp.bfloat16)
                terms = (g_content, g_position, g_segment, g_same * query_s, g_other * query_s)
                sums = [old + jnp.sum(term, axis=0, keepdims=True) for old, term in zip(sums, terms)]
            if stream == 0:
                advance(2 * grid_at)
        gproj_c[:, PAIR : 2 * PAIR] = jnp.transpose(key_acc[...]).astype(jnp.bfloat16)
        gproj_c[:, 2 * PAIR :] = jnp.transpose(value_acc[...]).astype(jnp.bfloat16)
        triple = nn(turn_b[:, :seq_len], gproj_c[...])
        g_query = triple[:, :PAIR] + nn(turn_b[:, seq_len:], gproj_q[...])
        g_rel = nt(turn_a[...], rel_acc[...].astype(jnp.bfloat16))
        vectors = jnp.concatenate(sums, axis=0)
        piece = EARLY + late
        lanes = pl.ds(pl.multiple_of(late * PAIR, PAIR), PAIR)

        @pl.when(near)
        def _():
            swap_copy(piece).wait_send()

        work[piece, :, :PAIR] = g_query.astype(jnp.bfloat16)
        work[piece, :, PAIR : 3 * PAIR] = triple[:, PAIR:].astype(jnp.bfloat16)
        work[piece, :, 3 * PAIR :] = g_rel.astype(jnp.bfloat16)

        @pl.when(jnp.logical_not(near))
        def _():
            small_far[0:5, lanes] = vectors
            swap_copy(piece).start()

            @pl.when(turn == pairs - 2)
            def _():
                tiny_copy(0).start()

        @pl.when(near)
        def _():
            small_work[0, 0:5, lanes] = vectors
            settle(piece)

    advance(2 * grid_at + 1)

    @pl.when(grid_at > feeds)
    def _():
        weights = jnp.concatenate([square_w[0], square_w[1], square_w[2]], axis=1)
        total[:seq_len, :] += nt(gproj_c[...], weights)
        total[seq_len:, :] += nt(gproj_q[...], square_w[0])

    @pl.when(grid_at == last)
    def _():
        for at in range(0, total.shape[0], ROWS):
            vec_grad[at : at + ROWS, :] = total[at : at + ROWS, :].astype(jnp.bfloat16)
        begin_tick = final_slot + 1

        def finish_tick(tick, carry):
            for step in range(len(tiny_devices)):
                @pl.when(tick == begin_tick + step)
                def _():
                    tiny_copy(step).wait_recv()
                    small_work[step + 1] = small_work[step] + small_land[step]
                    if step + 1 < len(tiny_devices):
                        tiny_copy(step + 1).start()

            advance(tick)

            @pl.when(tick == begin_tick)
            def _():
                grad_copy(0).start()
                grad_copy(1).start()
                keep_copy(0).start()
                keep_copy(1).start()

            return carry

        lax.fori_loop(begin_tick, final_slot + 1 + offsets[-1], finish_tick, 0)
        small_out[...] = small_work[len(tiny_devices)]
        for step in range(len(tiny_devices)):
            tiny_copy(step).wait_send()
        for stream in range(2):
            rows_copy(stream).wait()
            grad_copy(stream).wait()
            keep_copy(stream).wait()

        def drain(piece, carry):
            for fold in range(FOLDS):
                fold_copy(fold, piece).wait_send()
                spread_copy(fold, piece).wait_send()
            store(piece).wait()
            return carry

        lax.fori_loop(0, COUNT, drain, 0)


def backward(
    dp_size, seg_hot, proj_c, proj_q, keys, values, rel_keys, lines, prob, squares,
    vec_c, vec_q, content_t, query_t, table_t, out_w, act, slope, up_w, down_w, low_rows, low_t, first_t,
    normal, scale, norms, sums, grad, rows_in,
):
    seq_len, width = proj_c.shape
    pairs = width // PAIR
    feeds = up_w.shape[1] // CHUNK
    rows = 2 * seq_len
    small_rows = 24
    more = max(1, dp_size.bit_length() - 1 - FOLDS)
    tiny = dp_size.bit_length()
    low = jnp.bfloat16
    dma = pltpu.SemaphoreType.DMA
    once = pl.Buffered(1)
    anywhere = pl.BlockSpec(memory_space=pl.ANY)
    whole = lambda g: (0, 0)

    def turn(g):
        at = jnp.maximum(g - feeds - 1, 0)
        return at // 2 + (1 - at % 2) * (pairs // 2)

    def chunk(g):
        at = jnp.minimum(g, feeds - 1)
        return (1 - at % 2) * (feeds // 2) + at // 2

    per_pair = lambda g: (0, turn(g))
    tile = pl.BlockSpec((seq_len, PAIR), per_pair)
    side = lambda g: (0, chunk(g))
    keep = lambda shape: pl.BlockSpec(shape, whole, pipeline_mode=once)
    pieces = pltpu.VMEM((COUNT, width, CHUNK), low)
    return pl.pallas_call(
        functools.partial(backward_body, dp_size),
        out_shape=(
            jax.ShapeDtypeStruct((COUNT, width, CHUNK), low),
            jax.ShapeDtypeStruct((small_rows, CHUNK), jnp.float32),
            jax.ShapeDtypeStruct((2, ROWS, width), low),
            jax.ShapeDtypeStruct((2, ROWS, width), low),
            jax.ShapeDtypeStruct((2, ROWS, width), low),
        ),
        grid_spec=pltpu.PrefetchScalarGridSpec(
            num_scalar_prefetch=0,
            grid=(feeds + 1 + pairs,),
            in_specs=[
                keep((seq_len, PAIR)),
                tile, tile, tile, tile,
                pl.BlockSpec((2 * seq_len, PAIR), per_pair),
                pl.BlockSpec((lines.shape[0], PAIR), per_pair),
                pl.BlockSpec((None, 2, 2, seq_len, seq_len), lambda g: (turn(g), 0, 0, 0, 0)),
                pl.BlockSpec((3, width, PAIR), lambda g: (0, 0, turn(g))),
                pl.BlockSpec((rows, CHUNK), side), pl.BlockSpec((rows, CHUNK), side),
                pl.BlockSpec((width, CHUNK), side), pl.BlockSpec((CHUNK, width), lambda g: (chunk(g), 0)),
                keep((rows, width)), keep((rows, 1)), keep((8, width)), keep((8, width)),
            ]
            + [anywhere] * 11,
            out_specs=[
                anywhere,
                pl.BlockSpec((small_rows, CHUNK), whole),
                anywhere, anywhere, anywhere,
            ],
            scratch_shapes=[
                pltpu.VMEM((PAIR, seq_len), low),
                pltpu.VMEM((PAIR, seq_len), jnp.float32),
                pltpu.VMEM((PAIR, seq_len), jnp.float32),
                pltpu.VMEM((PAIR, 2 * seq_len), jnp.float32),
                pltpu.VMEM((rows, width), jnp.float32),
                pltpu.VMEM((rows, width), low),
                pltpu.VMEM((rows, CHUNK), low),
                pltpu.VMEM((width, rows), low),
                pltpu.VMEM((width, rows), low),
                pltpu.VMEM((ROWS, ROWS), low),
                pltpu.VMEM((seq_len, width), low),
                pltpu.VMEM((seq_len, width), low),
                pltpu.VMEM((width, width), low),
                pieces, pieces, pieces,
                pltpu.VMEM((max(1, more - 1), COUNT if dp_size > 32 else 1, width >> FOLDS, CHUNK), low),
                pltpu.VMEM((tiny + 1, small_rows, CHUNK), jnp.float32),
                pltpu.VMEM((small_rows, CHUNK), jnp.float32),
                pltpu.VMEM((tiny, small_rows, CHUNK), jnp.float32),
                dma((COUNT,)), dma((COUNT,)), dma((COUNT,)),
                dma((FOLDS, COUNT)), dma((FOLDS, COUNT)), dma((FOLDS, COUNT)), dma((FOLDS, COUNT)),
                dma((more, COUNT)), dma((more, COUNT)), dma((tiny,)), dma((tiny,)),
                dma((10,)), dma((2,)), dma((4,)), dma((4,)),
            ],
        ),
        compiler_params=pltpu.CompilerParams(
            collective_id=0, has_side_effects=True, vmem_limit_bytes=67043328
        ),
        name="backward",
    )(
        seg_hot, proj_c, proj_q, keys, values, rel_keys, lines, prob, squares,
        act, slope, up_w, down_w, low_rows, scale, norms, sums,
        content_t, query_t, table_t, low_t, first_t, normal, grad, rows_in, vec_c, vec_q, out_w,
    )


def finish_body(
    piece_ref, tiny_ref, rows_in, came_in, keep_in, grad_in,
    down_ref, up_ref, out_ref, cbias_ref, pbias_ref, sbias_ref, embed_ref, gain1_ref, shift1_ref, ubias_ref,
    dbias_ref, gain2_ref, shift2_ref,
    content_out, query_out, content_grad, query_grad, query_out_w, key_out_w, value_out_w, rel_out_w,
    tokens, squares, load_sem, store_sem,
):
    at = pl.program_id(0)
    core = lax.axis_index("mp")
    cols = out_ref.shape[0]
    late = COUNT - EARLY
    sources = (
        (rows_in.at[core], came_in.at[0]),
        (rows_in.at[2 + core], came_in.at[1]),
        (keep_in.at[0], grad_in.at[0]),
        (keep_in.at[1], grad_in.at[1]),
    )
    loads = [
        pltpu.make_async_copy(source, tokens.at[index, side], load_sem.at[index, side])
        for index, pair in enumerate(sources)
        for side, source in enumerate(pair)
    ]
    stores = [
        pltpu.make_async_copy(
            tokens.at[index, side], target.at[core if side == 0 else 1 - core], store_sem.at[index, side]
        )
        for index, target in enumerate((content_out, query_out, content_grad, query_grad))
        for side in range(2)
    ]
    square_stores = [
        pltpu.make_async_copy(squares.at[index], target, store_sem.at[index, 2])
        for index, target in enumerate((query_out_w, key_out_w, value_out_w, rel_out_w))
    ]

    @pl.when(at == 0)
    def _():
        for copy in loads:
            copy.start()

    for turn in range(late):
        lanes = slice(turn * PAIR, (turn + 1) * PAIR)

        @pl.when(at == turn)
        def _():
            for index in range(4):
                part = piece_ref[:, index * PAIR : (index + 1) * PAIR]
                squares[index, :, lanes] = part.astype(jnp.float32)

    @pl.when(at == late - 1)
    def _():
        for copy in square_stores:
            copy.start()
        for copy in loads:
            copy.wait()
        for copy in stores:
            copy.start()

    early = at - late

    @pl.when((early >= 0) & (early < EARLY - 1) & (early % 2 == 0))
    def _():
        down_ref[...] = jnp.transpose(piece_ref[...]).astype(jnp.float32)

    @pl.when((early >= 0) & (early < EARLY - 1) & (early % 2 == 1))
    def _():
        up_ref[...] = piece_ref[...].astype(jnp.float32)

    @pl.when(early == EARLY - 1)
    def _():
        out_ref[...] = jnp.transpose(piece_ref[:, :cols]).astype(jnp.float32)
        for copy in stores + square_stores:
            copy.wait()

    @pl.when(at == 0)
    def _():
        for line, target in enumerate((cbias_ref, pbias_ref, sbias_ref)):
            target[...] = tiny_ref[line : line + 1, :cols].reshape(cols)
        embed_ref[...] = tiny_ref[3:5, :cols]
        for line in range(ubias_ref.shape[0] // CHUNK):
            ubias_ref[line * CHUNK : (line + 1) * CHUNK] = tiny_ref[5 + line : 6 + line, :].reshape(CHUNK)
        for line, target in enumerate((gain1_ref, shift1_ref, gain2_ref, shift2_ref, dbias_ref)):
            for side in range(2):
                spot = 8 + 2 * line + side
                target[side * cols : (side + 1) * cols] = tiny_ref[spot : spot + 1, :cols].reshape(cols)


def finish(pieces, rows_out, rows_came, keep_rows, grad_came, tiny, half_ff):
    count, rows, chunk = pieces.shape
    cols = rows // 2
    late = COUNT - EARLY
    flat = lambda size: jax.ShapeDtypeStruct((size,), jnp.float32)
    square = jax.ShapeDtypeStruct((rows, cols), jnp.float32)
    pair = jax.ShapeDtypeStruct(rows_came.shape, jnp.bfloat16)
    whole = lambda p: (0, 0)
    flat_at = lambda size: pl.BlockSpec((size,), lambda p: (0,))
    anywhere = pl.BlockSpec(memory_space=pl.ANY)
    at_chunk = lambda p: jnp.clip((p - late) // 2, 0, half_ff // chunk - 1)
    results = pl.pallas_call(
        finish_body,
        out_shape=(
            jax.ShapeDtypeStruct((half_ff, rows), jnp.float32),
            jax.ShapeDtypeStruct((rows, half_ff), jnp.float32),
            jax.ShapeDtypeStruct((cols, rows), jnp.float32),
            flat(cols), flat(cols), flat(cols), jax.ShapeDtypeStruct((2, cols), jnp.float32),
            flat(rows), flat(rows), flat(half_ff), flat(rows), flat(rows), flat(rows),
            pair, pair, pair, pair, square, square, square, square,
        ),
        grid=(count,),
        in_specs=[
            pl.BlockSpec((None, rows, chunk), lambda p: ((p + EARLY) % COUNT, 0, 0)),
            pl.BlockSpec(tiny.shape, whole, pipeline_mode=pl.Buffered(1)),
            anywhere, anywhere, anywhere, anywhere,
        ],
        out_specs=[
            pl.BlockSpec((chunk, rows), lambda p: (at_chunk(p), 0)),
            pl.BlockSpec((rows, chunk), lambda p: (0, at_chunk(p))),
            pl.BlockSpec((cols, rows), whole),
            flat_at(cols), flat_at(cols), flat_at(cols), pl.BlockSpec((2, cols), whole),
            flat_at(rows), flat_at(rows), flat_at(half_ff), flat_at(rows), flat_at(rows), flat_at(rows),
        ]
        + [anywhere] * 8,
        scratch_shapes=[
            pltpu.VMEM((4,) + rows_came.shape, jnp.bfloat16),
            pltpu.VMEM((4, rows, cols), jnp.float32),
            pltpu.SemaphoreType.DMA((4, 2)),
            pltpu.SemaphoreType.DMA((4, 3)),
        ],
        compiler_params=pltpu.CompilerParams(vmem_limit_bytes=60 << 20),
        name="finish",
    )(pieces, tiny, rows_out, rows_came, keep_rows, grad_came)
    return results[13:17] + results[:3] + results[17:21] + results[3:13]


def position_table(seq_len, width):
    distance = seq_len - 1.0 - np.arange(2 * seq_len - 1, dtype=np.float32)
    freq_exp = np.arange(0, width, 2).astype(np.float32) / np.float32(width)
    inverse = np.float32(1.0) / np.float32(10000.0) ** freq_exp
    angle = (distance[:, None] * inverse[None, :]).astype(np.float32)
    table = np.concatenate([np.sin(angle), np.cos(angle)], axis=1)
    table = np.concatenate([table, np.zeros((1, width), np.float32)], axis=0)
    return table.astype(ml_dtypes.bfloat16)


def on_device(
    dp_size,
    content_in,
    query_in,
    doc_lengths,
    order_ranks,
    segment_ids,
    target_flags,
    query_weight,
    key_weight,
    value_weight,
    out_weight,
    rel_weight,
    content_bias,
    position_bias,
    segment_bias,
    segment_embed,
    first_gain,
    first_shift,
    up_weight,
    up_bias,
    down_weight,
    down_bias,
    second_gain,
    second_shift,
    content_cot,
    query_cot,
):
    half, width = content_in.shape[1:]
    seq_len = order_ranks.shape[1]
    ff = up_weight.shape[1]
    table = position_table(seq_len, width)
    (
        vec_c, vec_q, prob, proj_c, proj_q, keys, values, rel_keys, seg_hot, content_t, query_t, lines, up_bias_use,
        content, query, cots, squares, out_use, up_use, down_use,
    ) = forward(
        content_in, query_in, content_cot, query_cot, query_weight, key_weight, value_weight, rel_weight,
        out_weight, up_weight, down_weight, doc_lengths, order_ranks, segment_ids, target_flags,
        content_bias, position_bias, segment_bias, segment_embed, up_bias, jnp.asarray(table),
    )
    act, slope, scale, sums, norms, first_t, normal, grad, low_rows, low_t, rows_out = feed_forward(
        vec_c, vec_q, content, query, cots, out_use, up_use, down_use, up_bias_use,
        (first_gain, first_shift, second_gain, second_shift, down_bias),
    )
    pieces, tiny, keep_rows, rows_came, grad_came = backward(
        dp_size, seg_hot, proj_c, proj_q, keys, values, rel_keys, lines, prob, squares,
        vec_c, vec_q, content_t, query_t, jnp.asarray(table.T), out_use, act, slope, up_use, down_use,
        low_rows, low_t, first_t, normal, scale, norms, sums, grad, rows_out,
    )
    (
        content_out, query_out, content_grad, query_grad, down_sum, up_sum, out_sum,
        query_sum, key_sum, value_sum, rel_sum, cbias_sum, pbias_sum, sbias_sum, embed_sum,
        gain1_sum, shift1_sum, ubias_sum, dbias_sum, gain2_sum, shift2_sum,
    ) = finish(pieces, rows_out.reshape(4, half, width), rows_came, keep_rows, grad_came, tiny, ff)
    return (
        content_out, query_out, content_grad, query_grad,
        query_sum, key_sum, value_sum, out_sum, rel_sum, cbias_sum, pbias_sum, sbias_sum, embed_sum,
        gain1_sum, shift1_sum, up_sum, ubias_sum, down_sum, dbias_sum, gain2_sum, shift2_sum,
    )


def solution(mesh):
    placed = (
        P("dp", "mp", None),
        P("dp", "mp", None),
        P("dp"),
        P("dp", None),
        P("dp", None),
        P("dp", None),
        P(None, "mp"),
        P(None, "mp"),
        P(None, "mp"),
        P("mp", None),
        P(None, "mp"),
        P("mp"),
        P("mp"),
        P("mp"),
        P(None, "mp"),
        P(),
        P(),
        P(None, "mp"),
        P("mp"),
        P("mp", None),
        P(),
        P(),
        P(),
        P("dp", "mp", None),
        P("dp", "mp", None),
    )
    return jax.shard_map(
        functools.partial(on_device, mesh.shape["dp"]),
        mesh=mesh,
        in_specs=placed,
        out_specs=(
            P("dp", "mp", None),
            P("dp", "mp", None),
            P("dp", "mp", None),
            P("dp", "mp", None),
            P(None, "mp"),
            P(None, "mp"),
            P(None, "mp"),
            P("mp", None),
            P(None, "mp"),
            P("mp"),
            P("mp"),
            P("mp"),
            P(None, "mp"),
            P(),
            P(),
            P(None, "mp"),
            P("mp"),
            P("mp", None),
            P(),
            P(),
            P(),
        ),
        check_vma=False,
    )
```

```python
import functools

import jax
import jax.numpy as jnp
import ml_dtypes
import numpy as np
from jax import lax
from jax.experimental import pallas as pl
from jax.experimental.pallas import tpu as pltpu
from jax.sharding import PartitionSpec as P

epsilon = 1e-06
DH = 64
PAIR = 2 * DH
ROWS = 256
NEG = -1e30
MESH = pl.DeviceIdType.MESH


def nt(left_op, right_op):
    return lax.dot_general(
        left_op, right_op, (((1,), (1,)), ((), ())), preferred_element_type=jnp.float32
    )


def nn(left_op, right_op):
    return jnp.dot(left_op, right_op, preferred_element_type=jnp.float32)


def lane_ids(rows):
    return lax.broadcasted_iota(jnp.int32, (rows, PAIR), 1)


def forward_body(
    content_in, query_in, content_cot, query_cot, query_w, key_w, value_w, rel_w, out_w, up_w, down_w,
    length_ref, order_ref, segment_ref, target_ref, cbias_ref, pbias_ref, sbias_ref, embed_ref, ubias_ref, table_ref,
    vec_c, vec_q, prob_ref, proj_c, proj_q, key_ref, value_ref, rel_ref, hot_ref, content_t, query_t, vectors_out, ubias_out,
    content_out, query_out, cots_out, square_out, out_all, up_all, down_all,
    tokens, squares, near_pack, far_pack, bounce_up, bounce_down, bounce_out, bounce_cot, mask_scr, ext_scr, rank_scr, proj_next, low_next, rel_next,
    token_sem, token_send, token_recv, square_sem, square_send, square_recv,
    bulk_load, bulk_store, bulk_send, bulk_recv, vector_send, vector_recv,
):
    step = pl.program_id(0)
    core = lax.axis_index("mp")
    seq_len = proj_c.shape[0]
    half = seq_len // 2
    cols = query_w.shape[1]
    feed = up_w.shape[1]
    blocks = seq_len // ROWS
    wide = seq_len + ROWS
    other = {"mp": 1 - core}
    mine = pl.ds(pl.multiple_of(core * half, half), half)

    def remote(source, target, send, recv):
        return pltpu.make_async_remote_copy(
            src_ref=source, dst_ref=target, send_sem=send, recv_sem=recv,
            device_id=other, device_id_type=MESH,
        )

    token_in = (content_in, query_in)
    square_in = (query_w, key_w, value_w, rel_w)
    token_load = [
        pltpu.make_async_copy(token_in[at].at[core], tokens.at[at, mine], token_sem.at[at]) for at in range(2)
    ]
    token_swap = [
        remote(token_in[at].at[1 - core], tokens.at[at, mine], token_send.at[at], token_recv.at[at])
        for at in range(2)
    ]
    square_load = [
        pltpu.make_async_copy(square_in[at], squares.at[at, :, :cols], square_sem.at[at]) for at in range(4)
    ]
    square_swap = [
        remote(square_in[at], squares.at[at, :, cols:], square_send.at[at], square_recv.at[at])
        for at in range(4)
    ]
    vector_swap = remote(near_pack, far_pack, vector_send, vector_recv)
    cot_in = (content_cot, query_cot)
    bulk_loads = [
        pltpu.make_async_copy(out_w, bounce_out, bulk_load.at[0]),
        pltpu.make_async_copy(up_w, bounce_up, bulk_load.at[1]),
        pltpu.make_async_copy(down_w, bounce_down, bulk_load.at[2]),
    ] + [
        pltpu.make_async_copy(cot_in[at].at[core], bounce_cot.at[at], bulk_load.at[3 + at]) for at in range(2)
    ]
    bulk_stores = [
        pltpu.make_async_copy(bounce_out, out_all.at[:cols], bulk_store.at[0]),
        pltpu.make_async_copy(bounce_up, up_all.at[:, :feed], bulk_store.at[1]),
        pltpu.make_async_copy(bounce_down, down_all.at[:feed], bulk_store.at[2]),
    ] + [
        pltpu.make_async_copy(bounce_cot.at[at], cots_out.at[at, mine], bulk_store.at[3 + at]) for at in range(2)
    ]
    bulk_swaps = [
        remote(out_w, out_all.at[cols:], bulk_send.at[0], bulk_recv.at[0]),
        remote(up_w, up_all.at[:, feed:], bulk_send.at[1], bulk_recv.at[1]),
        remote(down_w, down_all.at[feed:], bulk_send.at[2], bulk_recv.at[2]),
    ] + [
        remote(cot_in[at].at[1 - core], cots_out.at[at, mine], bulk_send.at[3 + at], bulk_recv.at[3 + at])
        for at in range(2)
    ]
    token_store = [
        pltpu.make_async_copy(tokens.at[at], (content_out, query_out)[at], bulk_store.at[5 + at]) for at in range(2)
    ]
    square_store = [
        pltpu.make_async_copy(squares.at[at], square_out.at[at], bulk_store.at[7 + at]) for at in range(3)
    ]

    @pl.when(step == 0)
    def _():
        for copy in token_load + square_load:
            copy.start()
        near_pack[...] = jnp.zeros_like(near_pack)
        for at, part in enumerate((cbias_ref, pbias_ref, sbias_ref)):
            near_pack[at : at + 1, :cols] = part[...].astype(jnp.float32).reshape(1, cols)
        near_pack[3:5, :cols] = embed_ref[...].astype(jnp.float32)
        near_pack[5:6, :] = ubias_ref[...].astype(jnp.float32).reshape(1, feed)
        vectors_out[:, :cols] = near_pack[:, :cols]
        ubias_out[:, :feed] = near_pack[5:6, :]
        barrier = pltpu.get_barrier_semaphore()
        pl.semaphore_signal(barrier, inc=1, device_id=other, device_id_type=MESH)
        pl.semaphore_wait(barrier, 1)
        for copy in token_swap + [vector_swap] + square_swap + bulk_swaps + bulk_loads:
            copy.start()
        place_j = lax.broadcasted_iota(jnp.int32, (1, seq_len), 1)
        ranks = order_ref[pl.ds(core, 1), :].astype(jnp.float32)
        segments = segment_ref[pl.ds(core, 1), :].astype(jnp.float32)
        targets = target_ref[pl.ds(core, 1), :].astype(jnp.float32)
        length = length_ref[core]
        live = jnp.where(place_j >= 2, targets, 0.0)
        rank_scr[...] = jnp.transpose(jnp.broadcast_to(ranks, (PAIR, seq_len)))
        lane = lane_ids(seq_len)
        seg_turn = jnp.transpose(jnp.broadcast_to(segments, (PAIR, seq_len)))
        hot = (seg_turn == (lane % 4).astype(jnp.float32)) & (lane < 8)
        hot_ref[...] = jnp.where(hot, 1.0, 0.0).astype(jnp.bfloat16)
        base = jnp.where(place_j < length, 0.0, NEG)
        for block in range(blocks):
            rows = slice(block * ROWS, (block + 1) * ROWS)
            rank_i = jnp.concatenate([rank_scr[rows, :]] * (seq_len // PAIR), axis=1)
            seen = jnp.where((live == 0.0) | (ranks < rank_i), base, NEG)
            column = lax.broadcasted_iota(jnp.int32, (ROWS, seq_len), 1)
            line = lax.broadcasted_iota(jnp.int32, (ROWS, seq_len), 0) + block * ROWS
            diagonal = column == line
            mask_scr[0, rows, :] = jnp.where(diagonal, 0.0, seen)
            mask_scr[1, rows, :] = jnp.where(diagonal, NEG, seen)
        for copy in token_load + square_load:
            copy.wait()
        for copy in token_swap:
            copy.wait_recv()
        for copy in token_store:
            copy.start()

    @pl.when(step == 1)
    def _():
        for copy in bulk_loads:
            copy.wait()
        for copy in bulk_stores:
            copy.start()
        content_t[...] = jnp.transpose(tokens[0])
        query_t[...] = jnp.transpose(tokens[1])

    @pl.when(step == pl.num_programs(0) // 2 - 1)
    def _():
        for copy in square_swap + [vector_swap]:
            copy.wait_recv()
        for copy in square_store:
            copy.start()
        vectors_out[:, cols:] = far_pack[:, :cols]
        ubias_out[:, feed:] = far_pack[5:6, :]

    pair_lanes = pl.ds(pl.multiple_of(step * PAIR, PAIR), PAIR)
    lines = vectors_out[:, pair_lanes]
    double = pl.ds(pl.multiple_of((step // 2) * 2 * PAIR, 2 * PAIR), 2 * PAIR)

    @pl.when(step % 2 == 0)
    def _():
        six_w = jnp.concatenate([squares[at, :, double] for at in range(3)], axis=1)
        for block in range(blocks):
            rows = slice(block * ROWS, (block + 1) * ROWS)
            six = nn(tokens[0, rows, :], six_w)
            proj_c[rows, :] = six[:, :PAIR]
            proj_next[0, rows, :] = six[:, PAIR : 2 * PAIR]
            key_ref[rows, :] = six[:, 2 * PAIR : 3 * PAIR].astype(jnp.bfloat16)
            low_next[0, rows, :] = six[:, 3 * PAIR : 4 * PAIR].astype(jnp.bfloat16)
            value_ref[rows, :] = six[:, 4 * PAIR : 5 * PAIR].astype(jnp.bfloat16)
            low_next[1, rows, :] = six[:, 5 * PAIR :].astype(jnp.bfloat16)
            two = nn(tokens[1, rows, :], squares[0, :, double])
            proj_q[rows, :] = two[:, :PAIR]
            proj_next[1, rows, :] = two[:, PAIR:]
        for block in range(2 * blocks):
            rows = slice(block * ROWS, (block + 1) * ROWS)
            two = nn(table_ref[rows, :], squares[3, :, double]).astype(jnp.bfloat16)
            rel_ref[rows, :] = two[:, :PAIR]
            rel_next[rows, :] = two[:, PAIR:]

    @pl.when(step % 2 == 1)
    def _():
        proj_c[...] = proj_next[0]
        proj_q[...] = proj_next[1]
        key_ref[...] = low_next[0]
        value_ref[...] = low_next[1]
        rel_ref[...] = rel_next[...]

    ext_scr[:, :PAIR] = key_ref[...]
    ext_scr[:, PAIR:] = hot_ref[...]
    lane = lane_ids(ROWS)
    diff = lines[3:4, :] - lines[4:5, :]
    zero = jnp.zeros((), jnp.bfloat16)

    def rough(stream, block, head):
        rows = pl.ds(block * ROWS, ROWS)
        own = (lane >= DH) if head else (lane < DH)
        proj = (proj_c, proj_q)[stream][rows, :]
        query_c = ((proj + lines[0:1, :]) * 0.125).astype(jnp.bfloat16)
        query_p = ((proj + lines[1:2, :]) * 0.125).astype(jnp.bfloat16)
        seg_gap = (proj + lines[2:3, :]) * (diff * 0.125)
        gap = jnp.sum(jnp.where(own, seg_gap, 0.0), axis=1, keepdims=True)
        gap_high = gap.astype(jnp.bfloat16).astype(jnp.float32)
        seg_part = jnp.where(lane < 4, gap_high, gap - gap_high) * hot_ref[rows, :].astype(jnp.float32)
        left = jnp.concatenate([jnp.where(own, query_c, zero), seg_part.astype(jnp.bfloat16)], axis=1)
        window = rel_ref[pl.ds(seq_len - (block + 1) * ROWS, wide), :]
        scores = nt(left, ext_scr[...])
        table = nt(jnp.where(own, query_p, zero), window)
        return scores, table

    def settle(stream, block, head, scores, table):
        rows = pl.ds(block * ROWS, ROWS)
        table = pltpu.roll(table, 1, 1, stride=1, stride_axis=0)
        scores = scores + table[:, ROWS:] + mask_scr[stream, rows, :]
        top = jnp.max(scores, axis=1, keepdims=True)
        terms = jnp.exp(scores - top)
        total = jnp.sum(terms, axis=1, keepdims=True)
        prob = (terms * (1.0 / total)).astype(jnp.bfloat16)
        prob_ref[stream, head, rows, :] = prob
        return nn(prob, value_ref[...])

    turns = [(stream, block, head) for stream in range(2) for block in range(blocks) for head in range(2)]
    ahead = rough(*turns[0])
    part_first = None
    for at, (stream, block, head) in enumerate(turns):
        now = ahead
        if at + 1 < len(turns):
            ahead = rough(*turns[at + 1])
        part = settle(stream, block, head, *now)
        if head == 0:
            part_first = part
        else:
            rows = pl.ds(block * ROWS, ROWS)
            (vec_c, vec_q)[stream][rows, :] = jnp.where(lane < DH, part_first, part).astype(jnp.bfloat16)

    @pl.when(step == pl.num_programs(0) - 1)
    def _():
        for copy in token_swap + square_swap + [vector_swap]:
            copy.wait_send()
        for copy in bulk_swaps:
            copy.wait()
        for copy in bulk_stores + token_store + square_store:
            copy.wait()


def forward(
    content_in, query_in, content_cot, query_cot, query_w, key_w, value_w, rel_w, out_w, up_w, down_w,
    lengths, orders, segments, targets, cbias, pbias, sbias, embed, ubias, table,
):
    once = pl.Buffered(1)
    half, width = content_in.shape[1:]
    seq_len = 2 * half
    pairs = width // PAIR
    cols = query_w.shape[1]
    feed = up_w.shape[1]
    lines = 8
    keep = lambda shape: pl.BlockSpec(shape, lambda p: (0,) * len(shape), pipeline_mode=once)
    low = jnp.bfloat16
    dma = pltpu.SemaphoreType.DMA
    whole = lambda p: (0, 0)
    anywhere = pl.BlockSpec(memory_space=pl.ANY)
    tile = pl.BlockSpec((seq_len, PAIR), lambda p: (0, p))
    low_tokens = jax.ShapeDtypeStruct((seq_len, width), low)
    turned = jax.ShapeDtypeStruct((width, seq_len), low)
    return pl.pallas_call(
        forward_body,
        out_shape=(
            low_tokens, low_tokens,
            jax.ShapeDtypeStruct((pairs, 2, 2, seq_len, seq_len), low),
            jax.ShapeDtypeStruct((seq_len, width), jnp.float32),
            jax.ShapeDtypeStruct((seq_len, width), jnp.float32),
            low_tokens, low_tokens,
            jax.ShapeDtypeStruct((2 * seq_len, width), low),
            jax.ShapeDtypeStruct((seq_len, PAIR), low),
            turned, turned,
            jax.ShapeDtypeStruct((lines, width), jnp.float32),
            jax.ShapeDtypeStruct((1, 2 * feed), jnp.float32),
            low_tokens, low_tokens,
            jax.ShapeDtypeStruct((2, seq_len, width), low),
            jax.ShapeDtypeStruct((3, width, width), low),
            jax.ShapeDtypeStruct((width, width), low),
            jax.ShapeDtypeStruct((width, 2 * feed), low),
            jax.ShapeDtypeStruct((2 * feed, width), low),
        ),
        grid_spec=pltpu.PrefetchScalarGridSpec(
            num_scalar_prefetch=0,
            grid=(pairs,),
            in_specs=[anywhere] * 11
            + [
                pl.BlockSpec(memory_space=pltpu.SMEM),
                keep(orders.shape), keep(orders.shape), keep(orders.shape),
                keep(cbias.shape), keep(cbias.shape), keep(cbias.shape), keep(embed.shape), keep(ubias.shape),
                keep((2 * seq_len, width)),
            ],
            out_specs=[
                tile, tile,
                pl.BlockSpec((None, 2, 2, seq_len, seq_len), lambda p: (p, 0, 0, 0, 0)),
                tile, tile, tile, tile,
                pl.BlockSpec((2 * seq_len, PAIR), lambda p: (0, p)),
                pl.BlockSpec((seq_len, PAIR), whole),
                pl.BlockSpec((width, seq_len), whole),
                pl.BlockSpec((width, seq_len), whole),
                pl.BlockSpec((lines, width), whole),
                pl.BlockSpec((1, 2 * feed), whole),
            ]
            + [anywhere] * 7,
            scratch_shapes=[
                pltpu.VMEM((2, seq_len, width), low),
                pltpu.VMEM((4, width, width), low),
                pltpu.VMEM((lines, feed), jnp.float32),
                pltpu.VMEM((lines, feed), jnp.float32),
                pltpu.VMEM((width, feed), low),
                pltpu.VMEM((feed, width), low),
                pltpu.VMEM((cols, width), low),
                pltpu.VMEM((2, half, width), low),
                pltpu.VMEM((2, seq_len, seq_len), jnp.float32),
                pltpu.VMEM((seq_len, 2 * PAIR), low),
                pltpu.VMEM((seq_len, PAIR), jnp.float32),
                pltpu.VMEM((2, seq_len, PAIR), jnp.float32),
                pltpu.VMEM((2, seq_len, PAIR), low),
                pltpu.VMEM((2 * seq_len, PAIR), low),
                dma((2,)), dma((2,)), dma((2,)), dma((4,)), dma((4,)), dma((4,)),
                dma((5,)), dma((10,)), dma((5,)), dma((5,)), dma, dma,
            ],
        ),
        compiler_params=pltpu.CompilerParams(
            collective_id=1, has_side_effects=True, vmem_limit_bytes=60 << 20
        ),
        name="attend_forward",
    )(
        content_in, query_in, content_cot, query_cot, query_w, key_w, value_w, rel_w, out_w, up_w, down_w,
        lengths, orders, segments, targets, cbias, pbias, sbias, embed, ubias, table,
    )


GELU_A = 0.7978845608028654
GELU_B = 0.044715


def norm_parts(value_in):
    center = value_in - jnp.mean(value_in, axis=1, keepdims=True)
    scale = lax.rsqrt(jnp.mean(center * center, axis=1, keepdims=True) + epsilon)
    return center * scale, scale


def norm_pull(normal, scale, grad):
    return scale * (
        grad
        - jnp.mean(grad, axis=1, keepdims=True)
        - normal * jnp.mean(grad * normal, axis=1, keepdims=True)
    )


def feed_forward_body(
    vec_c, vec_q, content, query, out_ref, up_ref, down_ref, up_bias,
    gain1_ref, shift1_ref, gain2_ref, shift2_ref, dbias_ref, cots_in,
    act_ref, slope_ref, scale_ref, sums_ref, norms,
    first_t_out, normal_out, grad_out, low_out, low_t_out, rows_out,
    first_scr, total_scr, cots, first_t, normal_ref, grad_ref, low_ref, low_t, rows_ref, cot_sem, out_sem,
):
    step = pl.program_id(0)
    half_rows = vec_c.shape[0]
    last = pl.num_programs(0) - 1
    cot_copy = pltpu.make_async_copy(cots_in, cots, cot_sem)

    def lines_copy(at, source, target, start):
        here = pl.ds(start, ROWS)
        return pltpu.make_async_copy(source.at[here], target.at[here], out_sem.at[at, start // ROWS])

    first_copies = [pltpu.make_async_copy(first_t, first_t_out, out_sem.at[0, 0])] + [
        lines_copy(1, normal_ref, normal_out, start) for start in range(0, 2 * half_rows, ROWS)
    ]
    late_copies = [
        [
            lines_copy(2, grad_ref, grad_out, start),
            lines_copy(3, low_ref, low_out, start),
            lines_copy(4, rows_ref, rows_out, start),
            pltpu.make_async_copy(
                low_t.at[:, pl.ds(start, ROWS)], low_t_out.at[:, pl.ds(start, ROWS)], out_sem.at[5, start // ROWS]
            ),
        ]
        for start in range(0, 2 * half_rows, ROWS)
    ]
    chunks = [(s, at) for s in range(2) for at in range(0, half_rows, ROWS)]

    @pl.when(step == 0)
    def _():
        cot_copy.start()
        norms[...] = jnp.zeros_like(norms)
        for at, part in enumerate((gain1_ref, shift1_ref, gain2_ref, shift2_ref, dbias_ref)):
            norms[at : at + 1, :] = part[...].astype(jnp.float32).reshape(1, part.shape[0])
        for stream, at in chunks:
            here = pl.ds(at, ROWS)
            there = slice(stream * half_rows + at, stream * half_rows + at + ROWS)
            mixed = nn((vec_c, vec_q)[stream][here, :], out_ref[...])
            mixed = mixed + (content, query)[stream][here, :].astype(jnp.float32)
            normal, scale = norm_parts(mixed)
            first = (normal * norms[0:1, :] + norms[1:2, :]).astype(jnp.bfloat16)
            first_scr[there, :] = first
            first_t[:, there] = jnp.transpose(first)
            normal_ref[there, :] = normal.astype(jnp.bfloat16)
            scale_ref[there, :] = scale
            total_scr[there, :] = first.astype(jnp.float32) + norms[4:5, :]
        for copy in first_copies:
            copy.start()

    spots = [slice(s * half_rows + at, s * half_rows + at + ROWS) for s, at in chunks]
    ahead = nn(first_scr[spots[0], :], up_ref[...])
    for turn, there in enumerate(spots):
        value = ahead + up_bias[...]
        if turn + 1 < len(spots):
            ahead = nn(first_scr[spots[turn + 1], :], up_ref[...])
        square = value * value
        half = 0.5 + 0.5 * jnp.tanh(value * (GELU_A + (GELU_A * GELU_B) * square))
        wide = value * half
        act = wide.astype(jnp.bfloat16)
        slope = half + (wide * (1.0 - half)) * ((2.0 * GELU_A) + (6.0 * GELU_A * GELU_B) * square)
        act_ref[there, :] = act
        slope_ref[there, :] = slope.astype(jnp.bfloat16)
        total_scr[there, :] += nn(act, down_ref[...])

    @pl.when(step == last)
    def _():
        cot_copy.wait()
        sums = [jnp.zeros((1, content.shape[1]), jnp.float32) for _ in range(3)]
        for stream, at in chunks:
            here = pl.ds(at, ROWS)
            there = slice(stream * half_rows + at, stream * half_rows + at + ROWS)
            normal, scale = norm_parts(total_scr[there, :])
            rows_ref[there, :] = (normal * norms[2:3, :] + norms[3:4, :]).astype(jnp.bfloat16)
            cot = cots[stream, here, :].astype(jnp.float32)
            grad = norm_pull(normal, scale, cot * norms[2:3, :])
            grad_ref[there, :] = grad
            low = grad.astype(jnp.bfloat16)
            low_ref[there, :] = low
            low_t[:, there] = jnp.transpose(low)
            for at_sum, term in enumerate((cot * normal, cot, grad)):
                sums[at_sum] = sums[at_sum] + jnp.sum(term, axis=0, keepdims=True)
            for copy in late_copies[(stream * half_rows + at) // ROWS]:
                copy.start()
        sums_ref[...] = jnp.concatenate(sums + [jnp.zeros((5, content.shape[1]), jnp.float32)], axis=0)
        for copy in first_copies + sum(late_copies, []):
            copy.wait()


def feed_forward(vec_c, vec_q, content, query, cots, out_use, up_use, down_use, up_bias, vectors):
    seq_len, width = content.shape
    hidden = up_use.shape[1]
    cols = 512
    rows = 2 * seq_len
    low = jnp.bfloat16
    once = pl.Buffered(1)
    whole = lambda f: (0, 0)
    side = lambda f: (0, f)
    keep = lambda shape: pl.BlockSpec(shape, whole, pipeline_mode=once)
    stream = keep((seq_len, width))
    flat = pl.BlockSpec((width,), lambda f: (0,))
    anywhere = pl.BlockSpec(memory_space=pl.ANY)
    return pl.pallas_call(
        feed_forward_body,
        out_shape=(
            jax.ShapeDtypeStruct((rows, hidden), low),
            jax.ShapeDtypeStruct((rows, hidden), low),
            jax.ShapeDtypeStruct((rows, 1), jnp.float32),
            jax.ShapeDtypeStruct((8, width), jnp.float32),
            jax.ShapeDtypeStruct((8, width), jnp.float32),
            jax.ShapeDtypeStruct((width, rows), low),
            jax.ShapeDtypeStruct((rows, width), low),
            jax.ShapeDtypeStruct((rows, width), jnp.float32),
            jax.ShapeDtypeStruct((rows, width), low),
            jax.ShapeDtypeStruct((width, rows), low),
            jax.ShapeDtypeStruct((rows, width), low),
        ),
        grid=(hidden // cols,),
        in_specs=[
            stream, stream, stream, stream,
            keep((width, width)),
            pl.BlockSpec((width, cols), side),
            pl.BlockSpec((cols, width), lambda f: (f, 0)),
            pl.BlockSpec((1, cols), side),
            flat, flat, flat, flat, flat,
            anywhere,
        ],
        out_specs=[
            pl.BlockSpec((rows, cols), side),
            pl.BlockSpec((rows, cols), side),
            pl.BlockSpec((rows, 1), whole),
            pl.BlockSpec((8, width), whole),
            pl.BlockSpec((8, width), whole),
        ]
        + [anywhere] * 6,
        scratch_shapes=[
            pltpu.VMEM((rows, width), low),
            pltpu.VMEM((rows, width), jnp.float32),
            pltpu.VMEM(cots.shape, low),
            pltpu.VMEM((width, rows), low),
            pltpu.VMEM((rows, width), low),
            pltpu.VMEM((rows, width), jnp.float32),
            pltpu.VMEM((rows, width), low),
            pltpu.VMEM((width, rows), low),
            pltpu.VMEM((rows, width), low),
            pltpu.SemaphoreType.DMA,
            pltpu.SemaphoreType.DMA((6, rows // ROWS)),
        ],
        compiler_params=pltpu.CompilerParams(vmem_limit_bytes=60 << 20),
        name="feed_forward",
    )(vec_c, vec_q, content, query, out_use, up_use, down_use, up_bias, *vectors, cots)


FOLDS = 4
EARLY = 7
COUNT = 10
CHUNK = 512


def backward_body(dp_size, *refs):
    (
        seg_hot, proj_c, proj_q, key_ref, value_ref, rel_ref, bias_ref, prob_ref,
        square_w, act_ref, slope_ref, up_ref, down_ref, scale_ref, norms, sums_in,
        content_t, query_t, table_t, low_t, first_t, normal_in, grad_in, rows_in, vec_c_in, vec_q_in, out_in, low_in,
        sum_out, small_out, keep_out, rows_came, grad_came,
        vt_scr, key_acc, value_acc, rel_acc, total, vec_grad, hid_scr, turn_a, turn_b, flip_scr, vec_c, vec_q, out_w, low_ref,
        work, swapped, landed, extra, small_work, small_far, small_land,
        store_sem, swap_send, swap_recv, fold_send, fold_recv, spread_send, spread_recv,
        more_send, more_recv, tiny_send, tiny_recv, side_sem, keep_sem, back_send, back_recv,
    ) = refs
    seq_len = key_ref.shape[0]
    gproj_c = hid_scr.at[:seq_len, : 3 * PAIR]
    gproj_q = hid_scr.at[seq_len:, :PAIR]
    ext_scr = hid_scr.at[seq_len:, PAIR : 3 * PAIR]
    grid_at = pl.program_id(0)
    feeds = 6
    pairs = 6
    half_pairs = pairs // 2
    last = pl.num_programs(0) - 1
    rows, width = total.shape[1], work.shape[2]
    cols = rows // 2
    place = lax.axis_index("dp")
    core = lax.axis_index("mp")
    strides = [1 + core, 2 - core, 4, 8]
    more = [16 << step for step in range(8) if (16 << step) < dp_size]
    bits = [(place // stride) % 2 for stride in strides]
    partners = [place + (1 - 2 * bit) * stride for bit, stride in zip(bits, strides)]
    more_partners = [place + (1 - 2 * ((place // stride) % 2)) * stride for stride in more]
    lengths = [rows >> (fold + 1) for fold in range(FOLDS)]
    starts, begin = [], 0
    for bit, length in zip(bits, lengths):
        begin = begin + bit * length
        starts.append(begin)
    land_at = [rows - 2 * length for length in lengths]
    offsets = [0, 3, 6, 8, 10, 12, 14, 16, 19]
    final_slot = 25

    def kept(fold):
        return pl.ds(pl.multiple_of(starts[fold], 16), lengths[fold])

    def given(fold):
        return pl.ds(pl.multiple_of(starts[fold] + (1 - 2 * bits[fold]) * lengths[fold], 16), lengths[fold])

    def remote(source, target, send, recv, device):
        return pltpu.make_async_remote_copy(
            src_ref=source, dst_ref=target, send_sem=send, recv_sem=recv,
            device_id=device, device_id_type=MESH,
        )

    def swap_copy(piece):
        return remote(
            work.at[piece], swapped.at[piece], swap_send.at[piece], swap_recv.at[piece], {"mp": 1 - core}
        )

    def fold_copy(fold, piece, lanes):
        return remote(
            work.at[piece, given(fold), :lanes],
            landed.at[piece, pl.ds(land_at[fold], lengths[fold]), :lanes],
            fold_send.at[fold, piece], fold_recv.at[fold, piece], {"dp": partners[fold]},
        )

    def spread_copy(fold, piece, lanes):
        return remote(
            swapped.at[piece, kept(fold), :lanes],
            swapped.at[piece, kept(fold), :lanes],
            spread_send.at[fold, piece], spread_recv.at[fold, piece], {"dp": partners[fold]},
        )

    def extra_ref(step, piece):
        if step == 0:
            return landed.at[piece, pl.ds(rows - lengths[-1], lengths[-1])]
        return extra.at[step - 1, piece]

    def spread_away(fold, piece, lanes):
        return remote(
            swapped.at[piece, kept(fold), :lanes], swapped.at[piece, given(fold), :lanes],
            spread_send.at[fold, piece], spread_recv.at[fold, piece], {"dp": partners[fold]},
        )

    def sized(piece, act):
        @pl.when(piece == EARLY - 1)
        def _():
            act(cols)

        @pl.when(piece != EARLY - 1)
        def _():
            act(width)

    def more_copy(step, piece):
        return remote(
            work.at[piece, kept(FOLDS - 1)],
            extra_ref(step, piece),
            more_send.at[step, piece], more_recv.at[step, piece], {"dp": more_partners[step]},
        )

    def store(piece):
        return pltpu.make_async_copy(swapped.at[piece], sum_out.at[piece], store_sem.at[piece])

    def add_rows(piece, where, other):
        mine = work[piece, where, :].astype(jnp.float32)
        work[piece, where, :] = (mine + other.astype(jnp.float32)).astype(jnp.bfloat16)

    tiny_devices = [{"mp": 1 - core}] + [{"dp": partner} for partner in partners + more_partners]

    def tiny_copy(step):
        return remote(
            small_far if step == 0 else small_work.at[step],
            small_land.at[step], tiny_send.at[step], tiny_recv.at[step], tiny_devices[step],
        )

    far_rows = (1 - core) * ROWS

    def rows_copy(stream):
        return remote(
            rows_in.at[pl.ds(pl.multiple_of(stream * seq_len + far_rows, ROWS), ROWS)], rows_came.at[stream],
            back_send.at[stream], back_recv.at[stream], {"mp": 1 - core},
        )

    def grad_copy(stream):
        return remote(
            vec_grad.at[pl.ds(pl.multiple_of(stream * seq_len + far_rows, ROWS), ROWS)], grad_came.at[stream],
            back_send.at[2 + stream], back_recv.at[2 + stream], {"mp": 1 - core},
        )

    def keep_copy(stream):
        return pltpu.make_async_copy(
            vec_grad.at[pl.ds(pl.multiple_of(stream * seq_len + core * ROWS, ROWS), ROWS)],
            keep_out.at[stream], keep_sem.at[stream],
        )

    side_loads = [
        pltpu.make_async_copy(source, target, side_sem.at[at])
        for at, (source, target) in enumerate(
            (
                (grad_in, total),
                (first_t, turn_a),
                (low_t, turn_b),
                (normal_in, vec_grad),
                (table_t, turn_a),
                (content_t, turn_b.at[:, :seq_len]),
                (query_t, turn_b.at[:, seq_len:]),
                (vec_c_in, vec_c),
                (vec_q_in, vec_q),
                (out_in, out_w),
                (low_in, low_ref),
            )
        )
    ]

    def stage(number, piece):
        if number == 0:
            sized(piece, lambda lanes: fold_copy(0, piece, lanes).start())
        elif number <= FOLDS:
            fold = number - 1
            sized(piece, lambda lanes: fold_copy(fold, piece, lanes).wait_recv())
            add_rows(piece, kept(fold), landed[piece, pl.ds(land_at[fold], lengths[fold]), :])
            if fold + 1 < FOLDS:
                sized(piece, lambda lanes: fold_copy(fold + 1, piece, lanes).start())
                return
            for step in range(len(more)):
                more_copy(step, piece).start()
                more_copy(step, piece).wait()
                add_rows(piece, kept(fold), extra_ref(step, piece)[...])
            swapped[piece, kept(fold), :] = work[piece, kept(fold), :]
            sized(piece, lambda lanes: spread_copy(fold, piece, lanes).start())
        else:
            fold = 2 * FOLDS - number
            sized(piece, lambda lanes: spread_away(fold, piece, lanes).wait_recv())
            if fold > 0:
                sized(piece, lambda lanes: spread_copy(fold - 1, piece, lanes).start())
            else:
                store(piece).start()

    def advance(tick):
        for number in reversed(range(2 * FOLDS + 1)):
            slot = tick - offsets[number]
            early = (slot == 2) | (slot == 3) | (slot == 6) | (slot == 7) | (slot == 10) | (slot == 11)
            late = (slot == 13) | (slot == 17) | (slot == 21) | (slot == final_slot)
            piece = jnp.where(slot < 13, 2 * ((slot - 2) // 4) + (slot - 2) % 4, EARLY - 1 + (slot - 13) // 4)

            @pl.when(early | late)
            def _():
                stage(number, piece)

    def settle(piece):
        swap_copy(piece).wait_recv()
        add_rows(piece, pl.ds(0, rows), swapped[piece])

    @pl.when(grid_at == 0)
    def _():
        barrier = pltpu.get_barrier_semaphore()
        for device in tiny_devices:
            pl.semaphore_signal(barrier, inc=1, device_id=device, device_id_type=MESH)
        pl.semaphore_wait(barrier, len(tiny_devices))
        for at in (2, 10, 0, 1, 3, 7, 8, 9):
            side_loads[at].start()
        rows_copy(0).start()
        rows_copy(1).start()
        small_work[0] = jnp.zeros_like(small_work[0])
        small_far[...] = jnp.zeros_like(small_far)
        for at in range(3):
            for side in range(2):
                line = sums_in[at : at + 1, side * cols : (side + 1) * cols]
                spot = slice(12 + 2 * at + side, 13 + 2 * at + side)
                small_work[0, spot, :cols] = line
                small_far[spot, :cols] = line
        line_at = lax.broadcasted_iota(jnp.int32, (ROWS, ROWS), 0)
        lane_at = lax.broadcasted_iota(jnp.int32, (ROWS, ROWS), 1)
        flip_scr[...] = jnp.where(line_at + lane_at == ROWS - 1, 1.0, 0.0).astype(jnp.bfloat16)

    @pl.when(grid_at < feeds)
    def _():
        chunk = grid_at // 2
        near = grid_at % 2 == 1
        bias_sum = jnp.zeros((1, width), jnp.float32)

        @pl.when(near)
        def _():
            swap_copy(2 * chunk).wait_send()

        @pl.when(grid_at == 0)
        def _():
            side_loads[2].wait()

        for at in range(0, rows, ROWS):
            here = slice(at, at + ROWS)
            work[2 * chunk, here, :] = nn(turn_b[here, :], act_ref[...]).astype(jnp.bfloat16)

        @pl.when(near)
        def _():
            settle(2 * chunk)

        @pl.when(jnp.logical_not(near))
        def _():
            swap_copy(2 * chunk).start()

        @pl.when(grid_at == 0)
        def _():
            for at in (10, 0, 1):
                side_loads[at].wait()

        advance(2 * grid_at)
        for at in range(0, total.shape[0], ROWS):
            here = slice(at, at + ROWS)
            grad_act = nt(low_ref[here, :], down_ref[...])
            hid = (grad_act * slope_ref[here, :].astype(jnp.float32)).astype(jnp.bfloat16)
            hid_scr[here, :] = hid
            bias_sum = bias_sum + jnp.sum(hid.astype(jnp.float32), axis=0, keepdims=True)
            total[here, :] += nt(hid, up_ref[...])

        @pl.when(near)
        def _():
            swap_copy(2 * chunk + 1).wait_send()

        for at in range(0, rows, ROWS):
            here = slice(at, at + ROWS)
            work[2 * chunk + 1, here, :] = nn(turn_a[here, :], hid_scr[...]).astype(jnp.bfloat16)

        @pl.when(near)
        def _():
            small_work[0, pl.ds(5 + chunk, 1), :] = bias_sum
            settle(2 * chunk + 1)

        @pl.when(jnp.logical_not(near))
        def _():
            small_far[pl.ds(5 + chunk, 1), :] = bias_sum
            swap_copy(2 * chunk + 1).start()

    @pl.when(grid_at == feeds)
    def _():
        advance(2 * grid_at)
        for copy in side_loads[4:7]:
            copy.start()
        for at in (3, 7, 8, 9):
            side_loads[at].wait()
        sums = [jnp.zeros((1, rows), jnp.float32) for _ in range(2)]
        out_piece = EARLY - 1
        near_sum = jnp.zeros((rows, cols), jnp.float32)
        far_sum = jnp.zeros((rows, cols), jnp.float32)
        for at in range(0, total.shape[0], ROWS):
            here = slice(at, at + ROWS)
            normal = vec_grad[here, :].astype(jnp.float32)
            grad = total[here, :]
            sums[0] = sums[0] + jnp.sum(grad * normal, axis=0, keepdims=True)
            sums[1] = sums[1] + jnp.sum(grad, axis=0, keepdims=True)
            grad = norm_pull(normal, scale_ref[here, :], grad * norms[0:1, :])
            total[here, :] = grad
            vec_grad[here, :] = grad.astype(jnp.bfloat16)
        for at in range(0, total.shape[0], ROWS):
            here = slice(at, at + ROWS)
            low = vec_grad[here, :]
            low_turn = jnp.transpose(low)
            vec = (vec_c, vec_q)[at // seq_len][at % seq_len : at % seq_len + ROWS, :]
            far_sum = far_sum + nn(low_turn, vec[:, cols:])
            near_sum = near_sum + nn(low_turn, vec[:, :cols])
            vec_grad[here, :] = nt(low, out_w[...]).astype(jnp.bfloat16)
        work[out_piece, :, :cols] = far_sum.astype(jnp.bfloat16)
        work[out_piece, :, cols:] = jnp.zeros((rows, width - cols), jnp.bfloat16)
        swap_copy(out_piece).start()
        for at in range(2):
            for side in range(2):
                line = sums[at][:, side * cols : (side + 1) * cols]
                spot = slice(8 + 2 * at + side, 9 + 2 * at + side)
                small_work[0, spot, :cols] = line
                small_far[spot, :cols] = line
        swap_copy(out_piece).wait()
        near_sum = near_sum + swapped[out_piece, :, :cols].astype(jnp.float32)
        work[out_piece, :, :cols] = near_sum.astype(jnp.bfloat16)

    @pl.when(grid_at > feeds)
    def _():
        turn = grid_at - feeds - 1
        late = turn // 2
        near = turn % 2 == 1
        pair = late + (1 - turn % 2) * half_pairs

        @pl.when(turn == 0)
        def _():
            for copy in side_loads[4:7]:
                copy.wait()

        pair_lanes = pl.ds(pl.multiple_of(pair * PAIR, PAIR), PAIR)
        blocks = seq_len // ROWS
        wide = seq_len + ROWS
        ext_scr[:, :PAIR] = (key_ref[...].astype(jnp.float32) * 0.125).astype(jnp.bfloat16)
        ext_scr[:, PAIR:] = (seg_hot[...].astype(jnp.float32) * 0.125).astype(jnp.bfloat16)
        vt_scr[...] = jnp.transpose(value_ref[...])
        key_acc[...] = jnp.zeros_like(key_acc)
        value_acc[...] = jnp.zeros_like(value_acc)
        rel_acc[...] = jnp.zeros_like(rel_acc)
        lane = lane_ids(ROWS)
        first = lane < DH
        sums = [jnp.zeros((1, PAIR), jnp.float32) for _ in range(5)]
        for stream in range(2):
            proj_ref = (proj_c, proj_q)[stream]
            vec_ref = (vec_c, vec_q)[stream]
            gproj_ref = (gproj_c, gproj_q)[stream]
            for block in range(blocks):
                where = pl.ds(block * ROWS, ROWS)
                start = seq_len - (block + 1) * ROWS
                proj = proj_ref[where, :]
                query_ct = jnp.transpose(((proj + bias_ref[0:1, :]) * 0.125).astype(jnp.bfloat16))
                query_p = ((proj + bias_ref[1:2, :]) * 0.125).astype(jnp.bfloat16)
                query_pt = jnp.transpose(nn(flip_scr[...], query_p).astype(jnp.bfloat16))
                query_s = proj + bias_ref[2:3, :]
                hot = jnp.where(lane < 4, seg_hot[where, :].astype(jnp.float32), 0.0)
                grad = vec_grad[pl.ds(stream * seq_len + block * ROWS, ROWS), pair_lanes]
                grad_t = jnp.transpose(grad)
                inner = grad.astype(jnp.float32) * vec_ref[where, pair_lanes].astype(jnp.float32)
                window = (rel_ref[pl.ds(start, wide), :].astype(jnp.float32) * 0.125).astype(jnp.bfloat16)
                parts = []
                for head in range(2):
                    own = (lane >= DH) if head else first
                    low, high = head * DH, (head + 1) * DH
                    prob = prob_ref[stream, head, where, :]
                    grad_prob = nn(jnp.where(own, grad, jnp.zeros((), jnp.bfloat16)), vt_scr[...])
                    row_inner = jnp.sum(jnp.where(own, inner, 0.0), axis=1, keepdims=True)
                    gscore = (prob.astype(jnp.float32) * (grad_prob - row_inner)).astype(jnp.bfloat16)
                    value_acc[low:high, :] += nn(grad_t[low:high, :], prob)
                    key_acc[low:high, :] += nn(query_ct[low:high, :], gscore)
                    both = nn(gscore, ext_scr[...])
                    table = nn(flip_scr[...], gscore).astype(jnp.bfloat16)
                    table = jnp.concatenate([table, jnp.zeros((ROWS, ROWS), jnp.bfloat16)], axis=1)
                    table = pltpu.roll(table, 0, 1, stride=1, stride_axis=0)
                    gpos = nn(table, window)
                    rel_acc[low:high, start : start + wide] += nn(query_pt[low:high, :], table)
                    tail = both[:, PAIR:]
                    tail = jnp.where(lane < 4, tail, 0.0)
                    g_same = jnp.sum(tail * hot, axis=1, keepdims=True)
                    g_other = jnp.sum(tail, axis=1, keepdims=True) - g_same
                    parts.append((both[:, :PAIR], gpos, g_same, g_other))
                g_content = jnp.where(first, parts[0][0], parts[1][0])
                g_position = jnp.where(first, parts[0][1], parts[1][1]).astype(jnp.bfloat16)
                g_position = nn(flip_scr[...], g_position)
                g_same = jnp.where(first, parts[0][2], parts[1][2])
                g_other = jnp.where(first, parts[0][3], parts[1][3])
                g_segment = g_same * bias_ref[3:4, :] + g_other * bias_ref[4:5, :]
                gproj_ref[where, :PAIR] = (g_content + g_position + g_segment).astype(jnp.bfloat16)
                terms = (g_content, g_position, g_segment, g_same * query_s, g_other * query_s)
                sums = [old + jnp.sum(term, axis=0, keepdims=True) for old, term in zip(sums, terms)]
            if stream == 0:
                advance(2 * grid_at)
        gproj_c[:, PAIR : 2 * PAIR] = jnp.transpose(key_acc[...]).astype(jnp.bfloat16)
        gproj_c[:, 2 * PAIR :] = jnp.transpose(value_acc[...]).astype(jnp.bfloat16)
        triple = nn(turn_b[:, :seq_len], gproj_c[...])
        g_query = triple[:, :PAIR] + nn(turn_b[:, seq_len:], gproj_q[...])
        g_rel = nt(turn_a[...], rel_acc[...].astype(jnp.bfloat16))
        vectors = jnp.concatenate(sums, axis=0)
        piece = EARLY + late
        lanes = pl.ds(pl.multiple_of(late * PAIR, PAIR), PAIR)

        @pl.when(near)
        def _():
            swap_copy(piece).wait_send()

        work[piece, :, :PAIR] = g_query.astype(jnp.bfloat16)
        work[piece, :, PAIR : 3 * PAIR] = triple[:, PAIR:].astype(jnp.bfloat16)
        work[piece, :, 3 * PAIR :] = g_rel.astype(jnp.bfloat16)

        @pl.when(jnp.logical_not(near))
        def _():
            small_far[0:5, lanes] = vectors
            swap_copy(piece).start()

            @pl.when(turn == pairs - 2)
            def _():
                tiny_copy(0).start()

        @pl.when(near)
        def _():
            small_work[0, 0:5, lanes] = vectors
            settle(piece)

    advance(2 * grid_at + 1)

    @pl.when(grid_at > feeds)
    def _():
        weights = jnp.concatenate([square_w[0], square_w[1], square_w[2]], axis=1)
        total[:seq_len, :] += nt(gproj_c[...], weights)
        total[seq_len:, :] += nt(gproj_q[...], square_w[0])

    @pl.when(grid_at == last)
    def _():
        for at in range(0, total.shape[0], ROWS):
            vec_grad[at : at + ROWS, :] = total[at : at + ROWS, :].astype(jnp.bfloat16)
        begin_tick = final_slot + 1

        def finish_tick(tick, carry):
            for step in range(len(tiny_devices)):
                @pl.when(tick == begin_tick + step)
                def _():
                    tiny_copy(step).wait_recv()
                    small_work[step + 1] = small_work[step] + small_land[step]
                    if step + 1 < len(tiny_devices):
                        tiny_copy(step + 1).start()

            advance(tick)

            @pl.when(tick == begin_tick)
            def _():
                grad_copy(0).start()
                grad_copy(1).start()
                keep_copy(0).start()
                keep_copy(1).start()

            return carry

        lax.fori_loop(begin_tick, final_slot + 1 + offsets[-1], finish_tick, 0)
        small_out[...] = small_work[len(tiny_devices)]
        for step in range(len(tiny_devices)):
            tiny_copy(step).wait_send()
        for stream in range(2):
            rows_copy(stream).wait()
            grad_copy(stream).wait()
            keep_copy(stream).wait()

        def drain(piece, carry):
            for fold in range(FOLDS):
                sized(piece, lambda lanes: fold_copy(fold, piece, lanes).wait_send())
                sized(piece, lambda lanes: spread_copy(fold, piece, lanes).wait_send())
            store(piece).wait()
            return carry

        lax.fori_loop(0, COUNT, drain, 0)


def backward(
    dp_size, seg_hot, proj_c, proj_q, keys, values, rel_keys, lines, prob, squares,
    vec_c, vec_q, content_t, query_t, table_t, out_w, act, slope, up_w, down_w, low_rows, low_t, first_t,
    normal, scale, norms, sums, grad, rows_in,
):
    seq_len, width = proj_c.shape
    pairs = width // PAIR
    feeds = up_w.shape[1] // CHUNK
    rows = 2 * seq_len
    small_rows = 24
    more = max(1, dp_size.bit_length() - 1 - FOLDS)
    tiny = dp_size.bit_length()
    low = jnp.bfloat16
    dma = pltpu.SemaphoreType.DMA
    once = pl.Buffered(1)
    anywhere = pl.BlockSpec(memory_space=pl.ANY)
    whole = lambda g: (0, 0)

    def turn(g):
        at = jnp.maximum(g - feeds - 1, 0)
        return at // 2 + (1 - at % 2) * (pairs // 2)

    def chunk(g):
        at = jnp.minimum(g, feeds - 1)
        return (1 - at % 2) * (feeds // 2) + at // 2

    per_pair = lambda g: (0, turn(g))
    tile = pl.BlockSpec((seq_len, PAIR), per_pair)
    side = lambda g: (0, chunk(g))
    keep = lambda shape: pl.BlockSpec(shape, whole, pipeline_mode=once)
    pieces = pltpu.VMEM((COUNT, width, CHUNK), low)
    return pl.pallas_call(
        functools.partial(backward_body, dp_size),
        out_shape=(
            jax.ShapeDtypeStruct((COUNT, width, CHUNK), low),
            jax.ShapeDtypeStruct((small_rows, CHUNK), jnp.float32),
            jax.ShapeDtypeStruct((2, ROWS, width), low),
            jax.ShapeDtypeStruct((2, ROWS, width), low),
            jax.ShapeDtypeStruct((2, ROWS, width), low),
        ),
        grid_spec=pltpu.PrefetchScalarGridSpec(
            num_scalar_prefetch=0,
            grid=(feeds + 1 + pairs,),
            in_specs=[
                keep((seq_len, PAIR)),
                tile, tile, tile, tile,
                pl.BlockSpec((2 * seq_len, PAIR), per_pair),
                pl.BlockSpec((lines.shape[0], PAIR), per_pair),
                pl.BlockSpec((None, 2, 2, seq_len, seq_len), lambda g: (turn(g), 0, 0, 0, 0)),
                pl.BlockSpec((3, width, PAIR), lambda g: (0, 0, turn(g))),
                pl.BlockSpec((rows, CHUNK), side), pl.BlockSpec((rows, CHUNK), side),
                pl.BlockSpec((width, CHUNK), side), pl.BlockSpec((CHUNK, width), lambda g: (chunk(g), 0)),
                keep((rows, 1)), keep((8, width)), keep((8, width)),
            ]
            + [anywhere] * 12,
            out_specs=[
                anywhere,
                pl.BlockSpec((small_rows, CHUNK), whole),
                anywhere, anywhere, anywhere,
            ],
            scratch_shapes=[
                pltpu.VMEM((PAIR, seq_len), low),
                pltpu.VMEM((PAIR, seq_len), jnp.float32),
                pltpu.VMEM((PAIR, seq_len), jnp.float32),
                pltpu.VMEM((PAIR, 2 * seq_len), jnp.float32),
                pltpu.VMEM((rows, width), jnp.float32),
                pltpu.VMEM((rows, width), low),
                pltpu.VMEM((rows, CHUNK), low),
                pltpu.VMEM((width, rows), low),
                pltpu.VMEM((width, rows), low),
                pltpu.VMEM((ROWS, ROWS), low),
                pltpu.VMEM((seq_len, width), low),
                pltpu.VMEM((seq_len, width), low),
                pltpu.VMEM((width, width), low),
                pltpu.VMEM((rows, width), low),
                pieces, pieces, pieces,
                pltpu.VMEM((max(1, more - 1), COUNT if dp_size > 32 else 1, width >> FOLDS, CHUNK), low),
                pltpu.VMEM((tiny + 1, small_rows, CHUNK), jnp.float32),
                pltpu.VMEM((small_rows, CHUNK), jnp.float32),
                pltpu.VMEM((tiny, small_rows, CHUNK), jnp.float32),
                dma((COUNT,)), dma((COUNT,)), dma((COUNT,)),
                dma((FOLDS, COUNT)), dma((FOLDS, COUNT)), dma((FOLDS, COUNT)), dma((FOLDS, COUNT)),
                dma((more, COUNT)), dma((more, COUNT)), dma((tiny,)), dma((tiny,)),
                dma((11,)), dma((2,)), dma((4,)), dma((4,)),
            ],
        ),
        compiler_params=pltpu.CompilerParams(
            collective_id=0, has_side_effects=True, vmem_limit_bytes=67043328
        ),
        name="backward",
    )(
        seg_hot, proj_c, proj_q, keys, values, rel_keys, lines, prob, squares,
        act, slope, up_w, down_w, scale, norms, sums,
        content_t, query_t, table_t, low_t, first_t, normal, grad, rows_in, vec_c, vec_q, out_w, low_rows,
    )


def finish_body(
    piece_ref, tiny_ref, rows_in, came_in, keep_in, grad_in,
    down_ref, up_ref, out_ref, cbias_ref, pbias_ref, sbias_ref, embed_ref, gain1_ref, shift1_ref, ubias_ref,
    dbias_ref, gain2_ref, shift2_ref,
    content_out, query_out, content_grad, query_grad, query_out_w, key_out_w, value_out_w, rel_out_w,
    tokens, squares, load_sem, store_sem,
):
    at = pl.program_id(0)
    core = lax.axis_index("mp")
    cols = out_ref.shape[0]
    late = COUNT - EARLY
    sources = (
        (rows_in.at[core], came_in.at[0]),
        (rows_in.at[2 + core], came_in.at[1]),
        (keep_in.at[0], grad_in.at[0]),
        (keep_in.at[1], grad_in.at[1]),
    )
    loads = [
        pltpu.make_async_copy(source, tokens.at[index, side], load_sem.at[index, side])
        for index, pair in enumerate(sources)
        for side, source in enumerate(pair)
    ]
    stores = [
        pltpu.make_async_copy(
            tokens.at[index, side], target.at[core if side == 0 else 1 - core], store_sem.at[index, side]
        )
        for index, target in enumerate((content_out, query_out, content_grad, query_grad))
        for side in range(2)
    ]
    square_stores = [
        pltpu.make_async_copy(squares.at[index], target, store_sem.at[index, 2])
        for index, target in enumerate((query_out_w, key_out_w, value_out_w, rel_out_w))
    ]

    @pl.when(at == 0)
    def _():
        for copy in loads:
            copy.start()

    for turn in range(late):
        lanes = slice(turn * PAIR, (turn + 1) * PAIR)

        @pl.when(at == turn)
        def _():
            for index in range(4):
                part = piece_ref[:, index * PAIR : (index + 1) * PAIR]
                squares[index, :, lanes] = part.astype(jnp.float32)

    @pl.when(at == late - 1)
    def _():
        for copy in square_stores:
            copy.start()
        for copy in loads:
            copy.wait()
        for copy in stores:
            copy.start()

    early = at - late

    @pl.when((early >= 0) & (early < EARLY - 1) & (early % 2 == 0))
    def _():
        down_ref[...] = jnp.transpose(piece_ref[...]).astype(jnp.float32)

    @pl.when((early >= 0) & (early < EARLY - 1) & (early % 2 == 1))
    def _():
        up_ref[...] = piece_ref[...].astype(jnp.float32)

    @pl.when(early == EARLY - 1)
    def _():
        out_ref[...] = jnp.transpose(piece_ref[:, :cols]).astype(jnp.float32)
        for copy in stores + square_stores:
            copy.wait()

    @pl.when(at == 0)
    def _():
        for line, target in enumerate((cbias_ref, pbias_ref, sbias_ref)):
            target[...] = tiny_ref[line : line + 1, :cols].reshape(cols)
        embed_ref[...] = tiny_ref[3:5, :cols]
        for line in range(ubias_ref.shape[0] // CHUNK):
            ubias_ref[line * CHUNK : (line + 1) * CHUNK] = tiny_ref[5 + line : 6 + line, :].reshape(CHUNK)
        for line, target in enumerate((gain1_ref, shift1_ref, gain2_ref, shift2_ref, dbias_ref)):
            for side in range(2):
                spot = 8 + 2 * line + side
                target[side * cols : (side + 1) * cols] = tiny_ref[spot : spot + 1, :cols].reshape(cols)


def finish(pieces, rows_out, rows_came, keep_rows, grad_came, tiny, half_ff):
    count, rows, chunk = pieces.shape
    cols = rows // 2
    late = COUNT - EARLY
    flat = lambda size: jax.ShapeDtypeStruct((size,), jnp.float32)
    square = jax.ShapeDtypeStruct((rows, cols), jnp.float32)
    pair = jax.ShapeDtypeStruct(rows_came.shape, jnp.bfloat16)
    whole = lambda p: (0, 0)
    flat_at = lambda size: pl.BlockSpec((size,), lambda p: (0,))
    anywhere = pl.BlockSpec(memory_space=pl.ANY)
    at_chunk = lambda p: jnp.clip((p - late) // 2, 0, half_ff // chunk - 1)
    results = pl.pallas_call(
        finish_body,
        out_shape=(
            jax.ShapeDtypeStruct((half_ff, rows), jnp.float32),
            jax.ShapeDtypeStruct((rows, half_ff), jnp.float32),
            jax.ShapeDtypeStruct((cols, rows), jnp.float32),
            flat(cols), flat(cols), flat(cols), jax.ShapeDtypeStruct((2, cols), jnp.float32),
            flat(rows), flat(rows), flat(half_ff), flat(rows), flat(rows), flat(rows),
            pair, pair, pair, pair, square, square, square, square,
        ),
        grid=(count,),
        in_specs=[
            pl.BlockSpec((None, rows, chunk), lambda p: ((p + EARLY) % COUNT, 0, 0)),
            pl.BlockSpec(tiny.shape, whole, pipeline_mode=pl.Buffered(1)),
            anywhere, anywhere, anywhere, anywhere,
        ],
        out_specs=[
            pl.BlockSpec((chunk, rows), lambda p: (at_chunk(p), 0)),
            pl.BlockSpec((rows, chunk), lambda p: (0, at_chunk(p))),
            pl.BlockSpec((cols, rows), whole),
            flat_at(cols), flat_at(cols), flat_at(cols), pl.BlockSpec((2, cols), whole),
            flat_at(rows), flat_at(rows), flat_at(half_ff), flat_at(rows), flat_at(rows), flat_at(rows),
        ]
        + [anywhere] * 8,
        scratch_shapes=[
            pltpu.VMEM((4,) + rows_came.shape, jnp.bfloat16),
            pltpu.VMEM((4, rows, cols), jnp.float32),
            pltpu.SemaphoreType.DMA((4, 2)),
            pltpu.SemaphoreType.DMA((4, 3)),
        ],
        compiler_params=pltpu.CompilerParams(vmem_limit_bytes=60 << 20),
        name="finish",
    )(pieces, tiny, rows_out, rows_came, keep_rows, grad_came)
    return results[13:17] + results[:3] + results[17:21] + results[3:13]


def position_table(seq_len, width):
    distance = seq_len - 1.0 - np.arange(2 * seq_len - 1, dtype=np.float32)
    freq_exp = np.arange(0, width, 2).astype(np.float32) / np.float32(width)
    inverse = np.float32(1.0) / np.float32(10000.0) ** freq_exp
    angle = (distance[:, None] * inverse[None, :]).astype(np.float32)
    table = np.concatenate([np.sin(angle), np.cos(angle)], axis=1)
    table = np.concatenate([table, np.zeros((1, width), np.float32)], axis=0)
    return table.astype(ml_dtypes.bfloat16)


def on_device(
    dp_size,
    content_in,
    query_in,
    doc_lengths,
    order_ranks,
    segment_ids,
    target_flags,
    query_weight,
    key_weight,
    value_weight,
    out_weight,
    rel_weight,
    content_bias,
    position_bias,
    segment_bias,
    segment_embed,
    first_gain,
    first_shift,
    up_weight,
    up_bias,
    down_weight,
    down_bias,
    second_gain,
    second_shift,
    content_cot,
    query_cot,
):
    half, width = content_in.shape[1:]
    seq_len = order_ranks.shape[1]
    ff = up_weight.shape[1]
    table = position_table(seq_len, width)
    (
        vec_c, vec_q, prob, proj_c, proj_q, keys, values, rel_keys, seg_hot, content_t, query_t, lines, up_bias_use,
        content, query, cots, squares, out_use, up_use, down_use,
    ) = forward(
        content_in, query_in, content_cot, query_cot, query_weight, key_weight, value_weight, rel_weight,
        out_weight, up_weight, down_weight, doc_lengths, order_ranks, segment_ids, target_flags,
        content_bias, position_bias, segment_bias, segment_embed, up_bias, jnp.asarray(table),
    )
    act, slope, scale, sums, norms, first_t, normal, grad, low_rows, low_t, rows_out = feed_forward(
        vec_c, vec_q, content, query, cots, out_use, up_use, down_use, up_bias_use,
        (first_gain, first_shift, second_gain, second_shift, down_bias),
    )
    pieces, tiny, keep_rows, rows_came, grad_came = backward(
        dp_size, seg_hot, proj_c, proj_q, keys, values, rel_keys, lines, prob, squares,
        vec_c, vec_q, content_t, query_t, jnp.asarray(table.T), out_use, act, slope, up_use, down_use,
        low_rows, low_t, first_t, normal, scale, norms, sums, grad, rows_out,
    )
    (
        content_out, query_out, content_grad, query_grad, down_sum, up_sum, out_sum,
        query_sum, key_sum, value_sum, rel_sum, cbias_sum, pbias_sum, sbias_sum, embed_sum,
        gain1_sum, shift1_sum, ubias_sum, dbias_sum, gain2_sum, shift2_sum,
    ) = finish(pieces, rows_out.reshape(4, half, width), rows_came, keep_rows, grad_came, tiny, ff)
    return (
        content_out, query_out, content_grad, query_grad,
        query_sum, key_sum, value_sum, out_sum, rel_sum, cbias_sum, pbias_sum, sbias_sum, embed_sum,
        gain1_sum, shift1_sum, up_sum, ubias_sum, down_sum, dbias_sum, gain2_sum, shift2_sum,
    )


def solution(mesh):
    placed = (
        P("dp", "mp", None),
        P("dp", "mp", None),
        P("dp"),
        P("dp", None),
        P("dp", None),
        P("dp", None),
        P(None, "mp"),
        P(None, "mp"),
        P(None, "mp"),
        P("mp", None),
        P(None, "mp"),
        P("mp"),
        P("mp"),
        P("mp"),
        P(None, "mp"),
        P(),
        P(),
        P(None, "mp"),
        P("mp"),
        P("mp", None),
        P(),
        P(),
        P(),
        P("dp", "mp", None),
        P("dp", "mp", None),
    )
    return jax.shard_map(
        functools.partial(on_device, mesh.shape["dp"]),
        mesh=mesh,
        in_specs=placed,
        out_specs=(
            P("dp", "mp", None),
            P("dp", "mp", None),
            P("dp", "mp", None),
            P("dp", "mp", None),
            P(None, "mp"),
            P(None, "mp"),
            P(None, "mp"),
            P("mp", None),
            P(None, "mp"),
            P("mp"),
            P("mp"),
            P("mp"),
            P(None, "mp"),
            P(),
            P(),
            P(None, "mp"),
            P("mp"),
            P("mp", None),
            P(),
            P(),
            P(),
        ),
        check_vma=False,
    )
```
